32 devices in a mesh: fsdp: 4 (over y, x), context: 2 (over core), tensor: 4 (over z).
Axes of the slice: x: 2, y: 2, z: 4, core: 2. Of those that a mesh axis runs over, the one named last changes fastest.
Arguments:
- block_input: bfloat16 [4, 2048, 2048], P('fsdp', 'context'), may hold values from -6 to 6
- doc_ids: int32 [4, 2048], P('fsdp'), may hold values from 0 to 7, never falling along the last dimension, each value on 1 to 1536 neighbouring positions
- norm_gain: float32 [2048], replicated, may hold values from 0.25 to 1.75
- in_proj: bfloat16 [2, 2048, 4096], P(None, 'fsdp', 'tensor'), may hold values from -0.125 to 0.125
- conv_weight: float32 [4, 4096], P(None, 'tensor'), may hold values from -0.5 to 0.5
- conv_bias: float32 [4096], P('tensor'), may hold values from -0.5 to 0.5
- x_proj: bfloat16 [4096, 160], P('tensor', 'fsdp'), may hold values from -1 to 1
- dt_proj: bfloat16 [128, 4096], P('fsdp', 'tensor'), may hold values from -2 to 2
- dt_bias: float32 [4096], P('tensor'), may hold values from -6.5 to -2.5
- a_log: float32 [16, 4096], P(None, 'tensor'), may hold values from 0 to 2.77
- d_skip: float32 [4096], P('tensor'), may hold values from 0.5 to 1.5
- out_proj: bfloat16 [4096, 2048], P('tensor', 'fsdp'), may hold values from -0.1875 to 0.1875
- grad_output: bfloat16 [4, 2048, 2048], P('fsdp', 'context'), may hold values from -6 to 6
Outputs:
- block_output: bfloat16 [4, 2048, 2048], P('fsdp', 'context')
- grad_input: bfloat16 [4, 2048, 2048], P('fsdp', 'context')
- grad_norm_gain: float32 [2048], replicated
- grad_in_proj: float32 [2, 2048, 4096], P(None, 'fsdp', 'tensor')
- grad_conv_weight: float32 [4, 4096], P(None, 'tensor')
- grad_conv_bias: float32 [4096], P('tensor')
- grad_x_proj: float32 [4096, 160], P('tensor', 'fsdp')
- grad_dt_proj: float32 [128, 4096], P('fsdp', 'tensor')
- grad_dt_bias: float32 [4096], P('tensor')
- grad_a_log: float32 [16, 4096], P(None, 'tensor')
- grad_d_skip: float32 [4096], P('tensor')
- grad_out_proj: float32 [4096, 2048], P('tensor', 'fsdp')
The draws below stay inside these ranges and needn't reach their ends.
Inputs may be any that keep to these rules, and one draw needn't show every extreme that they name: `doc_ids`: ids never fall along a sequence and start at 0 in each.
All inputs are finite; a program needn't handle non-finite values.
Results may differ from the reference program's by a relative error of at most 0.012.
The reference program's roundings to bfloat16 on the way count: a program that leaves them out, or rounds other values in their place, can miss the bound.
Values may be sent and summed in bfloat16 or wider, within the bound.
No kernel may reach another device: no remote copies, remote signals or barrier semaphores. Data moves between devices by JAX's collectives and lax.ppermute only.
A program may use at most 256 MiB of HBM per device.

```python
import math
import jax
import jax.numpy as jnp
import numpy as np
from jax import lax

DMODEL = 2048
INNER = 4096
STATE = 16
RANK = 128
CONV = 4
SEQ_LEN = 2048
SEQS = 4


def draw_x_proj(key, part):
    columns = RANK + 2 * STATE
    values = jnp.clip(jax.random.normal(key, (INNER, columns), jnp.float32), -6.0, 6.0)
    column_scale = jnp.where(jnp.arange(columns) < RANK, 0.25, 1.0).astype(jnp.float32)
    return (values * column_scale[None, :] * (1.0 / math.sqrt(INNER))).astype(jnp.bfloat16)


def block_levels(own_key, dims, cuts, least, top_value):
    def one(position, blocks):
        steps = jax.random.uniform(jax.random.fold_in(jax.random.fold_in(own_key, 6), position), (blocks,), jnp.float32, least / len(cuts), top_value / len(cuts))
        return jnp.repeat(jnp.exp(steps), dims[position] // blocks).reshape((-1,) + (1,) * (len(dims) - position - 1))

    loudness = one(*cuts[0])
    for cut in cuts[1:]:
        loudness = loudness * one(*cut)
    return loudness


def split_up(amount, total, limit, skew):
    portions = [(1 << 20) // math.isqrt(standing ** skew) + 1 for standing in range(2, amount + 1)]
    surplus, given = total - limit - (amount - 1), [1] * (amount - 1)
    while surplus > 0:
        free = [i for i in range(amount - 1) if given[i] < limit]
        whole, left = sum([portions[i] for i in free]), surplus
        for i in free:
            addition = min(limit - given[i], max(1, left * portions[i] // whole), surplus)
            given[i] = given[i] + addition
            surplus = surplus - addition
    return np.array([limit] + given)


def ragged(key, amount, total, bound, lean):
    if amount == 2:
        one = jax.random.randint(key, (), max(1, total - bound), min(bound, total - 1) + 1)
        return jnp.stack([one, total - one])
    tallies = jnp.asarray(split_up(amount, total, bound, lean), jnp.int32)
    couples = (amount - 1) // 2
    source_of, taker = tallies[1:1 + 2 * couples:2], tallies[2:2 + 2 * couples:2]
    slack = jnp.minimum(source_of - 1, bound - taker)
    passed = jax.random.randint(jax.random.fold_in(key, 1), (couples,), 0, 1 << 20) % (slack + 1)
    tallies = tallies.at[1:1 + 2 * couples:2].set(source_of - passed).at[2:2 + 2 * couples:2].set(taker + passed)
    return tallies[jax.random.permutation(jax.random.fold_in(key, 2), amount)]


def scatter_about(own_key, dims, deviation, most, cuts=(), held_as=jnp.bfloat16):
    level = block_levels(own_key, dims, cuts, -0.22, 0.18) if cuts else 1.0
    entries = jax.random.normal(own_key, dims, jnp.float32) * deviation * level
    return jnp.minimum(jnp.maximum(entries, -most), most).astype(held_as)


def setup_inputs(seed: int = 0) -> dict:
    key_list = jax.random.split(jax.random.key(seed), 14)
    return {
        "block_input": scatter_about(key_list[0], (SEQS, SEQ_LEN, DMODEL), 1.0, 6.0, ((0, 4), (1, 2))),
        "doc_ids": jax.vmap(lambda own: jnp.searchsorted(jnp.cumsum(ragged(own, max(2, SEQ_LEN // 256), SEQ_LEN, SEQ_LEN // 2 + SEQ_LEN // 4, 2)), jnp.arange(SEQ_LEN), side="right"))(jax.random.split(key_list[1], SEQS)).reshape((SEQS, SEQ_LEN)).astype(jnp.int32),
        "norm_gain": jnp.clip(1.0 + 0.15 * jax.random.normal(key_list[2], (DMODEL,), jnp.float32), 0.25, 1.75),
        "in_proj": scatter_about(key_list[3], (2, DMODEL, INNER), DMODEL ** -0.5, 0.125, ((1, 4), (2, 4))),
        "conv_weight": jnp.clip(jax.random.uniform(key_list[4], (CONV, INNER), jnp.float32, -0.5, 0.5) * block_levels(key_list[4], (CONV, INNER), ((1, 4),), -0.4, 0.0), -0.5, 0.5),
        "conv_bias": jnp.clip(jax.random.uniform(key_list[5], (INNER,), jnp.float32, -0.5, 0.5) * block_levels(key_list[5], (INNER,), ((0, 4),), -0.4, 0.0), -0.5, 0.5),
        "x_proj": draw_x_proj(jax.random.fold_in(key_list[13], 71), 0),
        "dt_proj": scatter_about(key_list[7], (RANK, INNER), (RANK // 16) ** -0.5, 2.0, ((0, 4), (1, 4))),
        "dt_bias": jnp.clip(-6.5 + 4.0 * jax.random.uniform(key_list[8], (INNER,), jnp.float32) ** block_levels(key_list[8], (INNER,), ((0, 4),), -0.2, 0.2), -6.5, -2.5),
        "a_log": jnp.clip(2.77 * jax.random.uniform(key_list[9], (STATE, INNER), jnp.float32) ** block_levels(key_list[9], (STATE, INNER), ((1, 4),), -0.2, 0.2), 0.0, 2.77),
        "d_skip": jnp.clip(0.5 + 1.0 * jax.random.uniform(key_list[10], (INNER,), jnp.float32) ** block_levels(key_list[10], (INNER,), ((0, 4),), -0.2, 0.2), 0.5, 1.5),
        "out_proj": scatter_about(key_list[11], (INNER, DMODEL), (INNER // 4) ** -0.5, 0.1875, ((0, 4), (1, 4))),
        "grad_output": scatter_about(key_list[12], (SEQS, SEQ_LEN, DMODEL), 1.0, 6.0, ((0, 4), (1, 2))),
    }


EPS = 1e-05
HIGHEST = lax.Precision.HIGHEST

@jax.custom_vjp
def low(v):
    return lax.optimization_barrier(v.astype(jnp.bfloat16)).astype(jnp.float32)

@jax.custom_vjp
def low_back(v):
    return v

def low_keep(v):
    return (low(v), None)

def low_pass(kept, grad):
    return (grad,)

def back_keep(v):
    return (v, None)

def back_low(kept, grad):
    return (low(grad),)
low.defvjp(low_keep, low_pass)
low_back.defvjp(back_keep, back_low)

def matmul(left_side, right_side):
    return jnp.dot(left_side, right_side, precision=HIGHEST, preferred_element_type=jnp.float32)

def selective_scan(step_sizes, activated, in_coef, out_coef, keeping, decay_rates):
    length = step_sizes.shape[0]
    block_len = math.gcd(length, 64)

    def one_token(state, token):
        step_now, value_now, in_now, out_now, keep_now = token
        factor = jnp.exp(step_now[None, :] * decay_rates) * keep_now
        state = factor * state + (step_now * value_now)[None, :] * in_now[:, None]
        return (state, lax.optimization_barrier(jnp.sum(out_now[:, None] * state, axis=0)))

    def one_block(state, tokens):
        return lax.scan(one_token, state, tokens)

    def split_rows(array):
        return array.reshape((length // block_len, block_len) + array.shape[1:])
    start_state = jnp.zeros(decay_rates.shape, jnp.float32)
    pieces = tuple((split_rows(array) for array in (step_sizes, activated, in_coef, out_coef, keeping)))
    _, outputs = lax.scan(jax.checkpoint(one_block), start_state, pieces)
    return outputs.reshape(length, decay_rates.shape[1])

def sequence(params, inputs, doc_ids):
    norm_gain, in_proj, conv_weight, conv_bias, x_proj, dt_proj, dt_bias, a_log, d_skip, out_proj = params
    length = inputs.shape[0]
    tail_len = conv_weight.shape[0] - 1
    inner = in_proj.shape[2]
    rank = dt_proj.shape[0]
    states = a_log.shape[0]
    inv_rms = lax.rsqrt(lax.optimization_barrier(jnp.mean(inputs * inputs, axis=-1, keepdims=True)) + EPS)
    normed = low(inputs * inv_rms * norm_gain)
    conv_input = low(low_back(matmul(normed, in_proj[0])))
    gate_input = low_back(matmul(normed, in_proj[1]))
    padded_ids = jnp.concatenate([jnp.full((tail_len,), -1, jnp.int32), doc_ids.astype(jnp.int32)])
    padded_input = jnp.concatenate([jnp.zeros((tail_len, inner), jnp.float32), conv_input], axis=0)
    conv_output = conv_bias
    for shift_by in range(tail_len + 1):
        lower_edge = tail_len - shift_by
        match_now = (padded_ids[lower_edge:lower_edge + length] == doc_ids).astype(jnp.float32)
        conv_output = conv_output + conv_weight[shift_by] * padded_input[lower_edge:lower_edge + length] * match_now[:, None]
    keeping = (padded_ids[tail_len - 1:tail_len - 1 + length] == doc_ids).astype(jnp.float32)
    activated = low(jax.nn.silu(conv_output))
    projections = low(low_back(matmul(activated, x_proj)))
    dt_logits = low_back(matmul(projections[:, :rank], dt_proj) + dt_bias)
    step_sizes = jax.nn.softplus(dt_logits)
    decay_rates = -jnp.exp(a_log)
    scanned = selective_scan(step_sizes, activated, projections[:, rank:rank + states], projections[:, rank + states:], keeping, decay_rates)
    mixed = scanned + d_skip * activated
    gated = low(mixed * jax.nn.silu(gate_input))
    return inputs + matmul(gated, out_proj)

def reference(block_input, doc_ids, norm_gain, in_proj, conv_weight, conv_bias, x_proj, dt_proj, dt_bias, a_log, d_skip, out_proj, grad_output):
    params = tuple((weight_item.astype(jnp.float32) for weight_item in (norm_gain, in_proj, conv_weight, conv_bias, x_proj, dt_proj, dt_bias, a_log, d_skip, out_proj)))
    inputs = block_input.astype(jnp.float32)

    def whole(inputs, params):

        def per_sequence(carry, item):
            return (carry, jax.checkpoint(sequence)(params, item[0], item[1]))
        _, outputs = lax.scan(per_sequence, jnp.zeros((), jnp.float32), (inputs, doc_ids))
        return outputs
    outputs, pullback = jax.vjp(whole, inputs, params)
    grad_in, grads = pullback(grad_output.astype(jnp.float32))
    return (outputs.astype(jnp.bfloat16), grad_in.astype(jnp.bfloat16), grads[0], grads[1], grads[2], grads[3], grads[4], grads[5], grads[6], grads[7], grads[8], grads[9])
```

```python
import functools

import jax
import jax.numpy as jnp
from jax import lax
from jax.experimental import pallas as pl
from jax.experimental.pallas import tpu as pltpu
from jax.sharding import PartitionSpec as P

LANES=128; GROUP=8

def fold(pending, value, level_masks):
    level=0
    while pending and pending[-1][0]==level:
        _, first = pending.pop()
        d = 1<<level
        if d < 4:
            value = jnp.where(level_masks[level], first + pltpu.roll(first, 8-d, 0), value + pltpu.roll(value, d, 0))
        else:
            x = jnp.where(level_masks[2], first, value); z = jnp.where(level_masks[2], value, first)
            value = x + pltpu.roll(z, 4, 0)
        level += 1
    pending.append((level,value))

def fold_down(pending, value, level_masks):
    level=0
    while pending and pending[-1][0]==level:
        _, later = pending.pop()
        d = 1<<level
        if d < 4:
            value = jnp.where(level_masks[level], value + pltpu.roll(value, 8-d, 0), later + pltpu.roll(later, d, 0))
        else:
            x = jnp.where(level_masks[2], value, later); z = jnp.where(level_masks[2], later, value)
            value = x + pltpu.roll(z, 4, 0)
        level += 1
    pending.append((level,value))

def masks():
    row = lax.broadcasted_iota(jnp.int32,(8,LANES),0)
    return [(row & d)==0 for d in (1,2,4)]

def tiles(ref, base, groups):
    return [ref[pl.ds(base, 8), g*LANES:(g+1)*LANES] for g in range(groups)]

def row(tile, r):
    return jnp.broadcast_to(tile[r:r+1, :], (8, LANES))

def fwd_kernel(dtf_ref, dtx_ref, bt_ref, ct_ref, a2_ref, y_ref, h_ref, last_ref, state_ref, *, halves, groups):
    chunk = dtf_ref.shape[0]
    @pl.when(pl.program_id(0)==0)
    def _(): state_ref[...] = jnp.zeros_like(state_ref)
    a2 = [[a2_ref[8*i:8*i+8, g*LANES:(g+1)*LANES] for g in range(groups)] for i in range(halves)]
    lane = lax.broadcasted_iota(jnp.int32,(8,LANES),1)
    lm = masks()
    def body(k, st):
        st = [list(s) for s in st]
        base = pl.multiple_of(k*8, 8)
        pend = [[] for _ in range(groups)]
        tf = tiles(dtf_ref, base, groups); tx = tiles(dtx_ref, base, groups)
        for r in range(8):
            t = base + r
            m = lane == t
            bc = [jnp.sum(jnp.where(m, bt_ref[8*i:8*i+8,:], 0.0), axis=1, keepdims=True) for i in range(halves)]
            cc = [jnp.sum(jnp.where(m, ct_ref[8*i:8*i+8,:], 0.0), axis=1, keepdims=True) for i in range(halves)]
            for g in range(groups):
                dtf = row(tf[g], r); dtx = row(tx[g], r)
                p = None
                for i in range(halves):
                    h_ref[pl.ds(pl.multiple_of(t*(8*halves)+8*i,8), 8), g*LANES:(g+1)*LANES] = st[i][g].astype(h_ref.dtype)
                    f = jnp.exp2(dtf*a2[i][g])
                    s = f*st[i][g] + dtx*bc[i]
                    st[i][g] = s
                    q = s*cc[i]
                    p = q if p is None else p+q
                fold(pend[g], p, lm)
        for g in range(groups):
            y_ref[pl.ds(base,8), g*LANES:(g+1)*LANES] = pend[g][0][1]
        return tuple(tuple(s) for s in st)
    st = tuple(tuple(state_ref[8*i:8*i+8, g*LANES:(g+1)*LANES] for g in range(groups)) for i in range(halves))
    st = lax.fori_loop(0, chunk//8, body, st)
    for i in range(halves):
        for g in range(groups):
            state_ref[8*i:8*i+8, g*LANES:(g+1)*LANES] = st[i][g]
            last_ref[8*i:8*i+8, g*LANES:(g+1)*LANES] = st[i][g]

def fwd(dtf, dtx, bt, ct, a2, h_dtype=jnp.float32, chunk=128):
    T,E = dtf.shape; N=a2.shape[0]
    halves, groups = N//8, E//LANES
    rows = lambda w: pl.BlockSpec((w,E), lambda c:(c,0))
    cols = pl.BlockSpec((N,chunk), lambda c:(0,c))
    whole = pl.BlockSpec((N,E), lambda c:(0,0))
    return pl.pallas_call(
        functools.partial(fwd_kernel, halves=halves, groups=groups),
        grid=(T//chunk,),
        in_specs=[rows(chunk), rows(chunk), cols, cols, whole],
        out_specs=[rows(chunk), rows(chunk*N), whole],
        out_shape=[jax.ShapeDtypeStruct((T,E),jnp.float32), jax.ShapeDtypeStruct((T*N,E),h_dtype), jax.ShapeDtypeStruct((N,E),jnp.float32)],
        scratch_shapes=[pltpu.VMEM((N,E),jnp.float32)],
        compiler_params=pltpu.CompilerParams(dimension_semantics=("arbitrary",), vmem_limit_bytes=40<<20),
    )(dtf,dtx,bt,ct,a2)

def bwd_kernel(dtf_ref, dtx_ref, u_ref, bt_ref, ct_ref, a2_ref, h_ref, last_ref,
               iw_ref, ds_ref, din_ref, dout_ref, da_ref, flow_ref, hcur_ref, *, halves, groups):
    chunk = dtf_ref.shape[0]
    @pl.when(pl.program_id(0)==0)
    def _():
        flow_ref[...] = jnp.zeros_like(flow_ref); da_ref[...] = jnp.zeros_like(da_ref)
        hcur_ref[...] = last_ref[...]
    sl = lambda g: slice(g*LANES,(g+1)*LANES)
    a2 = [[a2_ref[8*i:8*i+8, sl(g)] for g in range(groups)] for i in range(halves)]
    lane = lax.broadcasted_iota(jnp.int32,(8,LANES),1)
    lm = masks()
    grab = lambda ref: tuple(tuple(ref[8*i:8*i+8, sl(g)] for g in range(groups)) for i in range(halves))
    def body(k, carry):
        flow, da, hcur, din, dout = carry
        flow=[list(s) for s in flow]; da=[list(s) for s in da]; hcur=[list(s) for s in hcur]
        din=list(din); dout=list(dout)
        base = pl.multiple_of(chunk-8-k*8, 8)
        tf = tiles(dtf_ref, base, groups); tx = tiles(dtx_ref, base, groups); tu = tiles(u_ref, base, groups)
        piw = [[] for _ in range(groups)]; pds=[[] for _ in range(groups)]
        for r in range(7,-1,-1):
            t = base + r
            m = lane == t
            bc = [jnp.sum(jnp.where(m, bt_ref[8*i:8*i+8,:], 0.0), axis=1, keepdims=True) for i in range(halves)]
            cc = [jnp.sum(jnp.where(m, ct_ref[8*i:8*i+8,:], 0.0), axis=1, keepdims=True) for i in range(halves)]
            di=[None]*halves; do=[None]*halves
            for g in range(groups):
                dtf = row(tf[g],r); dtx=row(tx[g],r); u=row(tu[g],r)
                iw=None; ds=None
                for i in range(halves):
                    hp = h_ref[pl.ds(pl.multiple_of(t*(8*halves)+8*i,8),8), sl(g)].astype(jnp.float32)
                    f = jnp.exp2(dtf*a2[i][g])
                    adj = cc[i]*u + flow[i][g]
                    o = hcur[i][g]*u
                    do[i] = o if do[i] is None else do[i]+o
                    n_ = adj*dtx
                    di[i] = n_ if di[i] is None else di[i]+n_
                    fl = f*adj
                    flow[i][g]=fl
                    pulled = fl*hp
                    w = adj*bc[i]; iw = w if iw is None else iw+w
                    s = pulled*a2[i][g]; ds = s if ds is None else ds+s
                    da[i][g] = da[i][g] + pulled*dtf
                    hcur[i][g]=hp
                fold_down(piw[g], iw, lm); fold_down(pds[g], ds, lm)
            for i in range(halves):
                din[i] = jnp.where(m, jnp.sum(di[i],axis=1,keepdims=True), din[i])
                dout[i] = jnp.where(m, jnp.sum(do[i],axis=1,keepdims=True), dout[i])
        for g in range(groups):
            iw_ref[pl.ds(base,8), sl(g)] = piw[g][0][1]
            ds_ref[pl.ds(base,8), sl(g)] = pds[g][0][1]
        tt=lambda x: tuple(tuple(s) for s in x)
        return tt(flow),tt(da),tt(hcur),tuple(din),tuple(dout)
    z = tuple(jnp.zeros((8,LANES),jnp.float32) for _ in range(halves))
    flow,da,hcur,din,dout = lax.fori_loop(0, chunk//8, body, (grab(flow_ref),grab(da_ref),grab(hcur_ref),z,z))
    for i in range(halves):
        din_ref[8*i:8*i+8,:]=din[i]; dout_ref[8*i:8*i+8,:]=dout[i]
        for g in range(groups):
            flow_ref[8*i:8*i+8, sl(g)]=flow[i][g]; da_ref[8*i:8*i+8, sl(g)]=da[i][g]; hcur_ref[8*i:8*i+8, sl(g)]=hcur[i][g]

def bwd(dtf,dtx,u,bt,ct,a2,h,last,chunk=128):
    T,E=dtf.shape; N=a2.shape[0]
    halves, groups = N//8, E//LANES
    n=T//chunk
    rows=lambda w: pl.BlockSpec((w,E), lambda c:(n-1-c,0))
    cols=pl.BlockSpec((N,chunk), lambda c:(0,n-1-c))
    whole=pl.BlockSpec((N,E), lambda c:(0,0))
    f32=jnp.float32
    return pl.pallas_call(
        functools.partial(bwd_kernel, halves=halves, groups=groups),
        grid=(n,),
        in_specs=[rows(chunk)]*3+[cols,cols,whole,rows(chunk*N),whole],
        out_specs=[rows(chunk),rows(chunk),cols,cols,whole],
        out_shape=[jax.ShapeDtypeStruct((T,E),f32)]*2+[jax.ShapeDtypeStruct((N,T),f32)]*2+[jax.ShapeDtypeStruct((N,E),f32)],
        scratch_shapes=[pltpu.VMEM((N,E),f32)]*2,
        compiler_params=pltpu.CompilerParams(dimension_semantics=("arbitrary",), vmem_limit_bytes=40<<20),
    )(dtf,dtx,u,bt,ct,a2,h,last)


EPS = 1e-05
GONE = 1e4
LOG2E = 1.4426950408889634
BF16 = jnp.bfloat16
F32 = jnp.float32


def swap(array, axis, k):
    size = lax.axis_size(axis)
    return lax.ppermute(array, axis, [(i, i ^ k) for i in range(size)])


def gather(array, axis, dim):
    count, me, size = lax.axis_size(axis), lax.axis_index(axis), array.shape[dim]
    shape = array.shape[:dim] + (size * count,) + array.shape[dim + 1 :]
    out = jnp.zeros(shape, array.dtype)
    for k in range(count):
        piece = swap(array, axis, k) if k else array
        out = lax.dynamic_update_slice_in_dim(out, piece, (me ^ k) * size, dim)
    return out


def piece_of(array, axis, dim, index):
    size = array.shape[dim] // lax.axis_size(axis)
    return lax.dynamic_slice_in_dim(array, index * size, size, dim)


def scatter_sum(array, axis, dim, kind):
    me = lax.axis_index(axis)
    total = piece_of(array, axis, dim, me)
    for k in range(1, lax.axis_size(axis)):
        total = total + swap(piece_of(array, axis, dim, me ^ k).astype(kind), axis, k).astype(F32)
    return total


def doubling_sum(array, axes):
    for axis in axes:
        k = 1
        while k < lax.axis_size(axis):
            array = array + swap(array, axis, k)
            k *= 2
    return array


def dot(left, right, left_dim=1, right_dim=0):
    return lax.dot_general(left, right, (((left_dim,), (right_dim,)), ((), ())), preferred_element_type=F32)


def silu_slope(v):
    s = jax.nn.sigmoid(v)
    return s * (1.0 + v * (1.0 - s))


def inverse_rms(x):
    return lax.rsqrt(jnp.mean(x * x, axis=-1, keepdims=True) + EPS)


def shards(
    block_input,
    doc_ids,
    norm_gain,
    in_proj,
    conv_weight,
    conv_bias,
    x_proj,
    dt_proj,
    dt_bias,
    a_log,
    d_skip,
    out_proj,
    grad_output,
):
    seqs, piece, width = block_input.shape
    length = doc_ids.shape[1]
    ctx, ctxs = lax.axis_index("context"), lax.axis_size("context")
    taps, tail = conv_weight.shape[0], conv_weight.shape[0] - 1
    states = a_log.shape[0]
    rows = seqs * length
    inner = in_proj.shape[2] // ctxs
    rank = dt_proj.shape[0] * lax.axis_size("fsdp")

    def mine(array, dim):
        return piece_of(array, "context", dim, ctx)

    in_half = mine(in_proj, 2)
    w_conv = gather(in_half[0], "fsdp", 0)
    x_own = block_input.astype(F32)
    normed_own = (x_own * inverse_rms(x_own) * norm_gain).astype(BF16)
    normed = gather(normed_own, "context", 1).reshape(rows, width)
    small = jnp.concatenate([mine(x_proj, 0).T, mine(dt_proj, 1)], axis=0)
    xcols = x_proj.shape[1]
    small_all = gather(small[None], "fsdp", 0)
    w_x = small_all[:, :xcols].reshape(-1, inner)
    w_dt = small_all[:, xcols:].reshape(rank, inner)
    w_gate = gather(in_half[1], "fsdp", 0)
    w_out = gather(mine(out_proj, 0), "fsdp", 1)
    cotangent = gather(grad_output, "context", 1).reshape(rows, width)
    taps_w, bias, dt_b = mine(conv_weight, 1), mine(conv_bias, 0), mine(dt_bias, 0)
    rates = -jnp.exp(mine(a_log, 1))
    skip = mine(d_skip, 0)

    conv_input = dot(normed, w_conv).astype(BF16)
    padded_ids = jnp.concatenate([jnp.full((seqs, tail), -1, jnp.int32), doc_ids], axis=1)
    same = [
        (padded_ids[:, tail - k : tail - k + length] == doc_ids).astype(F32)[..., None]
        for k in range(taps)
    ]
    padded = jnp.pad(conv_input.reshape(seqs, length, inner), ((0, 0), (tail, 0), (0, 0))).astype(F32)
    shifted = [padded[:, tail - k : tail - k + length] for k in range(taps)]
    conv_output = bias
    for k in range(taps):
        conv_output = conv_output + taps_w[k] * shifted[k] * same[k]
    conv_flat = conv_output.reshape(rows, inner)
    activated = jax.nn.silu(conv_flat).astype(BF16)
    act = activated.astype(F32)

    def all_sum(part):
        part = scatter_sum(part, "context", 1, F32)
        part = scatter_sum(part, "tensor", 1, BF16).astype(BF16)
        return gather(gather(part, "tensor", 1), "context", 1)

    projections = all_sum(dot(w_x, activated, 1, 1))
    dt_input = projections[:rank]
    in_coef = projections[rank : rank + states].astype(F32)
    out_coef = projections[rank + states :].astype(F32)
    dt_logits = dot(dt_input, w_dt, 0, 0) + dt_b
    steps = jax.nn.softplus(dt_logits)
    keep = same[1].reshape(rows, 1)
    fading = jnp.where(keep > 0, steps, GONE)
    fed = steps * act
    rates2 = rates * LOG2E
    scanned, history, last = fwd(fading, fed, in_coef, out_coef, rates2)

    gate = dot(normed, w_gate)
    gate_value = jax.nn.silu(gate)
    mixed = scanned + skip * act
    gated = (mixed * gate_value).astype(BF16)
    d_gated = dot(cotangent, w_out, 1, 1)
    d_mixed = d_gated * gate_value
    d_gate = (d_gated * mixed * silu_slope(gate)).astype(BF16)

    def my_tokens(array):
        array = array.reshape(seqs, length, array.shape[-1])
        parts = [piece_of(array, "context", 1, ctx)]
        for k in range(1, ctxs):
            parts.append(swap(piece_of(array, "context", 1, ctx ^ k), "context", k))
        return [p.reshape(seqs * piece, p.shape[-1]) for p in parts]

    def all_halves(weight):
        return [weight] + [swap(weight, "context", k) for k in range(1, ctxs)]

    def over_tensor(part):
        return scatter_sum(part, "tensor", 0, BF16)

    zplace = lax.axis_index("tensor")

    def my_rows(array):
        return piece_of(array.reshape(seqs * piece, width), "tensor", 0, zplace).astype(F32)

    x_rows = my_rows(block_input)
    branch = dot(
        jnp.concatenate(my_tokens(gated), axis=1), jnp.concatenate(all_halves(w_out), axis=0)
    )
    branch = over_tensor(branch)
    block_output = gather((x_rows + branch).astype(BF16), "tensor", 0).reshape(block_input.shape)

    in_weighted, d_fade, d_in_coef, d_out_coef, d_rates = bwd(
        fading, fed, d_mixed, in_coef, out_coef, rates2, history, last
    )
    d_step = d_fade * (1.0 / LOG2E) + act * in_weighted
    d_logits = (d_step * jax.nn.sigmoid(dt_logits)).astype(BF16)
    d_part = jnp.concatenate([dot(w_dt, d_logits, 1, 1), d_in_coef, d_out_coef], axis=0)
    d_projections = all_sum(d_part)
    grad_out_part = dot(gated, cotangent, 0, 0)
    grad_gate_part = dot(normed, d_gate, 0, 0)
    grad_dt_part = dot(dt_input, d_logits)
    d_act = d_mixed * skip + steps * in_weighted + dot(d_projections, w_x, 0, 0)
    grad_x_part = dot(d_projections, activated)
    d_conv = (d_act * silu_slope(conv_flat)).reshape(seqs, length, inner)
    d_conv_input = jnp.zeros((seqs, length, inner), F32)
    tap_grads = []
    for k in range(taps):
        masked = d_conv * same[k]
        late = jnp.pad(masked, ((0, 0), (0, tail), (0, 0)))[:, k : k + length]
        d_conv_input = d_conv_input + taps_w[k] * late
        tap_grads.append(jnp.sum(masked * shifted[k], axis=(0, 1)))
    d_conv_input = d_conv_input.reshape(rows, inner).astype(BF16)
    grad_conv_part = dot(normed, d_conv_input, 0, 0)

    left = jnp.concatenate(my_tokens(d_gate) + my_tokens(d_conv_input), axis=1)
    right = jnp.concatenate(all_halves(w_gate) + all_halves(w_conv), axis=1)
    d_normed = over_tensor(dot(left, right, 1, 1))
    inv = inverse_rms(x_rows)
    scaled = d_normed * norm_gain
    inner_sum = jnp.sum(scaled * x_rows, axis=-1, keepdims=True)
    grad_rows = my_rows(grad_output) + inv * scaled - x_rows * (inv * inv * inv) * inner_sum / width
    grad_input = gather(grad_rows.astype(BF16), "tensor", 0).reshape(block_input.shape)
    grad_gain = doubling_sum(
        jnp.sum(d_normed * x_rows * inv, axis=0)[None], ("context", "fsdp", "tensor")
    )[0]

    def owned(part, dim, ctx_dim):
        return gather(scatter_sum(part, "fsdp", dim, BF16), "context", ctx_dim)

    grad_in = owned(jnp.stack([grad_conv_part, grad_gate_part]), 1, 2)
    grad_out = owned(grad_out_part, 1, 0)
    grad_x = owned(grad_x_part, 0, 1).T
    grad_dt = owned(grad_dt_part, 0, 1)
    thin = jnp.concatenate(
        [
            d_rates * rates,
            jnp.stack(tap_grads),
            jnp.sum(d_conv, axis=(0, 1))[None],
            jnp.sum(d_logits.astype(F32), axis=0)[None],
            jnp.sum(d_mixed * act, axis=0)[None],
        ],
        axis=0,
    )
    thin = gather(doubling_sum(thin, ("fsdp",)), "context", 1)
    return (
        block_output,
        grad_input,
        grad_gain,
        grad_in,
        thin[states : states + taps],
        thin[states + taps],
        grad_x,
        grad_dt,
        thin[states + taps + 1],
        thin[:states],
        thin[states + taps + 2],
        grad_out,
    )


def solution(mesh):
    placed = (
        P("fsdp", "context", None),
        P("fsdp", None),
        P(),
        P(None, "fsdp", "tensor"),
        P(None, "tensor"),
        P("tensor"),
        P("tensor", "fsdp"),
        P("fsdp", "tensor"),
        P("tensor"),
        P(None, "tensor"),
        P("tensor"),
        P("tensor", "fsdp"),
        P("fsdp", "context", None),
    )
    return jax.shard_map(
        shards,
        mesh=mesh,
        in_specs=placed,
        out_specs=(
            P("fsdp", "context", None),
            P("fsdp", "context", None),
            P(),
            P(None, "fsdp", "tensor"),
            P(None, "tensor"),
            P("tensor"),
            P("tensor", "fsdp"),
            P("fsdp", "tensor"),
            P("tensor"),
            P(None, "tensor"),
            P("tensor"),
            P("tensor", "fsdp"),
        ),
        check_vma=False,
    )
```

```python
import functools

import jax
import jax.numpy as jnp
from jax import lax
from jax.experimental import pallas as pl
from jax.experimental.layout import Layout, with_layout_constraint
from jax.experimental.pallas import tpu as pltpu
from jax.sharding import PartitionSpec as P

LANES = 128
SUB = 8
CHUNK = 128


def span(group):
    return slice(group * LANES, (group + 1) * LANES)


def blocks(ref, halves, groups):
    return [[ref[SUB * i : SUB * i + SUB, span(g)] for g in range(groups)] for i in range(halves)]


def put_blocks(ref, values):
    for i, line in enumerate(values):
        for g, value in enumerate(line):
            ref[SUB * i : SUB * i + SUB, span(g)] = value


def column(ref, halves, t):
    return [
        jnp.broadcast_to(ref[SUB * i : SUB * i + SUB, t : t + 1], (SUB, LANES))
        for i in range(halves)
    ]


def row(tile, r):
    return jnp.broadcast_to(tile[r : r + 1, :], (SUB, LANES))


def sublane_bits():
    index = lax.broadcasted_iota(jnp.int32, (SUB, LANES), 0)
    return [(index & d) == 0 for d in (1, 2, 4)]


def fold(pending, value, bits, falling):
    level = 0
    while pending and pending[-1][0] == level:
        _, other = pending.pop()
        early, late = (value, other) if falling else (other, value)
        d = 1 << level
        if d < 4:
            value = jnp.where(
                bits[level], early + pltpu.roll(early, SUB - d, 0), late + pltpu.roll(late, d, 0)
            )
        else:
            value = jnp.where(bits[level], early, late) + pltpu.roll(
                jnp.where(bits[level], late, early), d, 0
            )
        level += 1
    pending.append((level, value))


def total(values):
    return functools.reduce(lambda a, b: a + b, values)


def scan_kernel(fade_ref, fed_ref, in_ref, out_ref, rate_ref, y_ref, h_ref, last_ref, state_ref):
    chunk, width = fade_ref.shape
    halves, groups = rate_ref.shape[0] // SUB, width // LANES

    @pl.when(pl.program_id(0) == 0)
    def _():
        state_ref[...] = jnp.zeros_like(state_ref)

    rate = blocks(rate_ref, halves, groups)
    state = blocks(state_ref, halves, groups)
    bits = sublane_bits()
    for base in range(0, chunk, SUB):
        fade = [fade_ref[base : base + SUB, span(g)] for g in range(groups)]
        fed = [fed_ref[base : base + SUB, span(g)] for g in range(groups)]
        pending = [[] for _ in range(groups)]
        for r in range(SUB):
            t = base + r
            in_col, out_col = column(in_ref, halves, t), column(out_ref, halves, t)
            for g in range(groups):
                fade_row, fed_row = row(fade[g], r), row(fed[g], r)
                parts = []
                for i in range(halves):
                    place = (t * halves + i) * SUB
                    h_ref[place : place + SUB, span(g)] = state[i][g]
                    factor = jnp.exp2(fade_row * rate[i][g])
                    state[i][g] = factor * state[i][g] + fed_row * in_col[i]
                    parts.append(state[i][g] * out_col[i])
                fold(pending[g], total(parts), bits, False)
        for g in range(groups):
            y_ref[base : base + SUB, span(g)] = pending[g][0][1]
    put_blocks(state_ref, state)
    last_ref[...] = state_ref[...]


def lane_sums(products):
    ones = jnp.ones((SUB, LANES), jnp.bfloat16)
    high = products.astype(jnp.bfloat16)
    low = (products - high.astype(jnp.float32)).astype(jnp.bfloat16)
    across = (((1,), (1,)), ((), ()))
    return lax.dot_general(
        ones, high, across, preferred_element_type=jnp.float32
    ) + lax.dot_general(ones, low, across, preferred_element_type=jnp.float32)


def adjoint_kernel(
    fade_ref,
    fed_ref,
    up_ref,
    in_ref,
    out_ref,
    rate_ref,
    h_ref,
    last_ref,
    weighted_ref,
    pulled_ref,
    d_in_ref,
    d_out_ref,
    d_rate_ref,
    flow_ref,
    now_ref,
    in_part_ref,
    out_part_ref,
):
    chunk, width = fade_ref.shape
    halves, groups = rate_ref.shape[0] // SUB, width // LANES

    @pl.when(pl.program_id(0) == 0)
    def _():
        flow_ref[...] = jnp.zeros_like(flow_ref)
        d_rate_ref[...] = jnp.zeros_like(d_rate_ref)
        now_ref[...] = last_ref[...]

    rate = blocks(rate_ref, halves, groups)
    flow = blocks(flow_ref, halves, groups)
    d_rate = blocks(d_rate_ref, halves, groups)
    now = blocks(now_ref, halves, groups)
    bits = sublane_bits()
    for base in range(chunk - SUB, -SUB, -SUB):
        fade = [fade_ref[base : base + SUB, span(g)] for g in range(groups)]
        fed = [fed_ref[base : base + SUB, span(g)] for g in range(groups)]
        up = [up_ref[base : base + SUB, span(g)] for g in range(groups)]
        weighted = [[] for _ in range(groups)]
        slopes = [[] for _ in range(groups)]
        for r in range(SUB - 1, -1, -1):
            t = base + r
            in_col, out_col = column(in_ref, halves, t), column(out_ref, halves, t)
            in_parts = [[] for _ in range(halves)]
            out_parts = [[] for _ in range(halves)]
            for g in range(groups):
                fade_row, fed_row, up_row = row(fade[g], r), row(fed[g], r), row(up[g], r)
                by_in, by_rate = [], []
                for i in range(halves):
                    place = (t * halves + i) * SUB
                    before = h_ref[place : place + SUB, span(g)]
                    factor = jnp.exp2(fade_row * rate[i][g])
                    adjoint = out_col[i] * up_row + flow[i][g]
                    out_parts[i].append(now[i][g] * up_row)
                    in_parts[i].append(adjoint * fed_row)
                    flow[i][g] = factor * adjoint
                    pulled = flow[i][g] * before
                    by_in.append(adjoint * in_col[i])
                    by_rate.append(pulled * rate[i][g])
                    d_rate[i][g] = d_rate[i][g] + pulled * fade_row
                    now[i][g] = before
                fold(weighted[g], total(by_in), bits, True)
                fold(slopes[g], total(by_rate), bits, True)
            for i in range(halves):
                place = (t * halves + i) * SUB
                in_part_ref[place : place + SUB, :] = total(in_parts[i])
                out_part_ref[place : place + SUB, :] = total(out_parts[i])
        for g in range(groups):
            weighted_ref[base : base + SUB, span(g)] = weighted[g][0][1]
            pulled_ref[base : base + SUB, span(g)] = slopes[g][0][1]
    put_blocks(flow_ref, flow)
    put_blocks(d_rate_ref, d_rate)
    put_blocks(now_ref, now)
    d_in_ref[...] = lane_sums(in_part_ref[...])
    d_out_ref[...] = lane_sums(out_part_ref[...])


def fwd(fading, fed, in_coef, out_coef, rates, **unused):
    tokens, width = fading.shape
    states = rates.shape[0]
    by_row = lambda size: pl.BlockSpec((size, width), lambda c: (c, 0))
    cols = pl.BlockSpec((states, CHUNK), lambda c: (0, c))
    whole = pl.BlockSpec((states, width), lambda c: (0, 0))
    like = jax.ShapeDtypeStruct
    work = tokens * states * width
    return pl.pallas_call(
        scan_kernel,
        grid=(tokens // CHUNK,),
        in_specs=[by_row(CHUNK), by_row(CHUNK), cols, cols, whole],
        out_specs=[by_row(CHUNK), by_row(CHUNK * states), whole],
        out_shape=[
            like((tokens, width), jnp.float32),
            like((tokens * states, width), jnp.float32),
            like((states, width), jnp.float32),
        ],
        scratch_shapes=[pltpu.VMEM((states, width), jnp.float32)],
        compiler_params=pltpu.CompilerParams(
            dimension_semantics=("arbitrary",), vmem_limit_bytes=40 << 20
        ),
        cost_estimate=pl.CostEstimate(flops=2400 * work, bytes_accessed=6 * work, transcendentals=work),
        name="scan",
    )(fading, fed, in_coef, out_coef, rates)


def bwd(fading, fed, upstream, in_coef, out_coef, rates, history, last):
    tokens, width = fading.shape
    states = rates.shape[0]
    count = tokens // CHUNK
    by_row = lambda size: pl.BlockSpec((size, width), lambda c: (count - 1 - c, 0))
    cols = pl.BlockSpec((states, CHUNK), lambda c: (0, count - 1 - c))
    flat = pl.BlockSpec((SUB, CHUNK * states), lambda c: (0, count - 1 - c))
    whole = pl.BlockSpec((states, width), lambda c: (0, 0))
    like = jax.ShapeDtypeStruct
    work = tokens * states * width
    weighted, pulled, d_in, d_out, d_rate = pl.pallas_call(
        adjoint_kernel,
        grid=(count,),
        in_specs=[by_row(CHUNK)] * 3 + [cols, cols, whole, by_row(CHUNK * states), whole],
        out_specs=[by_row(CHUNK), by_row(CHUNK), flat, flat, whole],
        out_shape=[like((tokens, width), jnp.float32)] * 2
        + [like((SUB, tokens * states), jnp.float32)] * 2
        + [like((states, width), jnp.float32)],
        scratch_shapes=[pltpu.VMEM((states, width), jnp.float32)] * 2
        + [pltpu.VMEM((CHUNK * states, LANES), jnp.float32)] * 2,
        compiler_params=pltpu.CompilerParams(
            dimension_semantics=("arbitrary",), vmem_limit_bytes=40 << 20
        ),
        cost_estimate=pl.CostEstimate(flops=4800 * work, bytes_accessed=8 * work, transcendentals=work),
        name="adjoint",
    )(fading, fed, upstream, in_coef, out_coef, rates, history, last)
    by_state = lambda flat_sums: flat_sums[0].reshape(tokens, states).T
    return weighted, pulled, by_state(d_in), by_state(d_out), d_rate


EPS = 1e-05
GONE = 1e4
LOG2E = 1.4426950408889634
BF16 = jnp.bfloat16
F32 = jnp.float32


def swap(array, axis, k):
    size = lax.axis_size(axis)
    return lax.ppermute(array, axis, [(i, i ^ k) for i in range(size)])


def after(value, *others):
    return lax.optimization_barrier((value, others))[0]


def pieces_over(array, axis, hold=None):
    pieces = [array] + [swap(array, axis, k) for k in range(1, lax.axis_size(axis))]
    return pieces if hold is None else [after(piece, hold) for piece in pieces]


def assemble(pieces, axis, dim):
    me, size = lax.axis_index(axis), pieces[0].shape[dim]
    shape = pieces[0].shape[:dim] + (size * len(pieces),) + pieces[0].shape[dim + 1 :]
    out = jnp.zeros(shape, pieces[0].dtype)
    for k, piece in enumerate(pieces):
        out = lax.dynamic_update_slice_in_dim(out, piece, (me ^ k) * size, dim)
    return row_major(out)


def gather(array, axis, dim, hold=None):
    return assemble(pieces_over(array, axis, hold), axis, dim)


def row_major(array):
    return with_layout_constraint(array, Layout(major_to_minor=tuple(range(array.ndim))))


def piece_of(array, axis, dim, index):
    size = array.shape[dim] // lax.axis_size(axis)
    return lax.dynamic_slice_in_dim(array, index * size, size, dim)


def shares(array, axis, dim, kind):
    me = lax.axis_index(axis)
    own = piece_of(array, axis, dim, me).astype(F32)
    sent = [
        piece_of(array, axis, dim, me ^ k).astype(kind) for k in range(1, lax.axis_size(axis))
    ]
    return own, sent


def collect(own, sent, axis):
    return total([own] + [swap(part, axis, k + 1).astype(F32) for k, part in enumerate(sent)])


def scatter_sum(array, axis, dim, kind):
    return collect(*shares(array, axis, dim, kind), axis)


def doubling_sum(array, axes):
    for axis in axes:
        k = 1
        while k < lax.axis_size(axis):
            array = array + swap(array, axis, k)
            k *= 2
    return array


def dot(left, right, left_dim=1, right_dim=0):
    return lax.dot_general(left, right, (((left_dim,), (right_dim,)), ((), ())), preferred_element_type=F32)


def silu_slope(v):
    s = jax.nn.sigmoid(v)
    return s * (1.0 + v * (1.0 - s))


def inverse_rms(x):
    return lax.rsqrt(jnp.mean(x * x, axis=-1, keepdims=True) + EPS)


def shards(
    block_input,
    doc_ids,
    norm_gain,
    in_proj,
    conv_weight,
    conv_bias,
    x_proj,
    dt_proj,
    dt_bias,
    a_log,
    d_skip,
    out_proj,
    grad_output,
):
    seqs, piece, width = block_input.shape
    length = doc_ids.shape[1]
    ctx, ctxs = lax.axis_index("context"), lax.axis_size("context")
    taps, tail = conv_weight.shape[0], conv_weight.shape[0] - 1
    states = a_log.shape[0]
    rows = seqs * length
    inner = in_proj.shape[2] // ctxs
    rank = dt_proj.shape[0] * lax.axis_size("fsdp")

    def mine(array, dim):
        return piece_of(array, "context", dim, ctx)

    in_half = mine(in_proj, 2)
    xcols, dtrows, share = x_proj.shape[1], dt_proj.shape[0], in_proj.shape[1]
    x_own = block_input.reshape(seqs * piece, width).astype(F32)
    normed_own = (x_own * inverse_rms(x_own) * norm_gain).astype(BF16)
    first = pieces_over(
        jnp.concatenate([mine(x_proj, 0).T, mine(dt_proj, 1), in_half[0]], axis=0),
        "fsdp",
        normed_own,
    )
    w_x = assemble([p[:xcols] for p in first], "fsdp", 0)
    w_dt = assemble([p[xcols : xcols + dtrows] for p in first], "fsdp", 0)
    w_conv = assemble([p[xcols + dtrows :] for p in first], "fsdp", 0)
    normed = [normed_own] + [swap(normed_own, "context", k) for k in range(1, ctxs)]
    def whole_tokens(parts):
        out = jnp.zeros((seqs, length, parts[0].shape[-1]), parts[0].dtype)
        for k, part in enumerate(parts):
            part = part.reshape(seqs, piece, part.shape[-1])
            out = lax.dynamic_update_slice_in_dim(out, part, (ctx ^ k) * piece, 1)
        return out.reshape(rows, -1)

    def token_parts(array):
        array = array.reshape(seqs, length, array.shape[-1])
        parts = [piece_of(array, "context", 1, ctx ^ k) for k in range(ctxs)]
        return [part.reshape(seqs * piece, -1) for part in parts]

    def over_tokens(left, right):
        return total([dot(l, r, 0, 0) for l, r in zip(left, right)])

    taps_w, bias, dt_b = mine(conv_weight, 1), mine(conv_bias, 0), mine(dt_bias, 0)
    rates = -jnp.exp(mine(a_log, 1))
    skip = mine(d_skip, 0)

    conv_input = whole_tokens([dot(part, w_conv).astype(BF16) for part in normed])
    padded_ids = jnp.concatenate([jnp.full((seqs, tail), -1, jnp.int32), doc_ids], axis=1)
    same = [
        (padded_ids[:, tail - k : tail - k + length] == doc_ids).astype(F32)[..., None]
        for k in range(taps)
    ]
    padded = jnp.pad(conv_input.reshape(seqs, length, inner), ((0, 0), (tail, 0), (0, 0))).astype(F32)
    shifted = [padded[:, tail - k : tail - k + length] for k in range(taps)]
    conv_output = bias
    for k in range(taps):
        conv_output = conv_output + taps_w[k] * shifted[k] * same[k]
    conv_flat = conv_output.reshape(rows, inner)
    activated = jax.nn.silu(conv_flat).astype(BF16)
    act = activated.astype(F32)
    def all_sum(part):
        halved = scatter_sum(part, "context", 1, F32)
        summed = scatter_sum(halved, "tensor", 1, BF16).astype(BF16)
        return gather(gather(summed, "tensor", 1), "context", 1), halved

    projections, halved = all_sum(dot(w_x, activated, 1, 1))
    w_gate = after(
        lax.all_gather(after(in_half[1], first), "fsdp", axis=0, tiled=True), halved
    )
    w_out = lax.all_gather(after(mine(out_proj, 0).T, w_gate), "fsdp", axis=0, tiled=True)
    own_cotangent = grad_output.reshape(seqs * piece, width)
    cotangent = [own_cotangent] + [
        swap(after(own_cotangent, conv_input), "context", k) for k in range(1, ctxs)
    ]
    dt_input = projections[:rank]
    in_coef = projections[rank : rank + states].astype(F32)
    out_coef = projections[rank + states :].astype(F32)
    dt_logits = dot(dt_input, w_dt, 0, 0) + dt_b
    steps = jax.nn.softplus(dt_logits)
    keep = same[1].reshape(rows, 1)
    fading = jnp.where(keep > 0, steps, GONE)
    fed = steps * act
    rates2 = rates * LOG2E
    w_out = after(w_out, fading)
    scanned, history, last = fwd(fading, fed, in_coef, out_coef, rates2)

    gate = whole_tokens([dot(part, w_gate) for part in normed])
    gate_value = jax.nn.silu(gate)
    mixed = scanned + skip * act
    gated = (mixed * gate_value).astype(BF16)
    d_gated = whole_tokens([dot(part, w_out) for part in cotangent])
    d_mixed = d_gated * gate_value
    d_gate = (d_gated * mixed * silu_slope(gate)).astype(BF16)

    def my_tokens(parts):
        return [parts[0]] + [swap(parts[k], "context", k) for k in range(1, ctxs)]

    def all_halves(weight):
        return [weight] + [swap(weight, "context", k) for k in range(1, ctxs)]

    zplace = lax.axis_index("tensor")
    x_flat = block_input.reshape(seqs * piece, width)
    gated_parts = token_parts(gated)
    branch = dot(
        jnp.concatenate(my_tokens(gated_parts), axis=1),
        jnp.concatenate(all_halves(w_out), axis=1),
        1,
        1,
    ).astype(BF16)
    branch, d_mixed = after((branch, d_mixed))
    branch = lax.psum_scatter(branch, "tensor", scatter_dimension=0, tiled=True).astype(F32)

    in_weighted, d_fade, d_in_coef, d_out_coef, d_rates = bwd(
        fading, fed, d_mixed, in_coef, out_coef, rates2, history, last
    )
    in_weighted, d_fade, branch = after((in_weighted, d_fade, branch))
    x_rows = piece_of(x_flat, "tensor", 0, zplace).astype(F32)
    output_rows = (x_rows + branch).astype(BF16)
    d_step = d_fade * (1.0 / LOG2E) + act * in_weighted
    d_logits = (d_step * jax.nn.sigmoid(dt_logits)).astype(BF16)
    d_part = jnp.concatenate([dot(w_dt, d_logits, 1, 1), d_in_coef, d_out_coef], axis=0)
    d_part, output_rows = after((d_part, output_rows))
    block_output = lax.all_gather(output_rows[None], "tensor", axis=1, tiled=True)
    d_projections, halved = all_sum(d_part)
    gated_parts, d_gate = after((gated_parts, d_gate), halved)
    grad_out_part = over_tokens(cotangent, gated_parts)
    gate_parts = token_parts(d_gate)
    grad_gate_part = over_tokens(normed, gate_parts)
    grad_dt_part = dot(dt_input, d_logits)
    d_act = d_mixed * skip + steps * in_weighted + dot(d_projections, w_x, 0, 0)
    grad_x_part = dot(d_projections, activated)
    d_conv = (d_act * silu_slope(conv_flat)).reshape(seqs, length, inner)
    d_conv_input = jnp.zeros((seqs, length, inner), F32)
    tap_grads = []
    for k in range(taps):
        masked = d_conv * same[k]
        late = jnp.pad(masked, ((0, 0), (0, tail), (0, 0)))[:, k : k + length]
        d_conv_input = d_conv_input + taps_w[k] * late
        tap_grads.append(jnp.sum(masked * shifted[k], axis=(0, 1)))
    d_conv_input = d_conv_input.reshape(rows, inner).astype(BF16)
    conv_parts = token_parts(d_conv_input)
    left = jnp.concatenate(my_tokens(gate_parts) + my_tokens(conv_parts), axis=1)
    right = jnp.concatenate(all_halves(w_gate) + all_halves(w_conv), axis=1)
    partial = dot(left, right, 1, 1).astype(BF16)
    own_rows, sent_rows = shares(partial, "tensor", 0, BF16)
    grad_conv_part = over_tokens(normed, after(conv_parts, sent_rows))
    d_normed = collect(own_rows, sent_rows, "tensor")
    d_rows = piece_of(own_cotangent, "tensor", 0, zplace).astype(F32)
    inv = inverse_rms(x_rows)
    scaled = d_normed * norm_gain
    inner_sum = jnp.sum(scaled * x_rows, axis=-1, keepdims=True)
    grad_rows = d_rows + inv * scaled - x_rows * (inv * inv * inv) * inner_sum / width
    grad_rows, block_output = after((grad_rows.astype(BF16), block_output))
    gain = jnp.sum(d_normed * x_rows * inv, axis=0)
    devices = lax.axis_size("fsdp")

    def owned(*parts):
        pieces = [part.reshape(devices, -1, inner).astype(BF16) for part in parts]
        pieces = row_major(jnp.concatenate(pieces, axis=1).reshape(-1, inner))
        return lax.psum_scatter(pieces, "fsdp", scatter_dimension=0, tiled=True)

    early = owned(*after((grad_gate_part, grad_out_part), sent_rows, block_output))
    late = owned(grad_x_part, grad_dt_part, grad_conv_part)
    thin = jnp.concatenate(
        [
            d_rates * rates,
            jnp.stack(tap_grads),
            jnp.sum(d_conv, axis=(0, 1))[None],
            jnp.sum(d_logits.astype(F32), axis=0)[None],
            jnp.sum(d_mixed * act, axis=0)[None],
            gain.reshape(-1, inner),
        ],
        axis=0,
    )
    channels = states + taps + 3
    thin = doubling_sum(thin, ("fsdp",))
    others = [thin] + [swap(thin, "context", k) for k in range(1, ctxs)]
    gain = total([part[channels:] for part in others]).reshape(1, width)
    terms = []
    for _ in range(3):
        terms.append(gain.astype(BF16))
        gain = gain - terms[-1].astype(F32)
    half = grad_rows.shape[0] // 2
    fill = jnp.zeros((SUB * 2 - len(terms), width), BF16)
    early_rows = gather(grad_rows[:half], "tensor", 0).reshape(-1, half, width)
    late_rows = gather(jnp.concatenate([grad_rows[half:]] + terms + [fill]), "tensor", 0)
    late_rows = late_rows.reshape(-1, half + SUB * 2, width)
    grad_gain = total(
        [jnp.sum(late_rows[:, half + i].astype(F32), axis=0) for i in range(len(terms) - 1, -1, -1)]
    )
    grad_input = jnp.concatenate([early_rows, late_rows[:, :half]], axis=1).reshape(block_input.shape)

    def side_by_side(parts, dim):
        size = parts[0].shape[dim]
        shape = parts[0].shape[:dim] + (size * ctxs,) + parts[0].shape[dim + 1 :]
        out = jnp.zeros(shape, parts[0].dtype)
        for k, part in enumerate(parts):
            out = lax.dynamic_update_slice_in_dim(out, part, (ctx ^ k) * size, dim)
        return out

    thin = side_by_side([part[:channels] for part in others], 1)
    early, late = [
        [sums] + [swap(sums, "context", k) for k in range(1, ctxs)] for sums in (early, late)
    ]
    grad_in = jnp.stack(
        [
            side_by_side([part[xcols + dtrows :].astype(F32) for part in late], 1),
            side_by_side([part[:share].astype(F32) for part in early], 1),
        ]
    )
    grad_out = side_by_side([part[share:].T.astype(F32) for part in early], 0)
    grad_x = side_by_side([part[:xcols].T.astype(F32) for part in late], 0)
    grad_dt = side_by_side([part[xcols : xcols + dtrows].astype(F32) for part in late], 1)
    return (
        block_output.reshape(block_input.shape),
        grad_input,
        grad_gain,
        grad_in,
        thin[states : states + taps],
        thin[states + taps],
        grad_x,
        grad_dt,
        thin[states + taps + 1],
        thin[:states],
        thin[states + taps + 2],
        grad_out,
    )


def solution(mesh):
    placed = (
        P("fsdp", "context", None),
        P("fsdp", None),
        P(),
        P(None, "fsdp", "tensor"),
        P(None, "tensor"),
        P("tensor"),
        P("tensor", "fsdp"),
        P("fsdp", "tensor"),
        P("tensor"),
        P(None, "tensor"),
        P("tensor"),
        P("tensor", "fsdp"),
        P("fsdp", "context", None),
    )
    return jax.shard_map(
        shards,
        mesh=mesh,
        in_specs=placed,
        out_specs=(
            P("fsdp", "context", None),
            P("fsdp", "context", None),
            P(),
            P(None, "fsdp", "tensor"),
            P(None, "tensor"),
            P("tensor"),
            P("tensor", "fsdp"),
            P("fsdp", "tensor"),
            P("tensor"),
            P(None, "tensor"),
            P("tensor"),
            P("tensor", "fsdp"),
        ),
        check_vma=False,
    )
```

```python
import functools

import jax
import jax.numpy as jnp
from jax import lax
from jax.experimental import pallas as pl
from jax.experimental.layout import Layout, with_layout_constraint
from jax.experimental.pallas import tpu as pltpu
from jax.sharding import PartitionSpec as P

LANES = 128
SUB = 8
CHUNK = 128
VMEM_LIMIT = 40 << 20
GONE = 1e4
LOG2E = 1.4426950408889634


def span(group):
    return slice(group * LANES, (group + 1) * LANES)


def blocks(ref, halves, groups):
    return [[ref[SUB * i : SUB * i + SUB, span(g)] for g in range(groups)] for i in range(halves)]


def put_blocks(ref, values):
    for i, line in enumerate(values):
        for g, value in enumerate(line):
            ref[SUB * i : SUB * i + SUB, span(g)] = value


def column(ref, halves, t):
    return [
        jnp.broadcast_to(ref[SUB * i : SUB * i + SUB, t : t + 1], (SUB, LANES))
        for i in range(halves)
    ]


def row(tile, r):
    return jnp.broadcast_to(tile[r : r + 1, :], (SUB, LANES))


def sublane_bits():
    index = lax.broadcasted_iota(jnp.int32, (SUB, LANES), 0)
    return [(index & d) == 0 for d in (1, 2, 4)]


def fold(pending, value, bits, falling):
    level = 0
    while pending and pending[-1][0] == level:
        _, other = pending.pop()
        early, late = (value, other) if falling else (other, value)
        d = 1 << level
        if d < 4:
            value = jnp.where(
                bits[level], early + pltpu.roll(early, SUB - d, 0), late + pltpu.roll(late, d, 0)
            )
        else:
            value = jnp.where(bits[level], early, late) + pltpu.roll(
                jnp.where(bits[level], late, early), d, 0
            )
        level += 1
    pending.append((level, value))


def total(values):
    return functools.reduce(lambda a, b: a + b, values)


def soft_step(v):
    small = jnp.exp(-jnp.abs(v))
    slope = jnp.where(v >= 0, 1.0, small) / (1.0 + small)
    return jnp.maximum(v, 0.0) + jnp.log1p(small), slope


def step_rows(steps, act, keep_ref, fade_ref, fed_ref):
    for g in range(steps.shape[1] // LANES):
        fade_ref[:, span(g)] = jnp.where(keep_ref[...] > 0, steps[:, span(g)], GONE)
    fed_ref[...] = steps * act


def scan_kernel(
    proj_ref,
    act_ref,
    gate_ref,
    keep_ref,
    rate_ref,
    w_dt_ref,
    bias_ref,
    skip_ref,
    gated_ref,
    sloped_ref,
    steps_ref,
    slope_ref,
    h_ref,
    last_ref,
    state_ref,
    fade_ref,
    fed_ref,
    y_ref,
    coef_ref,
):
    chunk, width = act_ref.shape
    halves, groups = rate_ref.shape[0] // SUB, width // LANES
    states, rank = rate_ref.shape[0], w_dt_ref.shape[0]

    @pl.when(pl.program_id(0) == 0)
    def _():
        state_ref[...] = jnp.zeros_like(state_ref)

    logits = (
        lax.dot_general(
            proj_ref[:rank, :],
            w_dt_ref[...],
            (((0,), (0,)), ((), ())),
            preferred_element_type=jnp.float32,
        )
        + bias_ref[...]
    )
    steps, slope_ref[...] = soft_step(logits)
    steps_ref[...] = steps
    step_rows(steps, act_ref[...].astype(jnp.float32), keep_ref, fade_ref, fed_ref)
    coef_ref[...] = proj_ref[rank:, :].astype(jnp.float32)
    in_ref, out_ref = coef_ref.at[:states], coef_ref.at[states:]
    rate = blocks(rate_ref, halves, groups)
    state = blocks(state_ref, halves, groups)
    bits = sublane_bits()
    for base in range(0, chunk, SUB):
        fade = [fade_ref[base : base + SUB, span(g)] for g in range(groups)]
        fed = [fed_ref[base : base + SUB, span(g)] for g in range(groups)]
        pending = [[] for _ in range(groups)]
        for r in range(SUB):
            t = base + r
            in_col, out_col = column(in_ref, halves, t), column(out_ref, halves, t)
            for g in range(groups):
                fade_row, fed_row = row(fade[g], r), row(fed[g], r)
                parts = []
                for i in range(halves):
                    place = (t * halves + i) * SUB
                    h_ref[place : place + SUB, span(g)] = state[i][g]
                    factor = jnp.exp2(fade_row * rate[i][g])
                    state[i][g] = factor * state[i][g] + fed_row * in_col[i]
                    parts.append(state[i][g] * out_col[i])
                fold(pending[g], total(parts), bits, False)
        for g in range(groups):
            y_ref[base : base + SUB, span(g)] = pending[g][0][1]
    put_blocks(state_ref, state)
    last_ref[...] = state_ref[...]
    mixed = y_ref[...] + skip_ref[...] * act_ref[...].astype(jnp.float32)
    gate = gate_ref[...]
    sigmoid = jax.nn.sigmoid(gate)
    gated_ref[...] = (mixed * (gate * sigmoid)).astype(jnp.bfloat16)
    sloped_ref[...] = mixed * (sigmoid * (1.0 + gate * (1.0 - sigmoid)))


def lane_sums(products_ref, states):
    ones = jnp.ones((LANES, LANES), jnp.bfloat16)
    sums = jnp.dot(products_ref[...], ones, preferred_element_type=jnp.float32)
    lane = lax.broadcasted_iota(jnp.int32, (states, LANES), 1)
    result = jnp.zeros((states, LANES), jnp.float32)
    for t in range(CHUNK):
        result = jnp.where(lane == t, sums[t * states : (t + 1) * states], result)
    return result


def adjoint_kernel(
    proj_ref,
    act_ref,
    steps_ref,
    slope_ref,
    up_ref,
    keep_ref,
    rate_ref,
    w_dt_ref,
    skip_ref,
    h_ref,
    last_ref,
    d_logits_ref,
    d_act_ref,
    d_proj_ref,
    d_rate_ref,
    d_bias_ref,
    d_skip_ref,
    flow_ref,
    now_ref,
    in_part_ref,
    out_part_ref,
    fade_ref,
    fed_ref,
    weighted_ref,
    pulled_ref,
    coef_ref,
):
    chunk, width = act_ref.shape
    halves, groups = rate_ref.shape[0] // SUB, width // LANES
    states, rank = rate_ref.shape[0], w_dt_ref.shape[0]

    @pl.when(pl.program_id(0) == 0)
    def _():
        flow_ref[...] = jnp.zeros_like(flow_ref)
        d_rate_ref[...] = jnp.zeros_like(d_rate_ref)
        d_bias_ref[...] = jnp.zeros_like(d_bias_ref)
        d_skip_ref[...] = jnp.zeros_like(d_skip_ref)
        now_ref[...] = last_ref[...]

    step_rows(steps_ref[...], act_ref[...].astype(jnp.float32), keep_ref, fade_ref, fed_ref)
    coef_ref[...] = proj_ref[rank:, :].astype(jnp.float32)
    in_ref, out_ref = coef_ref.at[:states], coef_ref.at[states:]
    rate = blocks(rate_ref, halves, groups)
    flow = blocks(flow_ref, halves, groups)
    d_rate = blocks(d_rate_ref, halves, groups)
    now = blocks(now_ref, halves, groups)
    bits = sublane_bits()
    for base in range(chunk - SUB, -SUB, -SUB):
        fade = [fade_ref[base : base + SUB, span(g)] for g in range(groups)]
        fed = [fed_ref[base : base + SUB, span(g)] for g in range(groups)]
        up = [up_ref[base : base + SUB, span(g)] for g in range(groups)]
        weighted = [[] for _ in range(groups)]
        slopes = [[] for _ in range(groups)]
        for r in range(SUB - 1, -1, -1):
            t = base + r
            in_col, out_col = column(in_ref, halves, t), column(out_ref, halves, t)
            in_parts = [[] for _ in range(halves)]
            out_parts = [[] for _ in range(halves)]
            for g in range(groups):
                fade_row, fed_row, up_row = row(fade[g], r), row(fed[g], r), row(up[g], r)
                by_in, by_rate = [], []
                for i in range(halves):
                    place = (t * halves + i) * SUB
                    before = h_ref[place : place + SUB, span(g)]
                    factor = jnp.exp2(fade_row * rate[i][g])
                    adjoint = out_col[i] * up_row + flow[i][g]
                    out_parts[i].append(now[i][g] * up_row)
                    in_parts[i].append(adjoint * fed_row)
                    flow[i][g] = factor * adjoint
                    pulled = flow[i][g] * before
                    by_in.append(adjoint * in_col[i])
                    by_rate.append(pulled * rate[i][g])
                    d_rate[i][g] = d_rate[i][g] + pulled * fade_row
                    now[i][g] = before
                fold(weighted[g], total(by_in), bits, True)
                fold(slopes[g], total(by_rate), bits, True)
            place = slice(t * states, (t + 1) * states)
            for ref, parts in ((in_part_ref, in_parts), (out_part_ref, out_parts)):
                ref[place, :] = jnp.concatenate([total(part) for part in parts]).astype(jnp.bfloat16)
        for g in range(groups):
            weighted_ref[base : base + SUB, span(g)] = weighted[g][0][1]
            pulled_ref[base : base + SUB, span(g)] = slopes[g][0][1]
    put_blocks(flow_ref, flow)
    put_blocks(d_rate_ref, d_rate)
    put_blocks(now_ref, now)
    d_proj_ref[rank : rank + states, :] = lane_sums(in_part_ref, states)
    d_proj_ref[rank + states :, :] = lane_sums(out_part_ref, states)
    act = act_ref[...].astype(jnp.float32)
    d_step = pulled_ref[...] * (1.0 / LOG2E) + act * weighted_ref[...]
    d_logits = (d_step * slope_ref[...]).astype(jnp.bfloat16)
    d_logits_ref[...] = d_logits
    d_bias_ref[...] += jnp.sum(d_logits.astype(jnp.float32), axis=0, keepdims=True)
    d_skip_ref[...] += jnp.sum(up_ref[...] * act, axis=0, keepdims=True)
    d_act_ref[...] = up_ref[...] * skip_ref[...] + steps_ref[...] * weighted_ref[...]
    d_proj_ref[:rank, :] = lax.dot_general(
        w_dt_ref[...],
        d_logits,
        (((1,), (1,)), ((), ())),
        preferred_element_type=jnp.float32,
    )


def cost(scale, tokens, states, width):
    work = tokens * states * width
    return pl.CostEstimate(flops=scale * work, bytes_accessed=8 * work, transcendentals=work)


def whole(array):
    return pl.BlockSpec(array.shape, lambda c: (0,) * len(array.shape))


def scan(proj, act, gate, keep, rates, w_dt, bias, skip):
    tokens, width = act.shape
    states = rates.shape[0]
    by_row = lambda size, wide: pl.BlockSpec((size, wide), lambda c: (c, 0))
    like = jax.ShapeDtypeStruct
    scratch = lambda *shape: pltpu.VMEM(shape, jnp.float32)
    state = like((states, width), jnp.float32)
    return pl.pallas_call(
        scan_kernel,
        grid=(tokens // CHUNK,),
        in_specs=[
            pl.BlockSpec((proj.shape[0], CHUNK), lambda c: (0, c)),
            by_row(CHUNK, width),
            by_row(CHUNK, width),
            by_row(CHUNK, LANES),
            whole(rates),
            whole(w_dt),
            whole(bias),
            whole(skip),
        ],
        out_specs=[by_row(CHUNK, width)] * 4 + [by_row(CHUNK * states, width), whole(state)],
        out_shape=[
            like((tokens, width), jnp.bfloat16),
            like((tokens, width), jnp.float32),
            like((tokens, width), jnp.float32),
            like((tokens, width), jnp.float32),
            like((tokens * states, width), jnp.float32),
            state,
        ],
        scratch_shapes=[scratch(states, width)]
        + [scratch(CHUNK, width)] * 3
        + [scratch(2 * states, CHUNK)],
        compiler_params=pltpu.CompilerParams(
            dimension_semantics=("arbitrary",), vmem_limit_bytes=VMEM_LIMIT
        ),
        cost_estimate=cost(2400, tokens, states, width),
        name="scan",
    )(proj, act, gate, keep, rates, w_dt, bias, skip)


def adjoint(proj, act, steps, slope, upstream, keep, rates, w_dt, skip, history, last):
    tokens, width = act.shape
    states = rates.shape[0]
    count = tokens // CHUNK
    by_row = lambda size, wide: pl.BlockSpec((size, wide), lambda c: (count - 1 - c, 0))
    cols = pl.BlockSpec((proj.shape[0], CHUNK), lambda c: (0, count - 1 - c))
    like = jax.ShapeDtypeStruct
    scratch = lambda *shape: pltpu.VMEM(shape, jnp.float32)
    line = like((1, width), jnp.float32)
    return pl.pallas_call(
        adjoint_kernel,
        grid=(count,),
        in_specs=[cols]
        + [by_row(CHUNK, width)] * 4
        + [by_row(CHUNK, LANES), whole(rates), whole(w_dt), whole(skip)]
        + [by_row(CHUNK * states, width), whole(last)],
        out_specs=[by_row(CHUNK, width)] * 2 + [cols, whole(last), whole(line), whole(line)],
        out_shape=[
            like((tokens, width), jnp.bfloat16),
            like((tokens, width), jnp.float32),
            like(proj.shape, jnp.float32),
            like(last.shape, jnp.float32),
            line,
            line,
        ],
        scratch_shapes=[scratch(states, width)] * 2
        + [pltpu.VMEM((CHUNK * states, LANES), jnp.bfloat16)] * 2
        + [scratch(CHUNK, width)] * 4
        + [scratch(2 * states, CHUNK)],
        compiler_params=pltpu.CompilerParams(
            dimension_semantics=("arbitrary",), vmem_limit_bytes=VMEM_LIMIT
        ),
        cost_estimate=cost(4800, tokens, states, width),
        name="adjoint",
    )(proj, act, steps, slope, upstream, keep, rates, w_dt, skip, history, last)


EPS = 1e-05
BF16 = jnp.bfloat16
F32 = jnp.float32


def swap(array, axis, k):
    size = lax.axis_size(axis)
    return lax.ppermute(array, axis, [(i, i ^ k) for i in range(size)])


def after(value, *others):
    return lax.optimization_barrier((value, others))[0]


def pieces_over(array, axis, hold=None):
    pieces = [array] + [swap(array, axis, k) for k in range(1, lax.axis_size(axis))]
    return pieces if hold is None else [after(piece, hold) for piece in pieces]


def assemble(pieces, axis, dim):
    me, size = lax.axis_index(axis), pieces[0].shape[dim]
    shape = pieces[0].shape[:dim] + (size * len(pieces),) + pieces[0].shape[dim + 1 :]
    out = jnp.zeros(shape, pieces[0].dtype)
    for k, piece in enumerate(pieces):
        out = lax.dynamic_update_slice_in_dim(out, piece, (me ^ k) * size, dim)
    return row_major(out)


def gather(array, axis, dim, hold=None):
    return assemble(pieces_over(array, axis, hold), axis, dim)


def row_major(array):
    return with_layout_constraint(array, Layout(major_to_minor=tuple(range(array.ndim))))


def piece_of(array, axis, dim, index):
    size = array.shape[dim] // lax.axis_size(axis)
    return lax.dynamic_slice_in_dim(array, index * size, size, dim)


def shares(array, axis, dim, kind):
    me = lax.axis_index(axis)
    own = piece_of(array, axis, dim, me).astype(F32)
    sent = [
        piece_of(array, axis, dim, me ^ k).astype(kind) for k in range(1, lax.axis_size(axis))
    ]
    return own, sent


def collect(own, sent, axis):
    return total([own] + [swap(part, axis, k + 1).astype(F32) for k, part in enumerate(sent)])


def scatter_sum(array, axis, dim, kind):
    return collect(*shares(array, axis, dim, kind), axis)


def halving_sum(pieces, axis):
    k = 1
    while len(pieces) > 1:
        came = [swap(piece.astype(BF16), axis, k) for piece in pieces[1::2]]
        pieces = [own.astype(F32) + part.astype(F32) for own, part in zip(pieces[::2], came)]
        k *= 2
    return pieces[0]


def doubling_pieces(array, axis):
    k = lax.axis_size(axis) // 2
    pieces = {0: array}
    while k:
        pieces.update({j ^ k: swap(piece, axis, k) for j, piece in pieces.items()})
        k //= 2
    return [pieces[j] for j in range(len(pieces))]


def doubling_sum(array, axes):
    for axis in axes:
        k = 1
        while k < lax.axis_size(axis):
            array = array + swap(array, axis, k)
            k *= 2
    return array


def dot(left, right, left_dim=1, right_dim=0):
    return lax.dot_general(left, right, (((left_dim,), (right_dim,)), ((), ())), preferred_element_type=F32)


def silu_slope(v):
    s = jax.nn.sigmoid(v)
    return s * (1.0 + v * (1.0 - s))


def inverse_rms(x):
    return lax.rsqrt(jnp.mean(x * x, axis=-1, keepdims=True) + EPS)


def shards(
    block_input,
    doc_ids,
    norm_gain,
    in_proj,
    conv_weight,
    conv_bias,
    x_proj,
    dt_proj,
    dt_bias,
    a_log,
    d_skip,
    out_proj,
    grad_output,
):
    seqs, piece, width = block_input.shape
    length = doc_ids.shape[1]
    ctx, ctxs = lax.axis_index("context"), lax.axis_size("context")
    taps, tail = conv_weight.shape[0], conv_weight.shape[0] - 1
    states = a_log.shape[0]
    rows = seqs * length
    inner = in_proj.shape[2] // ctxs
    rank = dt_proj.shape[0] * lax.axis_size("fsdp")

    def mine(array, dim):
        return piece_of(array, "context", dim, ctx)

    in_half = mine(in_proj, 2)
    xcols, dtrows, share = x_proj.shape[1], dt_proj.shape[0], in_proj.shape[1]
    x_own = block_input.reshape(seqs * piece, width).astype(F32)
    normed_own = (x_own * inverse_rms(x_own) * norm_gain).astype(BF16)
    first = pieces_over(
        jnp.concatenate([mine(x_proj, 0).T, mine(dt_proj, 1), in_half[0]], axis=0),
        "fsdp",
        normed_own,
    )
    w_x = assemble([p[:xcols] for p in first], "fsdp", 0)
    w_dt = assemble([p[xcols : xcols + dtrows] for p in first], "fsdp", 0)
    w_conv = assemble([p[xcols + dtrows :] for p in first], "fsdp", 0)
    normed = [normed_own] + [swap(normed_own, "context", k) for k in range(1, ctxs)]
    def whole_tokens(parts):
        out = jnp.zeros((seqs, length, parts[0].shape[-1]), parts[0].dtype)
        for k, part in enumerate(parts):
            part = part.reshape(seqs, piece, part.shape[-1])
            out = lax.dynamic_update_slice_in_dim(out, part, (ctx ^ k) * piece, 1)
        return out.reshape(rows, -1)

    def token_parts(array):
        array = array.reshape(seqs, length, array.shape[-1])
        parts = [piece_of(array, "context", 1, ctx ^ k) for k in range(ctxs)]
        return [part.reshape(seqs * piece, -1) for part in parts]

    def over_tokens(left, right):
        return total([dot(l, r, 0, 0) for l, r in zip(left, right)])

    taps_w, bias, dt_b = mine(conv_weight, 1), mine(conv_bias, 0), mine(dt_bias, 0)
    rates = -jnp.exp(mine(a_log, 1))
    skip = mine(d_skip, 0)

    conv_input = whole_tokens([dot(part, w_conv).astype(BF16) for part in normed])
    padded_ids = jnp.concatenate([jnp.full((seqs, tail), -1, jnp.int32), doc_ids], axis=1)
    same = [
        (padded_ids[:, tail - k : tail - k + length] == doc_ids).astype(F32)[..., None]
        for k in range(taps)
    ]
    padded = jnp.pad(conv_input.reshape(seqs, length, inner), ((0, 0), (tail, 0), (0, 0))).astype(F32)
    shifted = [padded[:, tail - k : tail - k + length] for k in range(taps)]
    conv_output = bias
    for k in range(taps):
        conv_output = conv_output + taps_w[k] * shifted[k] * same[k]
    conv_flat = conv_output.reshape(rows, inner)
    activated = jax.nn.silu(conv_flat).astype(BF16)
    def all_sum(part):
        halved = scatter_sum(part, "context", 1, F32)
        summed = scatter_sum(halved, "tensor", 1, BF16).astype(BF16)
        return gather(gather(summed, "tensor", 1), "context", 1), halved

    projections, halved = all_sum(dot(w_x, activated, 1, 1))
    w_gate = after(
        lax.all_gather(after(in_half[1], first), "fsdp", axis=0, tiled=True), halved
    )
    w_out = lax.all_gather(after(mine(out_proj, 0).T, w_gate), "fsdp", axis=0, tiled=True)
    own_cotangent = grad_output.reshape(seqs * piece, width)
    cotangent = [own_cotangent] + [
        swap(after(own_cotangent, conv_input), "context", k) for k in range(1, ctxs)
    ]
    dt_input = projections[:rank]
    keep = jnp.broadcast_to(same[1].reshape(rows, 1), (rows, LANES))
    w_out = after(w_out, projections)
    gate = whole_tokens([dot(part, w_gate) for part in normed])
    gated, sloped, steps, slope, history, last = scan(
        projections, activated, gate, keep, rates * LOG2E, w_dt, dt_b[None], skip[None]
    )

    def my_tokens(parts):
        return [parts[0]] + [swap(parts[k], "context", k) for k in range(1, ctxs)]

    def all_halves(weight):
        return [weight] + [swap(weight, "context", k) for k in range(1, ctxs)]

    zplace = lax.axis_index("tensor")
    x_flat = block_input.reshape(seqs * piece, width)
    gated_parts = token_parts(gated)
    branch = dot(
        jnp.concatenate(my_tokens(gated_parts), axis=1),
        jnp.concatenate(all_halves(w_out), axis=1),
        1,
        1,
    ).astype(BF16)
    w_out_late = after(w_out, branch)
    d_gated = whole_tokens([dot(part, w_out_late) for part in cotangent])
    d_mixed = d_gated * jax.nn.silu(gate)
    d_gate = (d_gated * sloped).astype(BF16)
    branch = lax.psum_scatter(branch, "tensor", scatter_dimension=0, tiled=True).astype(F32)

    d_logits, d_act, d_part, d_rates, d_bias, d_skips = adjoint(
        projections, activated, steps, slope, d_mixed, keep, rates * LOG2E, w_dt, skip[None],
        history, last,
    )
    grad_out_part = over_tokens(cotangent, gated_parts)
    d_part, branch, grad_out_part = after((d_part, branch, grad_out_part))
    x_rows = piece_of(x_flat, "tensor", 0, zplace).astype(F32)
    output_rows = (x_rows + branch).astype(BF16)
    d_part, output_rows = after((d_part, output_rows))
    block_output = lax.all_gather(output_rows[None], "tensor", axis=1, tiled=True)
    d_projections, halved = all_sum(d_part)
    gate_parts = token_parts(d_gate)
    grad_dt_part = dot(dt_input, d_logits)
    d_act = d_act + dot(d_projections, w_x, 0, 0)
    grad_x_part = dot(d_projections, activated)
    d_conv = (d_act * silu_slope(conv_flat)).reshape(seqs, length, inner)
    d_conv_input = jnp.zeros((seqs, length, inner), F32)
    tap_grads = []
    for k in range(taps):
        masked = d_conv * same[k]
        late = jnp.pad(masked, ((0, 0), (0, tail), (0, 0)))[:, k : k + length]
        d_conv_input = d_conv_input + taps_w[k] * late
        tap_grads.append(jnp.sum(masked * shifted[k], axis=(0, 1)))
    d_conv_input = d_conv_input.reshape(rows, inner).astype(BF16)
    conv_parts = token_parts(d_conv_input)
    left = jnp.concatenate(my_tokens(gate_parts) + my_tokens(conv_parts), axis=1)
    right = jnp.concatenate(all_halves(w_gate) + all_halves(w_conv), axis=1)
    partial = dot(left, right, 1, 1).astype(BF16)
    row_parts = [
        piece_of(partial, "tensor", 0, zplace ^ k) for k in range(lax.axis_size("tensor"))
    ]
    row_parts, block_output = after((row_parts, block_output))
    d_normed = halving_sum(row_parts, "tensor")
    grad_conv_part = over_tokens(normed, conv_parts)
    grad_gate_part = over_tokens(normed, gate_parts)
    d_rows = piece_of(own_cotangent, "tensor", 0, zplace).astype(F32)
    inv = inverse_rms(x_rows)
    scaled = d_normed * norm_gain
    inner_sum = jnp.sum(scaled * x_rows, axis=-1, keepdims=True)
    grad_rows = d_rows + inv * scaled - x_rows * (inv * inv * inv) * inner_sum / width
    grad_rows = grad_rows.astype(BF16)
    gain = jnp.sum(d_normed * x_rows * inv, axis=0)
    devices = lax.axis_size("fsdp")

    def owned(*parts):
        pieces = [part.reshape(devices, -1, inner).astype(BF16) for part in parts]
        fill = -sum(piece.shape[1] for piece in pieces) % LANES
        pieces.append(jnp.zeros((devices, fill, inner), BF16))
        pieces = row_major(jnp.concatenate(pieces, axis=1).reshape(-1, inner))
        return lax.psum_scatter(pieces, "fsdp", scatter_dimension=0, tiled=True)

    sums = owned(grad_conv_part, grad_gate_part, grad_out_part, grad_x_part, grad_dt_part)
    thin = jnp.concatenate(
        [
            d_rates * rates,
            jnp.stack(tap_grads),
            jnp.sum(d_conv, axis=(0, 1))[None],
            d_bias,
            d_skips,
            gain.reshape(-1, inner),
        ],
        axis=0,
    )
    channels = states + taps + 3
    thin = doubling_sum(thin, ("fsdp",))
    others = [thin] + [swap(thin, "context", k) for k in range(1, ctxs)]
    gain = total([part[channels:] for part in others]).reshape(1, width)
    grad_gain = doubling_sum(gain, ("tensor",))[0]
    count = grad_rows.shape[0]
    grad_input = jnp.zeros((count * lax.axis_size("tensor"), width), BF16)
    for k, part in enumerate(doubling_pieces(grad_rows, "tensor")):
        grad_input = lax.dynamic_update_slice_in_dim(grad_input, part, (zplace ^ k) * count, 0)
    grad_input = grad_input.reshape(block_input.shape)

    def side_by_side(parts, dim):
        size = parts[0].shape[dim]
        shape = parts[0].shape[:dim] + (size * ctxs,) + parts[0].shape[dim + 1 :]
        out = jnp.zeros(shape, parts[0].dtype)
        for k, part in enumerate(parts):
            out = lax.dynamic_update_slice_in_dim(out, part, (ctx ^ k) * size, dim)
        return out

    thin = side_by_side([part[:channels] for part in others], 1)
    sums = [sums] + [swap(sums, "context", k) for k in range(1, ctxs)]
    grad_in = side_by_side(
        [part[: 2 * share].reshape(2, share, inner).astype(F32) for part in sums], 2
    )
    grad_out = side_by_side([part[2 * share : 3 * share].T.astype(F32) for part in sums], 0)
    thin_at = 3 * share + xcols
    grad_x = side_by_side([part[3 * share : thin_at].T.astype(F32) for part in sums], 0)
    grad_dt = side_by_side([part[thin_at : thin_at + dtrows].astype(F32) for part in sums], 1)
    return (
        block_output.reshape(block_input.shape),
        grad_input,
        grad_gain,
        grad_in,
        thin[states : states + taps],
        thin[states + taps],
        grad_x,
        grad_dt,
        thin[states + taps + 1],
        thin[:states],
        thin[states + taps + 2],
        grad_out,
    )


def solution(mesh):
    placed = (
        P("fsdp", "context", None),
        P("fsdp", None),
        P(),
        P(None, "fsdp", "tensor"),
        P(None, "tensor"),
        P("tensor"),
        P("tensor", "fsdp"),
        P("fsdp", "tensor"),
        P("tensor"),
        P(None, "tensor"),
        P("tensor"),
        P("tensor", "fsdp"),
        P("fsdp", "context", None),
    )
    return jax.shard_map(
        shards,
        mesh=mesh,
        in_specs=placed,
        out_specs=(
            P("fsdp", "context", None),
            P("fsdp", "context", None),
            P(),
            P(None, "fsdp", "tensor"),
            P(None, "tensor"),
            P("tensor"),
            P("tensor", "fsdp"),
            P("fsdp", "tensor"),
            P("tensor"),
            P(None, "tensor"),
            P("tensor"),
            P("tensor", "fsdp"),
        ),
        check_vma=False,
    )
```

```python
import functools

import jax
import jax.numpy as jnp
from jax import lax
from jax.experimental import pallas as pl
from jax.experimental.layout import Layout, with_layout_constraint
from jax.experimental.pallas import tpu as pltpu
from jax.sharding import PartitionSpec as P

LANES = 128
SUB = 8
CHUNK = 128
VMEM_LIMIT = 56 << 20
GONE = 1e4
LOG2E = 1.4426950408889634


def span(group):
    return slice(group * LANES, (group + 1) * LANES)


def blocks(ref, halves, groups):
    return [[ref[SUB * i : SUB * i + SUB, span(g)] for g in range(groups)] for i in range(halves)]


def put_blocks(ref, values):
    for i, line in enumerate(values):
        for g, value in enumerate(line):
            ref[SUB * i : SUB * i + SUB, span(g)] = value


def column(ref, halves, t):
    return [
        jnp.broadcast_to(ref[SUB * i : SUB * i + SUB, t : t + 1], (SUB, LANES))
        for i in range(halves)
    ]


def row(tile, r):
    return jnp.broadcast_to(tile[r : r + 1, :], (SUB, LANES))


def sublane_bits():
    index = lax.broadcasted_iota(jnp.int32, (SUB, LANES), 0)
    return [(index & d) == 0 for d in (1, 2, 4)]


def fold(pending, value, bits, falling):
    level = 0
    while pending and pending[-1][0] == level:
        _, other = pending.pop()
        early, late = (value, other) if falling else (other, value)
        d = 1 << level
        if d < 4:
            value = jnp.where(
                bits[level], early + pltpu.roll(early, SUB - d, 0), late + pltpu.roll(late, d, 0)
            )
        else:
            value = jnp.where(bits[level], early, late) + pltpu.roll(
                jnp.where(bits[level], late, early), d, 0
            )
        level += 1
    pending.append((level, value))


def total(values):
    return functools.reduce(lambda a, b: a + b, values)


def soft_step(v):
    small = jnp.exp(-jnp.abs(v))
    slope = jnp.where(v >= 0, 1.0, small) / (1.0 + small)
    return jnp.maximum(v, 0.0) + jnp.log1p(small), slope


def step_rows(steps, act, keep_ref, fade_ref, fed_ref):
    for g in range(steps.shape[1] // LANES):
        fade_ref[:, span(g)] = jnp.where(keep_ref[...] > 0, steps[:, span(g)], GONE)
    fed_ref[...] = steps * act


def scan_kernel(
    proj_ref,
    act_ref,
    gate_ref,
    keep_ref,
    rate_ref,
    w_dt_ref,
    bias_ref,
    skip_ref,
    gated_ref,
    sloped_ref,
    steps_ref,
    slope_ref,
    h_ref,
    last_ref,
    state_ref,
    fade_ref,
    fed_ref,
    y_ref,
    coef_ref,
):
    chunk, width = act_ref.shape
    halves, groups = rate_ref.shape[0] // SUB, width // LANES
    states, rank = rate_ref.shape[0], w_dt_ref.shape[0]

    @pl.when(pl.program_id(0) == 0)
    def _():
        state_ref[...] = jnp.zeros_like(state_ref)

    logits = (
        lax.dot_general(
            proj_ref[:rank, :],
            w_dt_ref[...],
            (((0,), (0,)), ((), ())),
            preferred_element_type=jnp.float32,
        )
        + bias_ref[...]
    )
    steps, slope_ref[...] = soft_step(logits)
    steps_ref[...] = steps
    step_rows(steps, act_ref[...].astype(jnp.float32), keep_ref, fade_ref, fed_ref)
    coef_ref[...] = proj_ref[rank:, :].astype(jnp.float32)
    in_ref, out_ref = coef_ref.at[:states], coef_ref.at[states:]
    rate = blocks(rate_ref, halves, groups)
    state = blocks(state_ref, halves, groups)
    bits = sublane_bits()
    for base in range(0, chunk, SUB):
        fade = [fade_ref[base : base + SUB, span(g)] for g in range(groups)]
        fed = [fed_ref[base : base + SUB, span(g)] for g in range(groups)]
        pending = [[] for _ in range(groups)]
        for r in range(SUB):
            t = base + r
            in_col, out_col = column(in_ref, halves, t), column(out_ref, halves, t)
            for g in range(groups):
                fade_row, fed_row = row(fade[g], r), row(fed[g], r)
                parts = []
                for i in range(halves):
                    place = (t * halves + i) * SUB
                    h_ref[place : place + SUB, span(g)] = state[i][g]
                    factor = jnp.exp2(fade_row * rate[i][g])
                    state[i][g] = factor * state[i][g] + fed_row * in_col[i]
                    parts.append(state[i][g] * out_col[i])
                fold(pending[g], total(parts), bits, False)
        for g in range(groups):
            y_ref[base : base + SUB, span(g)] = pending[g][0][1]
    put_blocks(state_ref, state)
    last_ref[...] = state_ref[...]
    mixed = y_ref[...] + skip_ref[...] * act_ref[...].astype(jnp.float32)
    gate = gate_ref[...]
    sigmoid = jax.nn.sigmoid(gate)
    gated_ref[...] = (mixed * (gate * sigmoid)).astype(jnp.bfloat16)
    sloped_ref[...] = mixed * (sigmoid * (1.0 + gate * (1.0 - sigmoid)))


def lane_sums(products_ref, states):
    ones = jnp.ones((LANES, LANES), jnp.bfloat16)
    sums = jnp.dot(products_ref[...], ones, preferred_element_type=jnp.float32)
    lane = lax.broadcasted_iota(jnp.int32, (states, LANES), 1)
    result = jnp.zeros((states, LANES), jnp.float32)
    for t in range(CHUNK):
        result = jnp.where(lane == t, sums[t * states : (t + 1) * states], result)
    return result


def adjoint_kernel(
    proj_ref,
    act_ref,
    steps_ref,
    slope_ref,
    up_ref,
    keep_ref,
    rate_ref,
    w_dt_ref,
    skip_ref,
    h_ref,
    last_ref,
    d_logits_ref,
    d_act_ref,
    d_proj_ref,
    d_rate_ref,
    d_bias_ref,
    d_skip_ref,
    flow_ref,
    now_ref,
    in_part_ref,
    out_part_ref,
    fade_ref,
    fed_ref,
    weighted_ref,
    pulled_ref,
    coef_ref,
):
    chunk, width = act_ref.shape
    halves, groups = rate_ref.shape[0] // SUB, width // LANES
    states, rank = rate_ref.shape[0], w_dt_ref.shape[0]

    @pl.when(pl.program_id(0) == 0)
    def _():
        flow_ref[...] = jnp.zeros_like(flow_ref)
        d_rate_ref[...] = jnp.zeros_like(d_rate_ref)
        d_bias_ref[...] = jnp.zeros_like(d_bias_ref)
        d_skip_ref[...] = jnp.zeros_like(d_skip_ref)
        now_ref[...] = last_ref[...]

    step_rows(steps_ref[...], act_ref[...].astype(jnp.float32), keep_ref, fade_ref, fed_ref)
    coef_ref[...] = proj_ref[rank:, :].astype(jnp.float32)
    in_ref, out_ref = coef_ref.at[:states], coef_ref.at[states:]
    rate = blocks(rate_ref, halves, groups)
    flow = blocks(flow_ref, halves, groups)
    d_rate = blocks(d_rate_ref, halves, groups)
    now = blocks(now_ref, halves, groups)
    bits = sublane_bits()
    for base in range(chunk - SUB, -SUB, -SUB):
        fade = [fade_ref[base : base + SUB, span(g)] for g in range(groups)]
        fed = [fed_ref[base : base + SUB, span(g)] for g in range(groups)]
        up = [up_ref[base : base + SUB, span(g)] for g in range(groups)]
        weighted = [[] for _ in range(groups)]
        slopes = [[] for _ in range(groups)]
        for r in range(SUB - 1, -1, -1):
            t = base + r
            in_col, out_col = column(in_ref, halves, t), column(out_ref, halves, t)
            in_parts = [[] for _ in range(halves)]
            out_parts = [[] for _ in range(halves)]
            for g in range(groups):
                fade_row, fed_row, up_row = row(fade[g], r), row(fed[g], r), row(up[g], r)
                by_in, by_rate = [], []
                for i in range(halves):
                    place = (t * halves + i) * SUB
                    before = h_ref[place : place + SUB, span(g)]
                    factor = jnp.exp2(fade_row * rate[i][g])
                    adjoint = out_col[i] * up_row + flow[i][g]
                    out_parts[i].append(now[i][g] * up_row)
                    in_parts[i].append(adjoint * fed_row)
                    flow[i][g] = factor * adjoint
                    pulled = flow[i][g] * before
                    by_in.append(adjoint * in_col[i])
                    by_rate.append(pulled * rate[i][g])
                    d_rate[i][g] = d_rate[i][g] + pulled * fade_row
                    now[i][g] = before
                fold(weighted[g], total(by_in), bits, True)
                fold(slopes[g], total(by_rate), bits, True)
            place = slice(t * states, (t + 1) * states)
            for ref, parts in ((in_part_ref, in_parts), (out_part_ref, out_parts)):
                ref[place, :] = jnp.concatenate([total(part) for part in parts]).astype(jnp.bfloat16)
        for g in range(groups):
            weighted_ref[base : base + SUB, span(g)] = weighted[g][0][1]
            pulled_ref[base : base + SUB, span(g)] = slopes[g][0][1]
    put_blocks(flow_ref, flow)
    put_blocks(d_rate_ref, d_rate)
    put_blocks(now_ref, now)
    d_proj_ref[rank : rank + states, :] = lane_sums(in_part_ref, states)
    d_proj_ref[rank + states :, :] = lane_sums(out_part_ref, states)
    act = act_ref[...].astype(jnp.float32)
    d_step = pulled_ref[...] * (1.0 / LOG2E) + act * weighted_ref[...]
    d_logits = (d_step * slope_ref[...]).astype(jnp.bfloat16)
    d_logits_ref[...] = d_logits
    d_bias_ref[...] += jnp.sum(d_logits.astype(jnp.float32), axis=0, keepdims=True)
    d_skip_ref[...] += jnp.sum(up_ref[...] * act, axis=0, keepdims=True)
    d_act_ref[...] = up_ref[...] * skip_ref[...] + steps_ref[...] * weighted_ref[...]
    d_proj_ref[:rank, :] = lax.dot_general(
        w_dt_ref[...],
        d_logits,
        (((1,), (1,)), ((), ())),
        preferred_element_type=jnp.float32,
    )


def cost(scale, tokens, states, width):
    work = tokens * states * width
    return pl.CostEstimate(flops=scale * work, bytes_accessed=8 * work, transcendentals=work)


def whole(array):
    return pl.BlockSpec(array.shape, lambda c: (0,) * len(array.shape))


def scan(proj, act, gate, keep, rates, w_dt, bias, skip):
    tokens, width = act.shape
    states = rates.shape[0]
    by_row = lambda size, wide: pl.BlockSpec((size, wide), lambda c: (c, 0))
    like = jax.ShapeDtypeStruct
    scratch = lambda *shape: pltpu.VMEM(shape, jnp.float32)
    state = like((states, width), jnp.float32)
    return pl.pallas_call(
        scan_kernel,
        grid=(tokens // CHUNK,),
        in_specs=[
            pl.BlockSpec((proj.shape[0], CHUNK), lambda c: (0, c)),
            by_row(CHUNK, width),
            by_row(CHUNK, width),
            by_row(CHUNK, LANES),
            whole(rates),
            whole(w_dt),
            whole(bias),
            whole(skip),
        ],
        out_specs=[by_row(CHUNK, width)] * 4 + [by_row(CHUNK * states, width), whole(state)],
        out_shape=[
            like((tokens, width), jnp.bfloat16),
            like((tokens, width), jnp.float32),
            like((tokens, width), jnp.float32),
            like((tokens, width), jnp.float32),
            like((tokens * states, width), jnp.float32),
            state,
        ],
        scratch_shapes=[scratch(states, width)]
        + [scratch(CHUNK, width)] * 3
        + [scratch(2 * states, CHUNK)],
        compiler_params=pltpu.CompilerParams(
            dimension_semantics=("arbitrary",), vmem_limit_bytes=VMEM_LIMIT
        ),
        cost_estimate=cost(2400, tokens, states, width),
        name="scan",
    )(proj, act, gate, keep, rates, w_dt, bias, skip)


def adjoint(proj, act, steps, slope, upstream, keep, rates, w_dt, skip, history, last):
    tokens, width = act.shape
    states = rates.shape[0]
    count = tokens // CHUNK
    by_row = lambda size, wide: pl.BlockSpec((size, wide), lambda c: (count - 1 - c, 0))
    cols = pl.BlockSpec((proj.shape[0], CHUNK), lambda c: (0, count - 1 - c))
    like = jax.ShapeDtypeStruct
    scratch = lambda *shape: pltpu.VMEM(shape, jnp.float32)
    line = like((1, width), jnp.float32)
    return pl.pallas_call(
        adjoint_kernel,
        grid=(count,),
        in_specs=[cols]
        + [by_row(CHUNK, width)] * 4
        + [by_row(CHUNK, LANES), whole(rates), whole(w_dt), whole(skip)]
        + [by_row(CHUNK * states, width), whole(last)],
        out_specs=[by_row(CHUNK, width)] * 2 + [cols, whole(last), whole(line), whole(line)],
        out_shape=[
            like((tokens, width), jnp.bfloat16),
            like((tokens, width), jnp.float32),
            like(proj.shape, jnp.float32),
            like(last.shape, jnp.float32),
            line,
            line,
        ],
        scratch_shapes=[scratch(states, width)] * 2
        + [pltpu.VMEM((CHUNK * states, LANES), jnp.bfloat16)] * 2
        + [scratch(CHUNK, width)] * 4
        + [scratch(2 * states, CHUNK)],
        compiler_params=pltpu.CompilerParams(
            dimension_semantics=("arbitrary",), vmem_limit_bytes=VMEM_LIMIT
        ),
        cost_estimate=cost(4800, tokens, states, width),
        name="adjoint",
    )(proj, act, steps, slope, upstream, keep, rates, w_dt, skip, history, last)


EPS = 1e-05
BF16 = jnp.bfloat16
F32 = jnp.float32


def swap(array, axis, k):
    size = lax.axis_size(axis)
    return lax.ppermute(array, axis, [(i, i ^ k) for i in range(size)])


def after(value, *others):
    return lax.optimization_barrier((value, others))[0]


def pieces_over(array, axis, hold=None):
    pieces = [array] + [swap(array, axis, k) for k in range(1, lax.axis_size(axis))]
    return pieces if hold is None else [after(piece, hold) for piece in pieces]


def assemble(pieces, axis, dim):
    me, size = lax.axis_index(axis), pieces[0].shape[dim]
    shape = pieces[0].shape[:dim] + (size * len(pieces),) + pieces[0].shape[dim + 1 :]
    out = jnp.zeros(shape, pieces[0].dtype)
    for k, piece in enumerate(pieces):
        out = lax.dynamic_update_slice_in_dim(out, piece, (me ^ k) * size, dim)
    return row_major(out)


def gather(array, axis, dim, hold=None):
    return assemble(pieces_over(array, axis, hold), axis, dim)


def row_major(array):
    return with_layout_constraint(array, Layout(major_to_minor=tuple(range(array.ndim))))


def piece_of(array, axis, dim, index):
    size = array.shape[dim] // lax.axis_size(axis)
    return lax.dynamic_slice_in_dim(array, index * size, size, dim)


def shares(array, axis, dim, kind):
    me = lax.axis_index(axis)
    own = piece_of(array, axis, dim, me).astype(F32)
    sent = [
        piece_of(array, axis, dim, me ^ k).astype(kind) for k in range(1, lax.axis_size(axis))
    ]
    return own, sent


def collect(own, sent, axis):
    return total([own] + [swap(part, axis, k + 1).astype(F32) for k, part in enumerate(sent)])


def scatter_sum(array, axis, dim, kind):
    return collect(*shares(array, axis, dim, kind), axis)


def halving_sum(pieces, axis):
    k = 1
    while len(pieces) > 1:
        came = [swap(piece.astype(BF16), axis, k) for piece in pieces[1::2]]
        pieces = [own.astype(F32) + part.astype(F32) for own, part in zip(pieces[::2], came)]
        k *= 2
    return pieces[0]


def doubling_pieces(array, axis):
    k = lax.axis_size(axis) // 2
    pieces = {0: array}
    while k:
        pieces.update({j ^ k: swap(piece, axis, k) for j, piece in pieces.items()})
        k //= 2
    return [pieces[j] for j in range(len(pieces))]


def doubling_sum(array, axes):
    for axis in axes:
        k = 1
        while k < lax.axis_size(axis):
            array = array + swap(array, axis, k)
            k *= 2
    return array


def dot(left, right, left_dim=1, right_dim=0):
    return lax.dot_general(left, right, (((left_dim,), (right_dim,)), ((), ())), preferred_element_type=F32)


def silu_slope(v):
    s = jax.nn.sigmoid(v)
    return s * (1.0 + v * (1.0 - s))


def inverse_rms(x):
    return lax.rsqrt(jnp.mean(x * x, axis=-1, keepdims=True) + EPS)


def shards(
    block_input,
    doc_ids,
    norm_gain,
    in_proj,
    conv_weight,
    conv_bias,
    x_proj,
    dt_proj,
    dt_bias,
    a_log,
    d_skip,
    out_proj,
    grad_output,
):
    seqs, piece, width = block_input.shape
    length = doc_ids.shape[1]
    ctx, ctxs = lax.axis_index("context"), lax.axis_size("context")
    taps, tail = conv_weight.shape[0], conv_weight.shape[0] - 1
    states = a_log.shape[0]
    rows = seqs * length
    inner = in_proj.shape[2] // ctxs
    rank = dt_proj.shape[0] * lax.axis_size("fsdp")

    def mine(array, dim):
        return piece_of(array, "context", dim, ctx)

    in_half = mine(in_proj, 2)
    xcols, dtrows, share = x_proj.shape[1], dt_proj.shape[0], in_proj.shape[1]
    x_own = block_input.reshape(seqs * piece, width).astype(F32)
    normed_own = (x_own * inverse_rms(x_own) * norm_gain).astype(BF16)
    first = pieces_over(
        jnp.concatenate([mine(x_proj, 0).T, mine(dt_proj, 1), in_half[0]], axis=0),
        "fsdp",
        normed_own,
    )
    w_x = assemble([p[:xcols] for p in first], "fsdp", 0)
    w_dt = assemble([p[xcols : xcols + dtrows] for p in first], "fsdp", 0)
    w_conv = assemble([p[xcols + dtrows :] for p in first], "fsdp", 0)
    normed = [normed_own] + [swap(normed_own, "context", k) for k in range(1, ctxs)]
    def whole_tokens(parts):
        out = jnp.zeros((seqs, length, parts[0].shape[-1]), parts[0].dtype)
        for k, part in enumerate(parts):
            part = part.reshape(seqs, piece, part.shape[-1])
            out = lax.dynamic_update_slice_in_dim(out, part, (ctx ^ k) * piece, 1)
        return out.reshape(rows, -1)

    def token_parts(array):
        array = array.reshape(seqs, length, array.shape[-1])
        parts = [piece_of(array, "context", 1, ctx ^ k) for k in range(ctxs)]
        return [part.reshape(seqs * piece, -1) for part in parts]

    def over_tokens(left, right):
        return total([dot(l, r, 0, 0) for l, r in zip(left, right)])

    taps_w, bias, dt_b = mine(conv_weight, 1), mine(conv_bias, 0), mine(dt_bias, 0)
    rates = -jnp.exp(mine(a_log, 1))
    skip = mine(d_skip, 0)

    conv_input = whole_tokens([dot(part, w_conv).astype(BF16) for part in normed])
    padded_ids = jnp.concatenate([jnp.full((seqs, tail), -1, jnp.int32), doc_ids], axis=1)
    same = [
        (padded_ids[:, tail - k : tail - k + length] == doc_ids).astype(F32)[..., None]
        for k in range(taps)
    ]
    padded = jnp.pad(conv_input.reshape(seqs, length, inner), ((0, 0), (tail, 0), (0, 0))).astype(F32)
    shifted = [padded[:, tail - k : tail - k + length] for k in range(taps)]
    conv_output = bias
    for k in range(taps):
        conv_output = conv_output + taps_w[k] * shifted[k] * same[k]
    conv_flat = conv_output.reshape(rows, inner)
    activated = jax.nn.silu(conv_flat).astype(BF16)
    def all_sum(part, *beside):
        halved = scatter_sum(part, "context", 1, F32)
        halved = after(halved, *beside)
        summed = scatter_sum(halved, "tensor", 1, BF16).astype(BF16)
        return gather(gather(summed, "tensor", 1), "context", 1), halved, summed

    projections, _, summed = all_sum(dot(w_x, activated, 1, 1))
    w_gate = after(
        lax.all_gather(after(in_half[1], first), "fsdp", axis=0, tiled=True), summed
    )
    w_out = lax.all_gather(after(mine(out_proj, 0).T, conv_input), "fsdp", axis=0, tiled=True)
    own_cotangent = grad_output.reshape(seqs * piece, width)
    cotangent = [own_cotangent] + [
        swap(after(own_cotangent, conv_input), "context", k) for k in range(1, ctxs)
    ]
    keep = jnp.broadcast_to(same[1].reshape(rows, 1), (rows, LANES))
    projections, keep = after((projections, keep))
    dt_input = projections[:rank]
    gate = whole_tokens([dot(part, w_gate) for part in normed])
    gated, sloped, steps, slope, history, last = scan(
        projections, activated, gate, keep, rates * LOG2E, w_dt, dt_b[None], skip[None]
    )
    w_out = after(w_out, gated)

    def my_tokens(parts):
        return [parts[0]] + [swap(parts[k], "context", k) for k in range(1, ctxs)]

    def all_halves(weight):
        return [weight] + [swap(weight, "context", k) for k in range(1, ctxs)]

    zplace = lax.axis_index("tensor")
    x_flat = block_input.reshape(seqs * piece, width)
    gated_parts = token_parts(gated)
    branch = dot(
        jnp.concatenate(my_tokens(gated_parts), axis=1),
        jnp.concatenate(all_halves(w_out), axis=1),
        1,
        1,
    ).astype(BF16)
    later = [after(part, branch) for part in cotangent[1:]]
    d_gated = whole_tokens([dot(part, w_out) for part in cotangent[:1] + later])
    d_mixed = d_gated * jax.nn.silu(gate)
    d_gate = (d_gated * sloped).astype(BF16)
    branch = lax.psum_scatter(branch, "tensor", scatter_dimension=0, tiled=True).astype(F32)

    d_logits, d_act, d_part, d_rates, d_bias, d_skips = adjoint(
        projections, activated, steps, slope, d_mixed, keep, rates * LOG2E, w_dt, skip[None],
        history, last,
    )
    gate_halves, conv_halves = all_halves(w_gate), all_halves(w_conv)
    d_part, branch, gate_halves, conv_halves = after((d_part, branch, gate_halves, conv_halves))
    x_rows = piece_of(x_flat, "tensor", 0, zplace).astype(F32)
    output_rows = (x_rows + branch).astype(BF16)
    d_projections, halved, summed = all_sum(d_part, output_rows)
    block_output = lax.all_gather(output_rows[None], "tensor", axis=1, tiled=True)
    gate_parts = token_parts(d_gate)
    late_gate, late_gated = after((gate_parts, gated_parts), halved)
    grad_out_part = over_tokens(cotangent, late_gated)
    grad_gate_part = over_tokens(normed, late_gate)
    grad_dt_part = dot(dt_input, d_logits)
    d_act = d_act + dot(d_projections, w_x, 0, 0)
    grad_x_part = dot(d_projections, activated)
    d_conv = (d_act * silu_slope(conv_flat)).reshape(seqs, length, inner)
    d_conv_input = jnp.zeros((seqs, length, inner), F32)
    tap_grads = []
    for k in range(taps):
        masked = d_conv * same[k]
        late = jnp.pad(masked, ((0, 0), (0, tail), (0, 0)))[:, k : k + length]
        d_conv_input = d_conv_input + taps_w[k] * late
        tap_grads.append(jnp.sum(masked * shifted[k], axis=(0, 1)))
    d_conv_input = d_conv_input.reshape(rows, inner).astype(BF16)
    conv_parts = token_parts(d_conv_input)
    left = jnp.concatenate(my_tokens(gate_parts) + my_tokens(conv_parts), axis=1)
    right = jnp.concatenate(gate_halves + conv_halves, axis=1)
    partial = dot(left, right, 1, 1).astype(BF16)
    row_parts = [
        piece_of(partial, "tensor", 0, zplace ^ k) for k in range(lax.axis_size("tensor"))
    ]
    row_parts, block_output = after((row_parts, block_output))
    d_normed = halving_sum(row_parts, "tensor")
    grad_conv_part = over_tokens(normed, conv_parts)
    d_rows = piece_of(own_cotangent, "tensor", 0, zplace).astype(F32)
    inv = inverse_rms(x_rows)
    scaled = d_normed * norm_gain
    inner_sum = jnp.sum(scaled * x_rows, axis=-1, keepdims=True)
    grad_rows = d_rows + inv * scaled - x_rows * (inv * inv * inv) * inner_sum / width
    grad_rows = after(grad_rows.astype(BF16))
    row_pieces = doubling_pieces(grad_rows, "tensor")
    gain = jnp.sum(d_normed * x_rows * inv, axis=0)
    devices = lax.axis_size("fsdp")

    def owned(*parts):
        pieces = [part.reshape(devices, -1, inner).astype(BF16) for part in parts]
        fill = -sum(piece.shape[1] for piece in pieces) % LANES
        pieces.append(jnp.zeros((devices, fill, inner), BF16))
        pieces = row_major(jnp.concatenate(pieces, axis=1).reshape(-1, inner))
        return lax.psum_scatter(pieces, "fsdp", scatter_dimension=0, tiled=True)

    sums = jnp.concatenate(
        [
            owned(*after((grad_conv_part, grad_x_part, grad_dt_part), d_normed)),
            owned(grad_gate_part, grad_out_part),
        ]
    )
    thin = jnp.concatenate(
        [
            d_rates * rates,
            jnp.stack(tap_grads),
            jnp.sum(d_conv, axis=(0, 1))[None],
            d_bias,
            d_skips,
            gain.reshape(-1, inner),
        ],
        axis=0,
    )
    channels = states + taps + 3
    thin = doubling_sum(after(thin, row_pieces[1]), ("fsdp",))
    others = [thin] + [swap(thin, "context", k) for k in range(1, ctxs)]
    def side_by_side(parts, dim):
        size = parts[0].shape[dim]
        shape = parts[0].shape[:dim] + (size * ctxs,) + parts[0].shape[dim + 1 :]
        out = jnp.zeros(shape, parts[0].dtype)
        for k, part in enumerate(parts):
            out = lax.dynamic_update_slice_in_dim(out, part, (ctx ^ k) * size, dim)
        return out

    thin = side_by_side([part[:channels] for part in others], 1)
    sums = [sums] + [swap(sums, "context", k) for k in range(1, ctxs)]
    conv_at = sums[0].shape[0] - 2 * share
    grad_in = side_by_side(
        [
            jnp.stack([part[:share], part[conv_at : conv_at + share]]).astype(F32)
            for part in sums
        ],
        2,
    )
    grad_out = side_by_side([part[conv_at + share :].T.astype(F32) for part in sums], 0)
    thin_at = share + xcols
    grad_x = side_by_side([part[share:thin_at].T.astype(F32) for part in sums], 0)
    grad_dt = side_by_side([part[thin_at : thin_at + dtrows].astype(F32) for part in sums], 1)
    gain = total([part[channels:] for part in others]).reshape(1, width)
    grad_gain = doubling_sum(gain, ("tensor",))[0]
    count = grad_rows.shape[0]
    grad_input = jnp.zeros((count * lax.axis_size("tensor"), width), BF16)
    row_pieces[-1] = after(row_pieces[-1], grad_in, grad_out, grad_x, grad_dt)
    for k, part in enumerate(row_pieces):
        grad_input = lax.dynamic_update_slice_in_dim(grad_input, part, (zplace ^ k) * count, 0)
    grad_input = grad_input.reshape(block_input.shape)

    return (
        block_output.reshape(block_input.shape),
        grad_input,
        grad_gain,
        grad_in,
        thin[states : states + taps],
        thin[states + taps],
        grad_x,
        grad_dt,
        thin[states + taps + 1],
        thin[:states],
        thin[states + taps + 2],
        grad_out,
    )


def solution(mesh):
    placed = (
        P("fsdp", "context", None),
        P("fsdp", None),
        P(),
        P(None, "fsdp", "tensor"),
        P(None, "tensor"),
        P("tensor"),
        P("tensor", "fsdp"),
        P("fsdp", "tensor"),
        P("tensor"),
        P(None, "tensor"),
        P("tensor"),
        P("tensor", "fsdp"),
        P("fsdp", "context", None),
    )
    return jax.shard_map(
        shards,
        mesh=mesh,
        in_specs=placed,
        out_specs=(
            P("fsdp", "context", None),
            P("fsdp", "context", None),
            P(),
            P(None, "fsdp", "tensor"),
            P(None, "tensor"),
            P("tensor"),
            P("tensor", "fsdp"),
            P("fsdp", "tensor"),
            P("tensor"),
            P(None, "tensor"),
            P("tensor"),
            P("tensor", "fsdp"),
        ),
        check_vma=False,
    )
```

```python
import functools

import jax
import jax.numpy as jnp
from jax import lax
from jax.experimental import pallas as pl
from jax.experimental.layout import Layout, with_layout_constraint
from jax.experimental.pallas import tpu as pltpu
from jax.sharding import PartitionSpec as P

LANES = 128
SUB = 8
CHUNK = 128
PARTS = 2
VMEM_LIMIT = 56 << 20
GONE = 1e4
LOG2E = 1.4426950408889634


def span(group):
    return slice(group * LANES, (group + 1) * LANES)


def blocks(ref, halves, groups):
    return [[ref[SUB * i : SUB * i + SUB, span(g)] for g in range(groups)] for i in range(halves)]


def put_blocks(ref, values):
    for i, line in enumerate(values):
        for g, value in enumerate(line):
            ref[SUB * i : SUB * i + SUB, span(g)] = value


def column(ref, halves, t):
    return [
        jnp.broadcast_to(ref[SUB * i : SUB * i + SUB, t : t + 1], (SUB, LANES))
        for i in range(halves)
    ]


def row(tile, r):
    return jnp.broadcast_to(tile[r : r + 1, :], (SUB, LANES))


def sublane_bits():
    index = lax.broadcasted_iota(jnp.int32, (SUB, LANES), 0)
    return [(index & d) == 0 for d in (1, 2, 4)]


def fold(pending, value, bits, falling):
    level = 0
    while pending and pending[-1][0] == level:
        _, other = pending.pop()
        early, late = (value, other) if falling else (other, value)
        d = 1 << level
        if d < 4:
            value = jnp.where(
                bits[level], early + pltpu.roll(early, SUB - d, 0), late + pltpu.roll(late, d, 0)
            )
        else:
            value = jnp.where(bits[level], early, late) + pltpu.roll(
                jnp.where(bits[level], late, early), d, 0
            )
        level += 1
    pending.append((level, value))


def total(values):
    return functools.reduce(lambda a, b: a + b, values)


def soft_step(v):
    small = jnp.exp(-jnp.abs(v))
    slope = jnp.where(v >= 0, 1.0, small) / (1.0 + small)
    return jnp.maximum(v, 0.0) + jnp.log1p(small), slope


def step_rows(steps, act, keep_ref, fade_ref, fed_ref):
    for g in range(steps.shape[1] // LANES):
        fade_ref[:, span(g)] = jnp.where(keep_ref[...] > 0, steps[:, span(g)], GONE)
    fed_ref[...] = steps * act


def scan_kernel(
    proj_ref,
    act_ref,
    gate_ref,
    keep_ref,
    rate_ref,
    w_dt_ref,
    bias_ref,
    skip_ref,
    gated_ref,
    sloped_ref,
    steps_ref,
    slope_ref,
    h_ref,
    last_ref,
    state_ref,
    fade_ref,
    fed_ref,
    y_ref,
    coef_ref,
):
    chunk, width = act_ref.shape
    halves, groups = rate_ref.shape[0] // SUB, width // LANES
    states, rank = rate_ref.shape[0], w_dt_ref.shape[0]

    @pl.when(pl.program_id(0) == 0)
    def _():
        state_ref[...] = jnp.zeros_like(state_ref)

    logits = (
        lax.dot_general(
            proj_ref[:rank, :],
            w_dt_ref[...],
            (((0,), (0,)), ((), ())),
            preferred_element_type=jnp.float32,
        )
        + bias_ref[...]
    )
    steps, slope_ref[...] = soft_step(logits)
    steps_ref[...] = steps
    step_rows(steps, act_ref[...].astype(jnp.float32), keep_ref, fade_ref, fed_ref)
    coef_ref[...] = proj_ref[rank:, :].astype(jnp.float32)
    in_ref, out_ref = coef_ref.at[:states], coef_ref.at[states:]
    rate = blocks(rate_ref, halves, groups)
    state = blocks(state_ref, halves, groups)
    bits = sublane_bits()
    for base in range(0, chunk, SUB):
        fade = [fade_ref[base : base + SUB, span(g)] for g in range(groups)]
        fed = [fed_ref[base : base + SUB, span(g)] for g in range(groups)]
        pending = [[] for _ in range(groups)]
        for r in range(SUB):
            t = base + r
            in_col, out_col = column(in_ref, halves, t), column(out_ref, halves, t)
            for g in range(groups):
                fade_row, fed_row = row(fade[g], r), row(fed[g], r)
                parts = []
                for i in range(halves):
                    place = (t * halves + i) * SUB
                    h_ref[place : place + SUB, span(g)] = state[i][g]
                    factor = jnp.exp2(fade_row * rate[i][g])
                    state[i][g] = factor * state[i][g] + fed_row * in_col[i]
                    parts.append(state[i][g] * out_col[i])
                fold(pending[g], total(parts), bits, False)
        for g in range(groups):
            y_ref[base : base + SUB, span(g)] = pending[g][0][1]
    put_blocks(state_ref, state)
    last_ref[...] = state_ref[...]
    mixed = y_ref[...] + skip_ref[...] * act_ref[...].astype(jnp.float32)
    gate = gate_ref[...]
    sigmoid = jax.nn.sigmoid(gate)
    gated_ref[...] = (mixed * (gate * sigmoid)).astype(jnp.bfloat16)
    sloped_ref[...] = mixed * (sigmoid * (1.0 + gate * (1.0 - sigmoid)))


def lane_sums(products_ref, states):
    ones = jnp.ones((LANES, LANES), jnp.bfloat16)
    sums = jnp.dot(products_ref[...], ones, preferred_element_type=jnp.float32)
    lane = lax.broadcasted_iota(jnp.int32, (states, LANES), 1)
    result = jnp.zeros((states, LANES), jnp.float32)
    for t in range(CHUNK):
        result = jnp.where(lane == t, sums[t * states : (t + 1) * states], result)
    return result


def adjoint_kernel(
    proj_ref,
    act_ref,
    steps_ref,
    slope_ref,
    up_ref,
    keep_ref,
    rate_ref,
    w_dt_ref,
    skip_ref,
    h_ref,
    last_ref,
    d_logits_ref,
    d_act_ref,
    d_proj_ref,
    d_rate_ref,
    d_bias_ref,
    d_skip_ref,
    flow_ref,
    now_ref,
    in_part_ref,
    out_part_ref,
    fade_ref,
    fed_ref,
    weighted_ref,
    pulled_ref,
    coef_ref,
):
    chunk, width = act_ref.shape
    halves, groups = rate_ref.shape[0] // SUB, width // LANES
    states, rank = rate_ref.shape[0], w_dt_ref.shape[0]
    size = chunk // PARTS

    @pl.when(pl.program_id(0) == 0)
    def _():
        flow_ref[...] = jnp.zeros_like(flow_ref)
        d_rate_ref[...] = jnp.zeros_like(d_rate_ref)
        d_bias_ref[...] = jnp.zeros_like(d_bias_ref)
        d_skip_ref[...] = jnp.zeros_like(d_skip_ref)
        now_ref[...] = last_ref[...]

    step_rows(steps_ref[...], act_ref[...].astype(jnp.float32), keep_ref, fade_ref, fed_ref)
    for part in range(PARTS):
        coef = proj_ref[rank:, :].astype(jnp.float32)
        coef_ref[part] = pltpu.roll(coef, -part * size % chunk, 1) if part else coef
    rate = blocks(rate_ref, halves, groups)
    bits = sublane_bits()

    def tokens(step, carry):
        flow, d_rate, now = jax.tree.map(lambda v: v, carry)
        part = PARTS - 1 - step
        in_ref, out_ref = coef_ref.at[part, :states], coef_ref.at[part, states:]
        for base in range(size - SUB, -SUB, -SUB):
            here = pl.ds(pl.multiple_of(part * size + base, SUB), SUB)
            fade = [fade_ref[here, span(g)] for g in range(groups)]
            fed = [fed_ref[here, span(g)] for g in range(groups)]
            up = [up_ref[here, span(g)] for g in range(groups)]
            weighted = [[] for _ in range(groups)]
            slopes = [[] for _ in range(groups)]
            for r in range(SUB - 1, -1, -1):
                t = base + r
                in_col, out_col = column(in_ref, halves, t), column(out_ref, halves, t)
                in_parts = [[] for _ in range(halves)]
                out_parts = [[] for _ in range(halves)]
                first = (part * size + t) * states
                for g in range(groups):
                    fade_row, fed_row, up_row = row(fade[g], r), row(fed[g], r), row(up[g], r)
                    by_in, by_rate = [], []
                    for i in range(halves):
                        place = pl.ds(pl.multiple_of(first + i * SUB, SUB), SUB)
                        before = h_ref[place, span(g)]
                        factor = jnp.exp2(fade_row * rate[i][g])
                        adjoint = out_col[i] * up_row + flow[i][g]
                        out_parts[i].append(now[i][g] * up_row)
                        in_parts[i].append(adjoint * fed_row)
                        flow[i][g] = factor * adjoint
                        pulled = flow[i][g] * before
                        by_in.append(adjoint * in_col[i])
                        by_rate.append(pulled * rate[i][g])
                        d_rate[i][g] = d_rate[i][g] + pulled * fade_row
                        now[i][g] = before
                    fold(weighted[g], total(by_in), bits, True)
                    fold(slopes[g], total(by_rate), bits, True)
                place = pl.ds(pl.multiple_of(first, states), states)
                for ref, parts in ((in_part_ref, in_parts), (out_part_ref, out_parts)):
                    ref[place, :] = jnp.concatenate([total(p) for p in parts]).astype(jnp.bfloat16)
            for g in range(groups):
                weighted_ref[here, span(g)] = weighted[g][0][1]
                pulled_ref[here, span(g)] = slopes[g][0][1]
        return flow, d_rate, now

    flow, d_rate, now = lax.fori_loop(
        0,
        PARTS,
        tokens,
        tuple(blocks(ref, halves, groups) for ref in (flow_ref, d_rate_ref, now_ref)),
    )
    put_blocks(flow_ref, flow)
    put_blocks(d_rate_ref, d_rate)
    put_blocks(now_ref, now)
    d_proj_ref[rank : rank + states, :] = lane_sums(in_part_ref, states)
    d_proj_ref[rank + states :, :] = lane_sums(out_part_ref, states)
    act = act_ref[...].astype(jnp.float32)
    d_step = pulled_ref[...] * (1.0 / LOG2E) + act * weighted_ref[...]
    d_logits = (d_step * slope_ref[...]).astype(jnp.bfloat16)
    d_logits_ref[...] = d_logits
    d_bias_ref[...] += jnp.sum(d_logits.astype(jnp.float32), axis=0, keepdims=True)
    d_skip_ref[...] += jnp.sum(up_ref[...] * act, axis=0, keepdims=True)
    d_act_ref[...] = up_ref[...] * skip_ref[...] + steps_ref[...] * weighted_ref[...]
    d_proj_ref[:rank, :] = lax.dot_general(
        w_dt_ref[...],
        d_logits,
        (((1,), (1,)), ((), ())),
        preferred_element_type=jnp.float32,
    )


def cost(scale, tokens, states, width):
    work = tokens * states * width
    return pl.CostEstimate(flops=scale * work, bytes_accessed=8 * work, transcendentals=work)


def whole(array):
    return pl.BlockSpec(array.shape, lambda c: (0,) * len(array.shape))


def scan(proj, act, gate, keep, rates, w_dt, bias, skip):
    tokens, width = act.shape
    states = rates.shape[0]
    by_row = lambda size, wide: pl.BlockSpec((size, wide), lambda c: (c, 0))
    like = jax.ShapeDtypeStruct
    scratch = lambda *shape: pltpu.VMEM(shape, jnp.float32)
    state = like((states, width), jnp.float32)
    return pl.pallas_call(
        scan_kernel,
        grid=(tokens // CHUNK,),
        in_specs=[
            pl.BlockSpec((proj.shape[0], CHUNK), lambda c: (0, c)),
            by_row(CHUNK, width),
            by_row(CHUNK, width),
            by_row(CHUNK, LANES),
            whole(rates),
            whole(w_dt),
            whole(bias),
            whole(skip),
        ],
        out_specs=[by_row(CHUNK, width)] * 4 + [by_row(CHUNK * states, width), whole(state)],
        out_shape=[
            like((tokens, width), jnp.bfloat16),
            like((tokens, width), jnp.float32),
            like((tokens, width), jnp.float32),
            like((tokens, width), jnp.float32),
            like((tokens * states, width), jnp.float32),
            state,
        ],
        scratch_shapes=[scratch(states, width)]
        + [scratch(CHUNK, width)] * 3
        + [scratch(2 * states, CHUNK)],
        compiler_params=pltpu.CompilerParams(
            dimension_semantics=("arbitrary",), vmem_limit_bytes=VMEM_LIMIT
        ),
        cost_estimate=cost(2400, tokens, states, width),
        name="scan",
    )(proj, act, gate, keep, rates, w_dt, bias, skip)


def adjoint(proj, act, steps, slope, upstream, keep, rates, w_dt, skip, history, last):
    tokens, width = act.shape
    states = rates.shape[0]
    count = tokens // CHUNK
    by_row = lambda size, wide: pl.BlockSpec((size, wide), lambda c: (count - 1 - c, 0))
    cols = pl.BlockSpec((proj.shape[0], CHUNK), lambda c: (0, count - 1 - c))
    like = jax.ShapeDtypeStruct
    scratch = lambda *shape: pltpu.VMEM(shape, jnp.float32)
    line = like((1, width), jnp.float32)
    return pl.pallas_call(
        adjoint_kernel,
        grid=(count,),
        in_specs=[cols]
        + [by_row(CHUNK, width)] * 4
        + [by_row(CHUNK, LANES), whole(rates), whole(w_dt), whole(skip)]
        + [by_row(CHUNK * states, width), whole(last)],
        out_specs=[by_row(CHUNK, width)] * 2 + [cols, whole(last), whole(line), whole(line)],
        out_shape=[
            like((tokens, width), jnp.bfloat16),
            like((tokens, width), jnp.float32),
            like(proj.shape, jnp.float32),
            like(last.shape, jnp.float32),
            line,
            line,
        ],
        scratch_shapes=[scratch(states, width)] * 2
        + [pltpu.VMEM((CHUNK * states, LANES), jnp.bfloat16)] * 2
        + [scratch(CHUNK, width)] * 4
        + [scratch(PARTS, 2 * states, CHUNK)],
        compiler_params=pltpu.CompilerParams(
            dimension_semantics=("arbitrary",), vmem_limit_bytes=VMEM_LIMIT
        ),
        cost_estimate=cost(4800, tokens, states, width),
        name="adjoint",
    )(proj, act, steps, slope, upstream, keep, rates, w_dt, skip, history, last)


EPS = 1e-05
BF16 = jnp.bfloat16
F32 = jnp.float32


def swap(array, axis, k):
    size = lax.axis_size(axis)
    return lax.ppermute(array, axis, [(i, i ^ k) for i in range(size)])


def after(value, *others):
    return lax.optimization_barrier((value, others))[0]


def pieces_over(array, axis, hold=None):
    pieces = [array] + [swap(array, axis, k) for k in range(1, lax.axis_size(axis))]
    return pieces if hold is None else [after(piece, hold) for piece in pieces]


def assemble(pieces, axis, dim):
    me, size = lax.axis_index(axis), pieces[0].shape[dim]
    shape = pieces[0].shape[:dim] + (size * len(pieces),) + pieces[0].shape[dim + 1 :]
    out = jnp.zeros(shape, pieces[0].dtype)
    for k, piece in enumerate(pieces):
        out = lax.dynamic_update_slice_in_dim(out, piece, (me ^ k) * size, dim)
    return row_major(out)


def gather(array, axis, dim, hold=None):
    return assemble(pieces_over(array, axis, hold), axis, dim)


def row_major(array):
    return with_layout_constraint(array, Layout(major_to_minor=tuple(range(array.ndim))))


def piece_of(array, axis, dim, index):
    size = array.shape[dim] // lax.axis_size(axis)
    return lax.dynamic_slice_in_dim(array, index * size, size, dim)


def shares(array, axis, dim, kind):
    me = lax.axis_index(axis)
    own = piece_of(array, axis, dim, me).astype(F32)
    sent = [
        piece_of(array, axis, dim, me ^ k).astype(kind) for k in range(1, lax.axis_size(axis))
    ]
    return own, sent


def collect(own, sent, axis):
    return total([own] + [swap(part, axis, k + 1).astype(F32) for k, part in enumerate(sent)])


def scatter_sum(array, axis, dim, kind):
    return collect(*shares(array, axis, dim, kind), axis)


def halving_sum(pieces, axis):
    k = 1
    while len(pieces) > 1:
        came = [swap(piece.astype(BF16), axis, k) for piece in pieces[1::2]]
        pieces = [own.astype(F32) + part.astype(F32) for own, part in zip(pieces[::2], came)]
        k *= 2
    return pieces[0]


def doubling_pieces(array, axis):
    k = lax.axis_size(axis) // 2
    pieces = {0: array}
    while k:
        pieces.update({j ^ k: swap(piece, axis, k) for j, piece in pieces.items()})
        k //= 2
    return [pieces[j] for j in range(len(pieces))]


def doubling_sum(array, axes):
    for axis in axes:
        k = 1
        while k < lax.axis_size(axis):
            array = array + swap(array, axis, k)
            k *= 2
    return array


def dot(left, right, left_dim=1, right_dim=0):
    return lax.dot_general(left, right, (((left_dim,), (right_dim,)), ((), ())), preferred_element_type=F32)


def silu_slope(v):
    s = jax.nn.sigmoid(v)
    return s * (1.0 + v * (1.0 - s))


def inverse_rms(x):
    return lax.rsqrt(jnp.mean(x * x, axis=-1, keepdims=True) + EPS)


def shards(
    block_input,
    doc_ids,
    norm_gain,
    in_proj,
    conv_weight,
    conv_bias,
    x_proj,
    dt_proj,
    dt_bias,
    a_log,
    d_skip,
    out_proj,
    grad_output,
):
    seqs, piece, width = block_input.shape
    length = doc_ids.shape[1]
    ctx, ctxs = lax.axis_index("context"), lax.axis_size("context")
    taps, tail = conv_weight.shape[0], conv_weight.shape[0] - 1
    states = a_log.shape[0]
    rows = seqs * length
    inner = in_proj.shape[2] // ctxs
    rank = dt_proj.shape[0] * lax.axis_size("fsdp")

    def mine(array, dim):
        return piece_of(array, "context", dim, ctx)

    in_half = mine(in_proj, 2)
    xcols, dtrows, share = x_proj.shape[1], dt_proj.shape[0], in_proj.shape[1]
    x_own = block_input.reshape(seqs * piece, width).astype(F32)
    normed_own = (x_own * inverse_rms(x_own) * norm_gain).astype(BF16)
    first = pieces_over(
        jnp.concatenate([mine(x_proj, 0).T, mine(dt_proj, 1), in_half[0]], axis=0),
        "fsdp",
        normed_own,
    )
    w_x = assemble([p[:xcols] for p in first], "fsdp", 0)
    w_dt = assemble([p[xcols : xcols + dtrows] for p in first], "fsdp", 0)
    w_conv = assemble([p[xcols + dtrows :] for p in first], "fsdp", 0)
    normed = [normed_own] + [swap(normed_own, "context", k) for k in range(1, ctxs)]
    def whole_tokens(parts):
        out = jnp.zeros((seqs, length, parts[0].shape[-1]), parts[0].dtype)
        for k, part in enumerate(parts):
            part = part.reshape(seqs, piece, part.shape[-1])
            out = lax.dynamic_update_slice_in_dim(out, part, (ctx ^ k) * piece, 1)
        return out.reshape(rows, -1)

    def token_parts(array):
        array = array.reshape(seqs, length, array.shape[-1])
        parts = [piece_of(array, "context", 1, ctx ^ k) for k in range(ctxs)]
        return [part.reshape(seqs * piece, -1) for part in parts]

    def over_tokens(left, right):
        return total([dot(l, r, 0, 0) for l, r in zip(left, right)])

    taps_w, bias, dt_b = mine(conv_weight, 1), mine(conv_bias, 0), mine(dt_bias, 0)
    rates = -jnp.exp(mine(a_log, 1))
    skip = mine(d_skip, 0)

    conv_input = whole_tokens([dot(part, w_conv).astype(BF16) for part in normed])
    padded_ids = jnp.concatenate([jnp.full((seqs, tail), -1, jnp.int32), doc_ids], axis=1)
    same = [
        (padded_ids[:, tail - k : tail - k + length] == doc_ids).astype(F32)[..., None]
        for k in range(taps)
    ]
    padded = jnp.pad(conv_input.reshape(seqs, length, inner), ((0, 0), (tail, 0), (0, 0))).astype(F32)
    shifted = [padded[:, tail - k : tail - k + length] for k in range(taps)]
    conv_output = bias
    for k in range(taps):
        conv_output = conv_output + taps_w[k] * shifted[k] * same[k]
    conv_flat = conv_output.reshape(rows, inner)
    activated = jax.nn.silu(conv_flat).astype(BF16)
    def all_sum(part, *beside):
        halved = scatter_sum(part, "context", 1, F32)
        halved = after(halved, *beside)
        summed = scatter_sum(halved, "tensor", 1, BF16).astype(BF16)
        return gather(gather(summed, "tensor", 1), "context", 1), halved, summed

    keep = jnp.broadcast_to(same[1].reshape(rows, 1), (rows, LANES))
    projections, _, summed = all_sum(dot(w_x, activated, 1, 1), keep)
    w_gate = after(
        lax.all_gather(after(in_half[1], first), "fsdp", axis=0, tiled=True), summed
    )
    w_out = lax.all_gather(after(mine(out_proj, 0).T, conv_input), "fsdp", axis=0, tiled=True)
    own_cotangent = grad_output.reshape(seqs * piece, width)
    cotangent = [own_cotangent] + [
        swap(after(own_cotangent, conv_input), "context", k) for k in range(1, ctxs)
    ]
    dt_input = projections[:rank]
    gate = whole_tokens([dot(part, w_gate) for part in normed])
    gated, sloped, steps, slope, history, last = scan(
        projections, activated, gate, keep, rates * LOG2E, w_dt, dt_b[None], skip[None]
    )
    w_out = after(w_out, gated)

    def my_tokens(parts):
        return [parts[0]] + [swap(parts[k], "context", k) for k in range(1, ctxs)]

    def all_halves(weight):
        return [weight] + [swap(weight, "context", k) for k in range(1, ctxs)]

    zplace = lax.axis_index("tensor")
    x_flat = block_input.reshape(seqs * piece, width)
    gated_parts = token_parts(gated)
    branch = dot(
        jnp.concatenate(my_tokens(gated_parts), axis=1),
        jnp.concatenate(all_halves(w_out), axis=1),
        1,
        1,
    ).astype(BF16)
    later = [after(part, branch) for part in cotangent[1:]]
    d_gated = whole_tokens([dot(part, w_out) for part in cotangent[:1] + later])
    d_mixed = d_gated * jax.nn.silu(gate)
    d_gate = (d_gated * sloped).astype(BF16)
    branch = lax.psum_scatter(branch, "tensor", scatter_dimension=0, tiled=True).astype(F32)

    d_logits, d_act, d_part, d_rates, d_bias, d_skips = adjoint(
        projections, activated, steps, slope, d_mixed, keep, rates * LOG2E, w_dt, skip[None],
        history, last,
    )
    gate_halves, conv_halves = all_halves(w_gate), all_halves(w_conv)
    d_part, branch, gate_halves, conv_halves = after((d_part, branch, gate_halves, conv_halves))
    x_rows = piece_of(x_flat, "tensor", 0, zplace).astype(F32)
    output_rows = (x_rows + branch).astype(BF16)
    d_projections, halved, summed = all_sum(d_part, output_rows)
    block_output = lax.all_gather(output_rows[None], "tensor", axis=1, tiled=True)
    gate_parts = token_parts(d_gate)
    late_gate, late_gated = after((gate_parts, gated_parts), halved)
    grad_out_part = over_tokens(cotangent, late_gated)
    grad_gate_part = over_tokens(normed, late_gate)
    grad_dt_part = dot(dt_input, d_logits)
    d_act = d_act + dot(d_projections, w_x, 0, 0)
    grad_x_part = dot(d_projections, activated)
    d_conv = (d_act * silu_slope(conv_flat)).reshape(seqs, length, inner)
    d_conv_input = jnp.zeros((seqs, length, inner), F32)
    tap_grads = []
    for k in range(taps):
        masked = d_conv * same[k]
        late = jnp.pad(masked, ((0, 0), (0, tail), (0, 0)))[:, k : k + length]
        d_conv_input = d_conv_input + taps_w[k] * late
        tap_grads.append(jnp.sum(masked * shifted[k], axis=(0, 1)))
    d_conv_input = d_conv_input.reshape(rows, inner).astype(BF16)
    conv_parts = token_parts(d_conv_input)
    left = jnp.concatenate(my_tokens(gate_parts) + my_tokens(conv_parts), axis=1)
    right = jnp.concatenate(gate_halves + conv_halves, axis=1)
    partial = dot(left, right, 1, 1).astype(BF16)
    row_parts = [
        piece_of(partial, "tensor", 0, zplace ^ k) for k in range(lax.axis_size("tensor"))
    ]
    row_parts, block_output = after((row_parts, block_output))
    d_normed = halving_sum(row_parts, "tensor")
    grad_conv_part = over_tokens(normed, conv_parts)
    d_rows = piece_of(own_cotangent, "tensor", 0, zplace).astype(F32)
    inv = inverse_rms(x_rows)
    scaled = d_normed * norm_gain
    inner_sum = jnp.sum(scaled * x_rows, axis=-1, keepdims=True)
    grad_rows = d_rows + inv * scaled - x_rows * (inv * inv * inv) * inner_sum / width
    grad_rows = after(grad_rows.astype(BF16))
    row_pieces = doubling_pieces(grad_rows, "tensor")
    gain = jnp.sum(d_normed * x_rows * inv, axis=0)
    devices = lax.axis_size("fsdp")

    def owned(parts, hold=()):
        pieces = [part.reshape(devices, -1, inner).astype(BF16) for part in parts]
        fill = -sum(piece.shape[1] for piece in pieces) % LANES
        pieces.append(jnp.zeros((devices, fill, inner), BF16))
        pieces = row_major(jnp.concatenate(pieces, axis=1).reshape(-1, inner))
        return lax.psum_scatter(after(pieces, hold), "fsdp", scatter_dimension=0, tiled=True)

    sums = jnp.concatenate(
        [
            owned((grad_conv_part, grad_x_part, grad_dt_part), d_normed),
            owned((grad_gate_part, grad_out_part)),
        ]
    )
    thin = jnp.concatenate(
        [
            d_rates * rates,
            jnp.stack(tap_grads),
            jnp.sum(d_conv, axis=(0, 1))[None],
            d_bias,
            d_skips,
            gain.reshape(-1, inner),
        ],
        axis=0,
    )
    channels = states + taps + 3
    thin = doubling_sum(after(thin, row_pieces[1]), ("fsdp",))
    others = [thin] + [swap(thin, "context", k) for k in range(1, ctxs)]
    def side_by_side(parts, dim):
        size = parts[0].shape[dim]
        shape = parts[0].shape[:dim] + (size * ctxs,) + parts[0].shape[dim + 1 :]
        out = jnp.zeros(shape, parts[0].dtype)
        for k, part in enumerate(parts):
            out = lax.dynamic_update_slice_in_dim(out, part, (ctx ^ k) * size, dim)
        return out

    thin = side_by_side([part[:channels] for part in others], 1)
    sums = [sums] + [swap(sums, "context", k) for k in range(1, ctxs)]
    conv_at = sums[0].shape[0] - 2 * share
    grad_in = side_by_side(
        [
            jnp.stack([part[:share], part[conv_at : conv_at + share]]).astype(F32)
            for part in sums
        ],
        2,
    )
    grad_out = side_by_side([part[conv_at + share :].T.astype(F32) for part in sums], 0)
    thin_at = share + xcols
    grad_x = side_by_side([part[share:thin_at].T.astype(F32) for part in sums], 0)
    grad_dt = side_by_side([part[thin_at : thin_at + dtrows].astype(F32) for part in sums], 1)
    gain = total([part[channels:] for part in others]).reshape(1, width)
    grad_gain = doubling_sum(gain, ("tensor",))[0]
    count = grad_rows.shape[0]
    grad_input = jnp.zeros((count * lax.axis_size("tensor"), width), BF16)
    row_pieces[-1] = after(row_pieces[-1], grad_in, grad_out, grad_x, grad_dt)
    for k, part in enumerate(row_pieces):
        grad_input = lax.dynamic_update_slice_in_dim(grad_input, part, (zplace ^ k) * count, 0)
    grad_input = grad_input.reshape(block_input.shape)

    return (
        block_output.reshape(block_input.shape),
        grad_input,
        grad_gain,
        grad_in,
        thin[states : states + taps],
        thin[states + taps],
        grad_x,
        grad_dt,
        thin[states + taps + 1],
        thin[:states],
        thin[states + taps + 2],
        grad_out,
    )


def solution(mesh):
    placed = (
        P("fsdp", "context", None),
        P("fsdp", None),
        P(),
        P(None, "fsdp", "tensor"),
        P(None, "tensor"),
        P("tensor"),
        P("tensor", "fsdp"),
        P("fsdp", "tensor"),
        P("tensor"),
        P(None, "tensor"),
        P("tensor"),
        P("tensor", "fsdp"),
        P("fsdp", "context", None),
    )
    return jax.shard_map(
        shards,
        mesh=mesh,
        in_specs=placed,
        out_specs=(
            P("fsdp", "context", None),
            P("fsdp", "context", None),
            P(),
            P(None, "fsdp", "tensor"),
            P(None, "tensor"),
            P("tensor"),
            P("tensor", "fsdp"),
            P("fsdp", "tensor"),
            P("tensor"),
            P(None, "tensor"),
            P("tensor"),
            P("tensor", "fsdp"),
        ),
        check_vma=False,
    )
```

```python
import functools

import jax
import jax.numpy as jnp
from jax import lax
from jax.experimental import pallas as pl
from jax.experimental.layout import Layout, with_layout_constraint
from jax.experimental.pallas import tpu as pltpu
from jax.sharding import PartitionSpec as P

LANES = 128
SUB = 8
CHUNK = 128
PARTS = 2
VMEM_LIMIT = 56 << 20
GONE = 1e4
LOG2E = 1.4426950408889634


def span(group):
    return slice(group * LANES, (group + 1) * LANES)


def blocks(ref, halves, groups):
    return [[ref[SUB * i : SUB * i + SUB, span(g)] for g in range(groups)] for i in range(halves)]


def put_blocks(ref, values):
    for i, line in enumerate(values):
        for g, value in enumerate(line):
            ref[SUB * i : SUB * i + SUB, span(g)] = value


def column(ref, halves, t):
    return [
        jnp.broadcast_to(ref[SUB * i : SUB * i + SUB, t : t + 1], (SUB, LANES))
        for i in range(halves)
    ]


def row(tile, r):
    return jnp.broadcast_to(tile[r : r + 1, :], (SUB, LANES))


def sublane_bits():
    index = lax.broadcasted_iota(jnp.int32, (SUB, LANES), 0)
    return [(index & d) == 0 for d in (1, 2, 4)]


def fold(pending, value, bits, falling):
    level = 0
    while pending and pending[-1][0] == level:
        _, other = pending.pop()
        early, late = (value, other) if falling else (other, value)
        d = 1 << level
        if d < 4:
            value = jnp.where(
                bits[level], early + pltpu.roll(early, SUB - d, 0), late + pltpu.roll(late, d, 0)
            )
        else:
            value = jnp.where(bits[level], early, late) + pltpu.roll(
                jnp.where(bits[level], late, early), d, 0
            )
        level += 1
    pending.append((level, value))


def total(values):
    return functools.reduce(lambda a, b: a + b, values)


def soft_step(v):
    small = jnp.exp(-jnp.abs(v))
    slope = jnp.where(v >= 0, 1.0, small) / (1.0 + small)
    return jnp.maximum(v, 0.0) + jnp.log1p(small), slope


def step_rows(steps, act, keep_ref, fade_ref, fed_ref):
    for g in range(steps.shape[1] // LANES):
        fade_ref[:, span(g)] = jnp.where(keep_ref[...] > 0, steps[:, span(g)], GONE)
    fed_ref[...] = steps * act


def scan_kernel(
    proj_ref,
    act_ref,
    gate_ref,
    keep_ref,
    rate_ref,
    w_dt_ref,
    bias_ref,
    skip_ref,
    gated_ref,
    sloped_ref,
    steps_ref,
    slope_ref,
    h_ref,
    last_ref,
    state_ref,
    fade_ref,
    fed_ref,
    y_ref,
    coef_ref,
):
    chunk, width = act_ref.shape
    halves, groups = rate_ref.shape[0] // SUB, width // LANES
    states, rank = rate_ref.shape[0], w_dt_ref.shape[0]

    @pl.when(pl.program_id(0) == 0)
    def _():
        state_ref[...] = jnp.zeros_like(state_ref)

    logits = (
        lax.dot_general(
            proj_ref[:rank, :],
            w_dt_ref[...],
            (((0,), (0,)), ((), ())),
            preferred_element_type=jnp.float32,
        )
        + bias_ref[...]
    )
    steps, slope_ref[...] = soft_step(logits)
    steps_ref[...] = steps
    step_rows(steps, act_ref[...].astype(jnp.float32), keep_ref, fade_ref, fed_ref)
    coef_ref[...] = proj_ref[rank:, :].astype(jnp.float32)
    in_ref, out_ref = coef_ref.at[:states], coef_ref.at[states:]
    rate = blocks(rate_ref, halves, groups)
    state = blocks(state_ref, halves, groups)
    bits = sublane_bits()
    for base in range(0, chunk, SUB):
        fade = [fade_ref[base : base + SUB, span(g)] for g in range(groups)]
        fed = [fed_ref[base : base + SUB, span(g)] for g in range(groups)]
        pending = [[] for _ in range(groups)]
        for r in range(SUB):
            t = base + r
            in_col, out_col = column(in_ref, halves, t), column(out_ref, halves, t)
            for g in range(groups):
                fade_row, fed_row = row(fade[g], r), row(fed[g], r)
                parts = []
                for i in range(halves):
                    place = (t * halves + i) * SUB
                    h_ref[place : place + SUB, span(g)] = state[i][g]
                    factor = jnp.exp2(fade_row * rate[i][g])
                    state[i][g] = factor * state[i][g] + fed_row * in_col[i]
                    parts.append(state[i][g] * out_col[i])
                fold(pending[g], total(parts), bits, False)
        for g in range(groups):
            y_ref[base : base + SUB, span(g)] = pending[g][0][1]
    put_blocks(state_ref, state)
    last_ref[...] = state_ref[...]
    mixed = y_ref[...] + skip_ref[...] * act_ref[...].astype(jnp.float32)
    gate = gate_ref[...]
    sigmoid = jax.nn.sigmoid(gate)
    gated_ref[...] = (mixed * (gate * sigmoid)).astype(jnp.bfloat16)
    sloped_ref[...] = mixed * (sigmoid * (1.0 + gate * (1.0 - sigmoid)))


def lane_sums(products_ref, states):
    ones = jnp.ones((LANES, LANES), jnp.bfloat16)
    sums = jnp.dot(products_ref[...], ones, preferred_element_type=jnp.float32)
    lane = lax.broadcasted_iota(jnp.int32, (states, LANES), 1)
    result = jnp.zeros((states, LANES), jnp.float32)
    for t in range(CHUNK):
        result = jnp.where(lane == t, sums[t * states : (t + 1) * states], result)
    return result


def adjoint_kernel(
    proj_ref,
    act_ref,
    steps_ref,
    slope_ref,
    up_ref,
    keep_ref,
    rate_ref,
    w_dt_ref,
    skip_ref,
    h_ref,
    last_ref,
    d_logits_ref,
    d_act_ref,
    d_proj_ref,
    d_rate_ref,
    d_bias_ref,
    d_skip_ref,
    flow_ref,
    now_ref,
    in_part_ref,
    out_part_ref,
    fade_ref,
    fed_ref,
    weighted_ref,
    pulled_ref,
    coef_ref,
):
    chunk, width = act_ref.shape
    halves, groups = rate_ref.shape[0] // SUB, width // LANES
    states, rank = rate_ref.shape[0], w_dt_ref.shape[0]
    size = chunk // PARTS

    @pl.when(pl.program_id(0) == 0)
    def _():
        flow_ref[...] = jnp.zeros_like(flow_ref)
        d_rate_ref[...] = jnp.zeros_like(d_rate_ref)
        d_bias_ref[...] = jnp.zeros_like(d_bias_ref)
        d_skip_ref[...] = jnp.zeros_like(d_skip_ref)
        now_ref[...] = last_ref[...]

    step_rows(steps_ref[...], act_ref[...].astype(jnp.float32), keep_ref, fade_ref, fed_ref)
    for part in range(PARTS):
        coef = proj_ref[rank:, :].astype(jnp.float32)
        coef_ref[part] = pltpu.roll(coef, -part * size % chunk, 1) if part else coef
    rate = blocks(rate_ref, halves, groups)
    bits = sublane_bits()

    def tokens(step, carry):
        flow, d_rate, now = jax.tree.map(lambda v: v, carry)
        part = PARTS - 1 - step
        in_ref, out_ref = coef_ref.at[part, :states], coef_ref.at[part, states:]
        for base in range(size - SUB, -SUB, -SUB):
            here = pl.ds(pl.multiple_of(part * size + base, SUB), SUB)
            fade = [fade_ref[here, span(g)] for g in range(groups)]
            fed = [fed_ref[here, span(g)] for g in range(groups)]
            up = [up_ref[here, span(g)] for g in range(groups)]
            weighted = [[] for _ in range(groups)]
            slopes = [[] for _ in range(groups)]
            for r in range(SUB - 1, -1, -1):
                t = base + r
                in_col, out_col = column(in_ref, halves, t), column(out_ref, halves, t)
                in_parts = [[] for _ in range(halves)]
                out_parts = [[] for _ in range(halves)]
                first = (part * size + t) * states
                for g in range(groups):
                    fade_row, fed_row, up_row = row(fade[g], r), row(fed[g], r), row(up[g], r)
                    by_in, by_rate = [], []
                    for i in range(halves):
                        place = pl.ds(pl.multiple_of(first + i * SUB, SUB), SUB)
                        before = h_ref[place, span(g)]
                        factor = jnp.exp2(fade_row * rate[i][g])
                        adjoint = out_col[i] * up_row + flow[i][g]
                        out_parts[i].append(now[i][g] * up_row)
                        in_parts[i].append(adjoint * fed_row)
                        flow[i][g] = factor * adjoint
                        pulled = flow[i][g] * before
                        by_in.append(adjoint * in_col[i])
                        by_rate.append(pulled * rate[i][g])
                        d_rate[i][g] = d_rate[i][g] + pulled * fade_row
                        now[i][g] = before
                    fold(weighted[g], total(by_in), bits, True)
                    fold(slopes[g], total(by_rate), bits, True)
                place = pl.ds(pl.multiple_of(first, states), states)
                for ref, parts in ((in_part_ref, in_parts), (out_part_ref, out_parts)):
                    ref[place, :] = jnp.concatenate([total(p) for p in parts]).astype(jnp.bfloat16)
            for g in range(groups):
                weighted_ref[here, span(g)] = weighted[g][0][1]
                pulled_ref[here, span(g)] = slopes[g][0][1]
        return flow, d_rate, now

    flow, d_rate, now = lax.fori_loop(
        0,
        PARTS,
        tokens,
        tuple(blocks(ref, halves, groups) for ref in (flow_ref, d_rate_ref, now_ref)),
    )
    put_blocks(flow_ref, flow)
    put_blocks(d_rate_ref, d_rate)
    put_blocks(now_ref, now)
    d_proj_ref[rank : rank + states, :] = lane_sums(in_part_ref, states)
    d_proj_ref[rank + states :, :] = lane_sums(out_part_ref, states)
    act = act_ref[...].astype(jnp.float32)
    d_step = pulled_ref[...] * (1.0 / LOG2E) + act * weighted_ref[...]
    d_logits = (d_step * slope_ref[...]).astype(jnp.bfloat16)
    d_logits_ref[...] = d_logits
    d_bias_ref[...] += jnp.sum(d_logits.astype(jnp.float32), axis=0, keepdims=True)
    d_skip_ref[...] += jnp.sum(up_ref[...] * act, axis=0, keepdims=True)
    d_act_ref[...] = up_ref[...] * skip_ref[...] + steps_ref[...] * weighted_ref[...]
    d_proj_ref[:rank, :] = lax.dot_general(
        w_dt_ref[...],
        d_logits,
        (((1,), (1,)), ((), ())),
        preferred_element_type=jnp.float32,
    )


def cost(scale, tokens, states, width):
    work = tokens * states * width
    return pl.CostEstimate(flops=scale * work, bytes_accessed=8 * work, transcendentals=work)


def whole(array):
    return pl.BlockSpec(array.shape, lambda c: (0,) * len(array.shape))


def scan(proj, act, gate, keep, rates, w_dt, bias, skip):
    tokens, width = act.shape
    states = rates.shape[0]
    by_row = lambda size, wide: pl.BlockSpec((size, wide), lambda c: (c, 0))
    like = jax.ShapeDtypeStruct
    scratch = lambda *shape: pltpu.VMEM(shape, jnp.float32)
    state = like((states, width), jnp.float32)
    return pl.pallas_call(
        scan_kernel,
        grid=(tokens // CHUNK,),
        in_specs=[
            pl.BlockSpec((proj.shape[0], CHUNK), lambda c: (0, c)),
            by_row(CHUNK, width),
            by_row(CHUNK, width),
            by_row(CHUNK, LANES),
            whole(rates),
            whole(w_dt),
            whole(bias),
            whole(skip),
        ],
        out_specs=[by_row(CHUNK, width)] * 4 + [by_row(CHUNK * states, width), whole(state)],
        out_shape=[
            like((tokens, width), jnp.bfloat16),
            like((tokens, width), jnp.float32),
            like((tokens, width), jnp.float32),
            like((tokens, width), jnp.float32),
            like((tokens * states, width), jnp.float32),
            state,
        ],
        scratch_shapes=[scratch(states, width)]
        + [scratch(CHUNK, width)] * 3
        + [scratch(2 * states, CHUNK)],
        compiler_params=pltpu.CompilerParams(
            dimension_semantics=("arbitrary",), vmem_limit_bytes=VMEM_LIMIT
        ),
        cost_estimate=cost(2400, tokens, states, width),
        name="scan",
    )(proj, act, gate, keep, rates, w_dt, bias, skip)


def adjoint(proj, act, steps, slope, upstream, keep, rates, w_dt, skip, history, last):
    tokens, width = act.shape
    states = rates.shape[0]
    count = tokens // CHUNK
    by_row = lambda size, wide: pl.BlockSpec((size, wide), lambda c: (count - 1 - c, 0))
    cols = pl.BlockSpec((proj.shape[0], CHUNK), lambda c: (0, count - 1 - c))
    like = jax.ShapeDtypeStruct
    scratch = lambda *shape: pltpu.VMEM(shape, jnp.float32)
    line = like((1, width), jnp.float32)
    return pl.pallas_call(
        adjoint_kernel,
        grid=(count,),
        in_specs=[cols]
        + [by_row(CHUNK, width)] * 4
        + [by_row(CHUNK, LANES), whole(rates), whole(w_dt), whole(skip)]
        + [by_row(CHUNK * states, width), whole(last)],
        out_specs=[by_row(CHUNK, width)] * 2 + [cols, whole(last), whole(line), whole(line)],
        out_shape=[
            like((tokens, width), jnp.bfloat16),
            like((tokens, width), jnp.float32),
            like(proj.shape, jnp.float32),
            like(last.shape, jnp.float32),
            line,
            line,
        ],
        scratch_shapes=[scratch(states, width)] * 2
        + [pltpu.VMEM((CHUNK * states, LANES), jnp.bfloat16)] * 2
        + [scratch(CHUNK, width)] * 4
        + [scratch(PARTS, 2 * states, CHUNK)],
        compiler_params=pltpu.CompilerParams(
            dimension_semantics=("arbitrary",), vmem_limit_bytes=VMEM_LIMIT
        ),
        cost_estimate=cost(4800, tokens, states, width),
        name="adjoint",
    )(proj, act, steps, slope, upstream, keep, rates, w_dt, skip, history, last)


EPS = 1e-05
BF16 = jnp.bfloat16
F32 = jnp.float32


def swap(array, axis, k):
    size = lax.axis_size(axis)
    return lax.ppermute(array, axis, [(i, i ^ k) for i in range(size)])


def after(value, *others):
    return lax.optimization_barrier((value, others))[0]


def pieces_over(array, axis, hold=None):
    pieces = [array] + [swap(array, axis, k) for k in range(1, lax.axis_size(axis))]
    return pieces if hold is None else [after(piece, hold) for piece in pieces]


def assemble(pieces, axis, dim):
    me, size = lax.axis_index(axis), pieces[0].shape[dim]
    shape = pieces[0].shape[:dim] + (size * len(pieces),) + pieces[0].shape[dim + 1 :]
    out = jnp.zeros(shape, pieces[0].dtype)
    for k, piece in enumerate(pieces):
        out = lax.dynamic_update_slice_in_dim(out, piece, (me ^ k) * size, dim)
    return row_major(out)


def gather(array, axis, dim, hold=None):
    return assemble(pieces_over(array, axis, hold), axis, dim)


def row_major(array):
    return with_layout_constraint(array, Layout(major_to_minor=tuple(range(array.ndim))))


def piece_of(array, axis, dim, index):
    size = array.shape[dim] // lax.axis_size(axis)
    return lax.dynamic_slice_in_dim(array, index * size, size, dim)


def shares(array, axis, dim, kind):
    me = lax.axis_index(axis)
    own = piece_of(array, axis, dim, me).astype(F32)
    sent = [
        piece_of(array, axis, dim, me ^ k).astype(kind) for k in range(1, lax.axis_size(axis))
    ]
    return own, sent


def collect(own, sent, axis):
    return total([own] + [swap(part, axis, k + 1).astype(F32) for k, part in enumerate(sent)])


def scatter_sum(array, axis, dim, kind):
    return collect(*shares(array, axis, dim, kind), axis)


def halving_sum(pieces, axis, k=1):
    while len(pieces) > 1:
        came = [swap(piece.astype(BF16), axis, k) for piece in pieces[1::2]]
        pieces = [own.astype(F32) + part.astype(F32) for own, part in zip(pieces[::2], came)]
        k *= 2
    return pieces[0]


def doubling_pieces(array, axis):
    k = lax.axis_size(axis) // 2
    pieces = {0: array}
    while k:
        pieces.update({j ^ k: swap(piece, axis, k) for j, piece in pieces.items()})
        k //= 2
    return [pieces[j] for j in range(len(pieces))]


def doubling_sum(array, axes):
    for axis in axes:
        k = 1
        while k < lax.axis_size(axis):
            array = array + swap(array, axis, k)
            k *= 2
    return array


def dot(left, right, left_dim=1, right_dim=0):
    return lax.dot_general(left, right, (((left_dim,), (right_dim,)), ((), ())), preferred_element_type=F32)


def silu_slope(v):
    s = jax.nn.sigmoid(v)
    return s * (1.0 + v * (1.0 - s))


def inverse_rms(x):
    return lax.rsqrt(jnp.mean(x * x, axis=-1, keepdims=True) + EPS)


def shards(
    block_input,
    doc_ids,
    norm_gain,
    in_proj,
    conv_weight,
    conv_bias,
    x_proj,
    dt_proj,
    dt_bias,
    a_log,
    d_skip,
    out_proj,
    grad_output,
):
    seqs, piece, width = block_input.shape
    length = doc_ids.shape[1]
    ctx, ctxs = lax.axis_index("context"), lax.axis_size("context")
    taps, tail = conv_weight.shape[0], conv_weight.shape[0] - 1
    states = a_log.shape[0]
    rows = seqs * length
    inner = in_proj.shape[2] // ctxs
    rank = dt_proj.shape[0] * lax.axis_size("fsdp")

    def mine(array, dim):
        return piece_of(array, "context", dim, ctx)

    in_half = mine(in_proj, 2)
    xcols, dtrows, share = x_proj.shape[1], dt_proj.shape[0], in_proj.shape[1]
    x_own = block_input.reshape(seqs * piece, width).astype(F32)
    normed_own = (x_own * inverse_rms(x_own) * norm_gain).astype(BF16)
    first = pieces_over(
        jnp.concatenate([mine(x_proj, 0).T, mine(dt_proj, 1), in_half[0]], axis=0),
        "fsdp",
        normed_own,
    )
    w_x = assemble([p[:xcols] for p in first], "fsdp", 0)
    w_dt = assemble([p[xcols : xcols + dtrows] for p in first], "fsdp", 0)
    w_conv = assemble([p[xcols + dtrows :] for p in first], "fsdp", 0)
    normed = [normed_own] + [swap(normed_own, "context", k) for k in range(1, ctxs)]
    def whole_tokens(parts):
        out = jnp.zeros((seqs, length, parts[0].shape[-1]), parts[0].dtype)
        for k, part in enumerate(parts):
            part = part.reshape(seqs, piece, part.shape[-1])
            out = lax.dynamic_update_slice_in_dim(out, part, (ctx ^ k) * piece, 1)
        return out.reshape(rows, -1)

    def token_parts(array):
        array = array.reshape(seqs, length, array.shape[-1])
        parts = [piece_of(array, "context", 1, ctx ^ k) for k in range(ctxs)]
        return [part.reshape(seqs * piece, -1) for part in parts]

    def over_tokens(left, right):
        return total([dot(l, r, 0, 0) for l, r in zip(left, right)])

    taps_w, bias, dt_b = mine(conv_weight, 1), mine(conv_bias, 0), mine(dt_bias, 0)
    rates = -jnp.exp(mine(a_log, 1))
    skip = mine(d_skip, 0)

    conv_input = whole_tokens([dot(part, w_conv).astype(BF16) for part in normed])
    padded_ids = jnp.concatenate([jnp.full((seqs, tail), -1, jnp.int32), doc_ids], axis=1)
    same = [
        (padded_ids[:, tail - k : tail - k + length] == doc_ids).astype(F32)[..., None]
        for k in range(taps)
    ]
    padded = jnp.pad(conv_input.reshape(seqs, length, inner), ((0, 0), (tail, 0), (0, 0))).astype(F32)
    shifted = [padded[:, tail - k : tail - k + length] for k in range(taps)]
    conv_output = bias
    for k in range(taps):
        conv_output = conv_output + taps_w[k] * shifted[k] * same[k]
    conv_flat = conv_output.reshape(rows, inner)
    activated = jax.nn.silu(conv_flat).astype(BF16)
    def all_sum(part, *beside):
        halved = scatter_sum(part, "context", 1, F32)
        halved = after(halved, *beside)
        summed = scatter_sum(halved, "tensor", 1, BF16).astype(BF16)
        return gather(gather(summed, "tensor", 1), "context", 1), halved, summed

    keep = jnp.broadcast_to(same[1].reshape(rows, 1), (rows, LANES))
    projections, _, summed = all_sum(dot(w_x, activated, 1, 1), keep)
    w_gate = after(
        lax.all_gather(after(in_half[1], first), "fsdp", axis=0, tiled=True), summed
    )
    w_out = lax.all_gather(after(mine(out_proj, 0).T, conv_input), "fsdp", axis=0, tiled=True)
    own_cotangent = grad_output.reshape(seqs * piece, width)
    cotangent = [own_cotangent] + [
        swap(after(own_cotangent, conv_input), "context", k) for k in range(1, ctxs)
    ]
    dt_input = projections[:rank]
    gate = whole_tokens([dot(part, w_gate) for part in normed])
    gated, sloped, steps, slope, history, last = scan(
        projections, activated, gate, keep, rates * LOG2E, w_dt, dt_b[None], skip[None]
    )
    w_out = after(w_out, gated)

    def my_tokens(parts):
        return [parts[0]] + [swap(parts[k], "context", k) for k in range(1, ctxs)]

    def all_halves(weight):
        return [weight] + [swap(weight, "context", k) for k in range(1, ctxs)]

    zplace = lax.axis_index("tensor")
    x_flat = block_input.reshape(seqs * piece, width)
    gated_parts = token_parts(gated)
    branch = dot(
        jnp.concatenate(my_tokens(gated_parts), axis=1),
        jnp.concatenate(all_halves(w_out), axis=1),
        1,
        1,
    ).astype(BF16)
    later = [after(part, branch) for part in cotangent[1:]]
    d_gated = whole_tokens([dot(part, w_out) for part in cotangent[:1] + later])
    d_mixed = d_gated * jax.nn.silu(gate)
    d_gate = (d_gated * sloped).astype(BF16)
    branch = lax.psum_scatter(branch, "tensor", scatter_dimension=0, tiled=True).astype(F32)

    d_logits, d_act, d_part, d_rates, d_bias, d_skips = adjoint(
        projections, activated, steps, slope, d_mixed, keep, rates * LOG2E, w_dt, skip[None],
        history, last,
    )
    gate_halves, conv_halves = all_halves(w_gate), all_halves(w_conv)
    d_part, branch, gate_halves, conv_halves = after((d_part, branch, gate_halves, conv_halves))
    x_rows = piece_of(x_flat, "tensor", 0, zplace).astype(F32)
    output_rows = (x_rows + branch).astype(BF16)
    d_projections, halved, summed = all_sum(d_part, output_rows)
    block_output = lax.all_gather(output_rows[None], "tensor", axis=1, tiled=True)
    gate_parts = token_parts(d_gate)
    late_gate = after(gate_parts, halved)
    grad_gate_part = over_tokens(normed, late_gate)
    grad_dt_part = dot(dt_input, d_logits)
    d_act = d_act + dot(d_projections, w_x, 0, 0)
    grad_x_part = dot(d_projections, activated)
    d_conv = (d_act * silu_slope(conv_flat)).reshape(seqs, length, inner)
    d_conv_input = jnp.zeros((seqs, length, inner), F32)
    tap_grads = []
    for k in range(taps):
        masked = d_conv * same[k]
        late = jnp.pad(masked, ((0, 0), (0, tail), (0, 0)))[:, k : k + length]
        d_conv_input = d_conv_input + taps_w[k] * late
        tap_grads.append(jnp.sum(masked * shifted[k], axis=(0, 1)))
    d_conv_input = d_conv_input.reshape(rows, inner).astype(BF16)
    conv_parts = token_parts(d_conv_input)
    left = jnp.concatenate(my_tokens(gate_parts) + my_tokens(conv_parts), axis=1)
    right = jnp.concatenate(gate_halves + conv_halves, axis=1)
    partial = dot(left, right, 1, 1).astype(BF16)
    row_parts = [
        piece_of(partial, "tensor", 0, zplace ^ k) for k in range(lax.axis_size("tensor"))
    ]
    row_parts, block_output = after((row_parts, block_output))
    came = [swap(part, "tensor", 1) for part in row_parts[1::2]]
    row_parts = [own.astype(F32) + part.astype(F32) for own, part in zip(row_parts[::2], came)]
    d_normed = halving_sum(row_parts, "tensor", 2)
    grad_out_part = over_tokens(cotangent, after(gated_parts, came[1]))
    grad_conv_part = over_tokens(normed, conv_parts)
    d_rows = piece_of(own_cotangent, "tensor", 0, zplace).astype(F32)
    inv = inverse_rms(x_rows)
    scaled = d_normed * norm_gain
    inner_sum = jnp.sum(scaled * x_rows, axis=-1, keepdims=True)
    grad_rows = d_rows + inv * scaled - x_rows * (inv * inv * inv) * inner_sum / width
    grad_rows = after(grad_rows.astype(BF16))
    row_pieces = doubling_pieces(grad_rows, "tensor")
    gain = jnp.sum(d_normed * x_rows * inv, axis=0)
    devices = lax.axis_size("fsdp")

    def owned(parts, hold=()):
        pieces = [part.reshape(devices, -1, inner).astype(BF16) for part in parts]
        fill = -sum(piece.shape[1] for piece in pieces) % LANES
        pieces.append(jnp.zeros((devices, fill, inner), BF16))
        pieces = row_major(jnp.concatenate(pieces, axis=1).reshape(-1, inner))
        return lax.psum_scatter(after(pieces, hold), "fsdp", scatter_dimension=0, tiled=True)

    sums = jnp.concatenate(
        [
            owned((grad_conv_part, grad_out_part, grad_x_part, grad_dt_part), d_normed),
            owned((grad_gate_part,)),
        ]
    )
    thin = jnp.concatenate(
        [
            d_rates * rates,
            jnp.stack(tap_grads),
            jnp.sum(d_conv, axis=(0, 1))[None],
            d_bias,
            d_skips,
            gain.reshape(-1, inner),
        ],
        axis=0,
    )
    channels = states + taps + 3
    thin = doubling_sum(after(thin, row_pieces[1]), ("fsdp",))
    others = [thin] + [swap(thin, "context", k) for k in range(1, ctxs)]
    def side_by_side(parts, dim):
        size = parts[0].shape[dim]
        shape = parts[0].shape[:dim] + (size * ctxs,) + parts[0].shape[dim + 1 :]
        out = jnp.zeros(shape, parts[0].dtype)
        for k, part in enumerate(parts):
            out = lax.dynamic_update_slice_in_dim(out, part, (ctx ^ k) * size, dim)
        return out

    thin = side_by_side([part[:channels] for part in others], 1)
    sums = [sums] + [swap(sums, "context", k) for k in range(1, ctxs)]
    grad_in = side_by_side(
        [jnp.stack([part[:share], part[-share:]]).astype(F32) for part in sums], 2
    )
    grad_out = side_by_side([part[share : 2 * share].T.astype(F32) for part in sums], 0)
    thin_at = 2 * share + xcols
    grad_x = side_by_side([part[2 * share : thin_at].T.astype(F32) for part in sums], 0)
    grad_dt = side_by_side([part[thin_at : thin_at + dtrows].astype(F32) for part in sums], 1)
    gain = total([part[channels:] for part in others]).reshape(1, width)
    grad_gain = doubling_sum(gain, ("tensor",))[0]
    count = grad_rows.shape[0]
    grad_input = jnp.zeros((count * lax.axis_size("tensor"), width), BF16)
    row_pieces[-1] = after(row_pieces[-1], grad_in, grad_out, grad_x, grad_dt)
    for k, part in enumerate(row_pieces):
        grad_input = lax.dynamic_update_slice_in_dim(grad_input, part, (zplace ^ k) * count, 0)
    grad_input = grad_input.reshape(block_input.shape)

    return (
        block_output.reshape(block_input.shape),
        grad_input,
        grad_gain,
        grad_in,
        thin[states : states + taps],
        thin[states + taps],
        grad_x,
        grad_dt,
        thin[states + taps + 1],
        thin[:states],
        thin[states + taps + 2],
        grad_out,
    )


def solution(mesh):
    placed = (
        P("fsdp", "context", None),
        P("fsdp", None),
        P(),
        P(None, "fsdp", "tensor"),
        P(None, "tensor"),
        P("tensor"),
        P("tensor", "fsdp"),
        P("fsdp", "tensor"),
        P("tensor"),
        P(None, "tensor"),
        P("tensor"),
        P("tensor", "fsdp"),
        P("fsdp", "context", None),
    )
    return jax.shard_map(
        shards,
        mesh=mesh,
        in_specs=placed,
        out_specs=(
            P("fsdp", "context", None),
            P("fsdp", "context", None),
            P(),
            P(None, "fsdp", "tensor"),
            P(None, "tensor"),
            P("tensor"),
            P("tensor", "fsdp"),
            P("fsdp", "tensor"),
            P("tensor"),
            P(None, "tensor"),
            P("tensor"),
            P("tensor", "fsdp"),
        ),
        check_vma=False,
    )
```

```python
import functools

import jax
import jax.numpy as jnp
from jax import lax
from jax.experimental import pallas as pl
from jax.experimental.layout import Layout, with_layout_constraint
from jax.experimental.pallas import tpu as pltpu
from jax.sharding import PartitionSpec as P

LANES = 128
SUB = 8
CHUNK = 128
PARTS = 2
VMEM_LIMIT = 50 << 20
GONE = 1e4
LOG2E = 1.4426950408889634


def span(group):
    return slice(group * LANES, (group + 1) * LANES)


def blocks(ref, halves, groups):
    return [[ref[SUB * i : SUB * i + SUB, span(g)] for g in range(groups)] for i in range(halves)]


def put_blocks(ref, values):
    for i, line in enumerate(values):
        for g, value in enumerate(line):
            ref[SUB * i : SUB * i + SUB, span(g)] = value


def column(ref, halves, t):
    return [
        jnp.broadcast_to(ref[SUB * i : SUB * i + SUB, t : t + 1], (SUB, LANES))
        for i in range(halves)
    ]


def row(tile, r):
    return jnp.broadcast_to(tile[r : r + 1, :], (SUB, LANES))


def sublane_bits():
    index = lax.broadcasted_iota(jnp.int32, (SUB, LANES), 0)
    return [(index & d) == 0 for d in (1, 2, 4)]


def fold(pending, value, bits, falling):
    level = 0
    while pending and pending[-1][0] == level:
        _, other = pending.pop()
        early, late = (value, other) if falling else (other, value)
        d = 1 << level
        if d < 4:
            value = jnp.where(
                bits[level], early + pltpu.roll(early, SUB - d, 0), late + pltpu.roll(late, d, 0)
            )
        else:
            value = jnp.where(bits[level], early, late) + pltpu.roll(
                jnp.where(bits[level], late, early), d, 0
            )
        level += 1
    pending.append((level, value))


def total(values):
    return functools.reduce(lambda a, b: a + b, values)


def soft_step(v):
    small = jnp.exp(-jnp.abs(v))
    slope = jnp.where(v >= 0, 1.0, small) / (1.0 + small)
    return jnp.maximum(v, 0.0) + jnp.log1p(small), slope


def step_rows(steps, act, keep_ref, fade_ref, fed_ref):
    for g in range(steps.shape[1] // LANES):
        fade_ref[:, span(g)] = jnp.where(keep_ref[...] > 0, steps[:, span(g)], GONE)
    fed_ref[...] = steps * act


def scan_kernel(
    proj_ref,
    act_ref,
    gate_ref,
    keep_ref,
    rate_ref,
    w_dt_ref,
    bias_ref,
    skip_ref,
    gated_ref,
    sloped_ref,
    steps_ref,
    slope_ref,
    h_ref,
    last_ref,
    state_ref,
    fade_ref,
    fed_ref,
    y_ref,
    coef_ref,
):
    chunk, width = act_ref.shape
    halves, groups = rate_ref.shape[0] // SUB, width // LANES
    states, rank = rate_ref.shape[0], w_dt_ref.shape[0]

    @pl.when(pl.program_id(0) == 0)
    def _():
        state_ref[...] = jnp.zeros_like(state_ref)

    logits = (
        lax.dot_general(
            proj_ref[:rank, :],
            w_dt_ref[...],
            (((0,), (0,)), ((), ())),
            preferred_element_type=jnp.float32,
        )
        + bias_ref[...]
    )
    steps, slope_ref[...] = soft_step(logits)
    steps_ref[...] = steps
    step_rows(steps, act_ref[...].astype(jnp.float32), keep_ref, fade_ref, fed_ref)
    coef_ref[...] = proj_ref[rank:, :].astype(jnp.float32)
    in_ref, out_ref = coef_ref.at[:states], coef_ref.at[states:]
    rate = blocks(rate_ref, halves, groups)
    state = blocks(state_ref, halves, groups)
    bits = sublane_bits()
    for base in range(0, chunk, SUB):
        fade = [fade_ref[base : base + SUB, span(g)] for g in range(groups)]
        fed = [fed_ref[base : base + SUB, span(g)] for g in range(groups)]
        pending = [[] for _ in range(groups)]
        for r in range(SUB):
            t = base + r
            in_col, out_col = column(in_ref, halves, t), column(out_ref, halves, t)
            for g in range(groups):
                fade_row, fed_row = row(fade[g], r), row(fed[g], r)
                parts = []
                for i in range(halves):
                    place = (t * halves + i) * SUB
                    h_ref[place : place + SUB, span(g)] = state[i][g]
                    factor = jnp.exp2(fade_row * rate[i][g])
                    state[i][g] = factor * state[i][g] + fed_row * in_col[i]
                    parts.append(state[i][g] * out_col[i])
                fold(pending[g], total(parts), bits, False)
        for g in range(groups):
            y_ref[base : base + SUB, span(g)] = pending[g][0][1]
    put_blocks(state_ref, state)
    last_ref[...] = state_ref[...]
    mixed = y_ref[...] + skip_ref[...] * act_ref[...].astype(jnp.float32)
    gate = gate_ref[...]
    sigmoid = jax.nn.sigmoid(gate)
    gated_ref[...] = (mixed * (gate * sigmoid)).astype(jnp.bfloat16)
    sloped_ref[...] = mixed * (sigmoid * (1.0 + gate * (1.0 - sigmoid)))


def lane_sums(products_ref, states):
    ones = jnp.ones((LANES, LANES), jnp.bfloat16)
    sums = jnp.dot(products_ref[...], ones, preferred_element_type=jnp.float32)
    lane = lax.broadcasted_iota(jnp.int32, (states, LANES), 1)
    result = jnp.zeros((states, LANES), jnp.float32)
    for t in range(CHUNK):
        result = jnp.where(lane == t, sums[t * states : (t + 1) * states], result)
    return result


def adjoint_kernel(
    proj_ref,
    act_ref,
    steps_ref,
    slope_ref,
    up_ref,
    keep_ref,
    rate_ref,
    w_dt_ref,
    skip_ref,
    h_ref,
    last_ref,
    d_logits_ref,
    d_act_ref,
    d_proj_ref,
    d_rate_ref,
    d_bias_ref,
    d_skip_ref,
    flow_ref,
    now_ref,
    in_part_ref,
    out_part_ref,
    fade_ref,
    fed_ref,
    weighted_ref,
    pulled_ref,
    coef_ref,
):
    chunk, width = act_ref.shape
    halves, groups = rate_ref.shape[0] // SUB, width // LANES
    states, rank = rate_ref.shape[0], w_dt_ref.shape[0]
    size = chunk // PARTS

    @pl.when(pl.program_id(0) == 0)
    def _():
        flow_ref[...] = jnp.zeros_like(flow_ref)
        d_rate_ref[...] = jnp.zeros_like(d_rate_ref)
        d_bias_ref[...] = jnp.zeros_like(d_bias_ref)
        d_skip_ref[...] = jnp.zeros_like(d_skip_ref)
        now_ref[...] = last_ref[...]

    step_rows(steps_ref[...], act_ref[...].astype(jnp.float32), keep_ref, fade_ref, fed_ref)
    for part in range(PARTS):
        coef = proj_ref[rank:, :].astype(jnp.float32)
        coef_ref[part] = pltpu.roll(coef, -part * size % chunk, 1) if part else coef
    rate = blocks(rate_ref, halves, groups)
    bits = sublane_bits()

    def tokens(step, carry):
        flow, d_rate, now = jax.tree.map(lambda v: v, carry)
        part = PARTS - 1 - step
        in_ref, out_ref = coef_ref.at[part, :states], coef_ref.at[part, states:]
        for base in range(size - SUB, -SUB, -SUB):
            here = pl.ds(pl.multiple_of(part * size + base, SUB), SUB)
            fade = [fade_ref[here, span(g)] for g in range(groups)]
            fed = [fed_ref[here, span(g)] for g in range(groups)]
            up = [up_ref[here, span(g)] for g in range(groups)]
            weighted = [[] for _ in range(groups)]
            slopes = [[] for _ in range(groups)]
            for r in range(SUB - 1, -1, -1):
                t = base + r
                in_col, out_col = column(in_ref, halves, t), column(out_ref, halves, t)
                in_parts = [[] for _ in range(halves)]
                out_parts = [[] for _ in range(halves)]
                first = (part * size + t) * states
                for g in range(groups):
                    fade_row, fed_row, up_row = row(fade[g], r), row(fed[g], r), row(up[g], r)
                    by_in, by_rate = [], []
                    for i in range(halves):
                        place = pl.ds(pl.multiple_of(first + i * SUB, SUB), SUB)
                        before = h_ref[place, span(g)]
                        factor = jnp.exp2(fade_row * rate[i][g])
                        adjoint = out_col[i] * up_row + flow[i][g]
                        out_parts[i].append(now[i][g] * up_row)
                        in_parts[i].append(adjoint * fed_row)
                        flow[i][g] = factor * adjoint
                        pulled = flow[i][g] * before
                        by_in.append(adjoint * in_col[i])
                        by_rate.append(pulled * rate[i][g])
                        d_rate[i][g] = d_rate[i][g] + pulled * fade_row
                        now[i][g] = before
                    fold(weighted[g], total(by_in), bits, True)
                    fold(slopes[g], total(by_rate), bits, True)
                place = pl.ds(pl.multiple_of(first, states), states)
                for ref, parts in ((in_part_ref, in_parts), (out_part_ref, out_parts)):
                    ref[place, :] = jnp.concatenate([total(p) for p in parts]).astype(jnp.bfloat16)
            for g in range(groups):
                weighted_ref[here, span(g)] = weighted[g][0][1]
                pulled_ref[here, span(g)] = slopes[g][0][1]
        return flow, d_rate, now

    flow, d_rate, now = lax.fori_loop(
        0,
        PARTS,
        tokens,
        tuple(blocks(ref, halves, groups) for ref in (flow_ref, d_rate_ref, now_ref)),
    )
    put_blocks(flow_ref, flow)
    put_blocks(d_rate_ref, d_rate)
    put_blocks(now_ref, now)
    d_proj_ref[rank : rank + states, :] = lane_sums(in_part_ref, states)
    d_proj_ref[rank + states :, :] = lane_sums(out_part_ref, states)
    act = act_ref[...].astype(jnp.float32)
    d_step = pulled_ref[...] * (1.0 / LOG2E) + act * weighted_ref[...]
    d_logits = (d_step * slope_ref[...]).astype(jnp.bfloat16)
    d_logits_ref[...] = d_logits
    d_bias_ref[...] += jnp.sum(d_logits.astype(jnp.float32), axis=0, keepdims=True)
    d_skip_ref[...] += jnp.sum(up_ref[...] * act, axis=0, keepdims=True)
    d_act_ref[...] = up_ref[...] * skip_ref[...] + steps_ref[...] * weighted_ref[...]
    d_proj_ref[:rank, :] = lax.dot_general(
        w_dt_ref[...],
        d_logits,
        (((1,), (1,)), ((), ())),
        preferred_element_type=jnp.float32,
    )


def cost(scale, tokens, states, width):
    work = tokens * states * width
    return pl.CostEstimate(flops=scale * work, bytes_accessed=8 * work, transcendentals=work)


def whole(array):
    return pl.BlockSpec(array.shape, lambda c: (0,) * len(array.shape))


def scan(proj, act, gate, keep, rates, w_dt, bias, skip):
    tokens, width = act.shape
    states = rates.shape[0]
    by_row = lambda size, wide: pl.BlockSpec((size, wide), lambda c: (c, 0))
    like = jax.ShapeDtypeStruct
    scratch = lambda *shape: pltpu.VMEM(shape, jnp.float32)
    state = like((states, width), jnp.float32)
    return pl.pallas_call(
        scan_kernel,
        grid=(tokens // CHUNK,),
        in_specs=[
            pl.BlockSpec((proj.shape[0], CHUNK), lambda c: (0, c)),
            by_row(CHUNK, width),
            by_row(CHUNK, width),
            by_row(CHUNK, LANES),
            whole(rates),
            whole(w_dt),
            whole(bias),
            whole(skip),
        ],
        out_specs=[by_row(CHUNK, width)] * 4 + [by_row(CHUNK * states, width), whole(state)],
        out_shape=[
            like((tokens, width), jnp.bfloat16),
            like((tokens, width), jnp.float32),
            like((tokens, width), jnp.float32),
            like((tokens, width), jnp.float32),
            like((tokens * states, width), jnp.float32),
            state,
        ],
        scratch_shapes=[scratch(states, width)]
        + [scratch(CHUNK, width)] * 3
        + [scratch(2 * states, CHUNK)],
        compiler_params=pltpu.CompilerParams(
            dimension_semantics=("arbitrary",), vmem_limit_bytes=VMEM_LIMIT
        ),
        cost_estimate=cost(2400, tokens, states, width),
        name="scan",
    )(proj, act, gate, keep, rates, w_dt, bias, skip)


def adjoint(proj, act, steps, slope, upstream, keep, rates, w_dt, skip, history, last):
    tokens, width = act.shape
    states = rates.shape[0]
    count = tokens // CHUNK
    by_row = lambda size, wide: pl.BlockSpec((size, wide), lambda c: (count - 1 - c, 0))
    cols = pl.BlockSpec((proj.shape[0], CHUNK), lambda c: (0, count - 1 - c))
    like = jax.ShapeDtypeStruct
    scratch = lambda *shape: pltpu.VMEM(shape, jnp.float32)
    line = like((1, width), jnp.float32)
    return pl.pallas_call(
        adjoint_kernel,
        grid=(count,),
        in_specs=[cols]
        + [by_row(CHUNK, width)] * 4
        + [by_row(CHUNK, LANES), whole(rates), whole(w_dt), whole(skip)]
        + [by_row(CHUNK * states, width), whole(last)],
        out_specs=[by_row(CHUNK, width)] * 2 + [cols, whole(last), whole(line), whole(line)],
        out_shape=[
            like((tokens, width), jnp.bfloat16),
            like((tokens, width), jnp.float32),
            like(proj.shape, jnp.float32),
            like(last.shape, jnp.float32),
            line,
            line,
        ],
        scratch_shapes=[scratch(states, width)] * 2
        + [pltpu.VMEM((CHUNK * states, LANES), jnp.bfloat16)] * 2
        + [scratch(CHUNK, width)] * 4
        + [scratch(PARTS, 2 * states, CHUNK)],
        compiler_params=pltpu.CompilerParams(
            dimension_semantics=("arbitrary",), vmem_limit_bytes=VMEM_LIMIT
        ),
        cost_estimate=cost(4800, tokens, states, width),
        name="adjoint",
    )(proj, act, steps, slope, upstream, keep, rates, w_dt, skip, history, last)


EPS = 1e-05
BF16 = jnp.bfloat16
F32 = jnp.float32


def swap(array, axis, k):
    size = lax.axis_size(axis)
    return lax.ppermute(array, axis, [(i, i ^ k) for i in range(size)])


def after(value, *others):
    return lax.optimization_barrier((value, others))[0]


def pieces_over(array, axis, hold=None):
    pieces = [array] + [swap(array, axis, k) for k in range(1, lax.axis_size(axis))]
    return pieces if hold is None else [after(piece, hold) for piece in pieces]


def assemble(pieces, axis, dim):
    me, size = lax.axis_index(axis), pieces[0].shape[dim]
    shape = pieces[0].shape[:dim] + (size * len(pieces),) + pieces[0].shape[dim + 1 :]
    out = jnp.zeros(shape, pieces[0].dtype)
    for k, piece in enumerate(pieces):
        out = lax.dynamic_update_slice_in_dim(out, piece, (me ^ k) * size, dim)
    return row_major(out)


def gather(array, axis, dim, hold=None):
    return assemble(pieces_over(array, axis, hold), axis, dim)


def row_major(array):
    return with_layout_constraint(array, Layout(major_to_minor=tuple(range(array.ndim))))


def piece_of(array, axis, dim, index):
    size = array.shape[dim] // lax.axis_size(axis)
    return lax.dynamic_slice_in_dim(array, index * size, size, dim)


def shares(array, axis, dim, kind):
    me = lax.axis_index(axis)
    own = piece_of(array, axis, dim, me).astype(F32)
    sent = [
        piece_of(array, axis, dim, me ^ k).astype(kind) for k in range(1, lax.axis_size(axis))
    ]
    return own, sent


def collect(own, sent, axis):
    return total([own] + [swap(part, axis, k + 1).astype(F32) for k, part in enumerate(sent)])


def scatter_sum(array, axis, dim, kind):
    return collect(*shares(array, axis, dim, kind), axis)


def halving_sum(pieces, axis, k=1):
    while len(pieces) > 1:
        came = [swap(piece.astype(BF16), axis, k) for piece in pieces[1::2]]
        pieces = [own.astype(F32) + part.astype(F32) for own, part in zip(pieces[::2], came)]
        k *= 2
    return pieces[0]


def doubling_pieces(array, axis):
    k = lax.axis_size(axis) // 2
    pieces = {0: array}
    while k:
        pieces.update({j ^ k: swap(piece, axis, k) for j, piece in pieces.items()})
        k //= 2
    return [pieces[j] for j in range(len(pieces))]


def doubling_sum(array, axes):
    for axis in axes:
        k = 1
        while k < lax.axis_size(axis):
            array = array + swap(array, axis, k)
            k *= 2
    return array


def dot(left, right, left_dim=1, right_dim=0):
    return lax.dot_general(left, right, (((left_dim,), (right_dim,)), ((), ())), preferred_element_type=F32)


def silu_slope(v):
    s = jax.nn.sigmoid(v)
    return s * (1.0 + v * (1.0 - s))


def inverse_rms(x):
    return lax.rsqrt(jnp.mean(x * x, axis=-1, keepdims=True) + EPS)


def shards(
    block_input,
    doc_ids,
    norm_gain,
    in_proj,
    conv_weight,
    conv_bias,
    x_proj,
    dt_proj,
    dt_bias,
    a_log,
    d_skip,
    out_proj,
    grad_output,
):
    seqs, piece, width = block_input.shape
    length = doc_ids.shape[1]
    ctx, ctxs = lax.axis_index("context"), lax.axis_size("context")
    taps, tail = conv_weight.shape[0], conv_weight.shape[0] - 1
    states = a_log.shape[0]
    rows = seqs * length
    inner = in_proj.shape[2] // ctxs
    rank = dt_proj.shape[0] * lax.axis_size("fsdp")

    def mine(array, dim):
        return piece_of(array, "context", dim, ctx)

    in_half = mine(in_proj, 2)
    xcols, dtrows, share = x_proj.shape[1], dt_proj.shape[0], in_proj.shape[1]
    x_own = block_input.reshape(seqs * piece, width).astype(F32)
    normed_own = (x_own * inverse_rms(x_own) * norm_gain).astype(BF16)
    first = pieces_over(
        jnp.concatenate([mine(x_proj, 0).T, mine(dt_proj, 1), in_half[0]], axis=0),
        "fsdp",
        normed_own,
    )
    w_x = assemble([p[:xcols] for p in first], "fsdp", 0)
    w_dt = assemble([p[xcols : xcols + dtrows] for p in first], "fsdp", 0)
    w_conv = assemble([p[xcols + dtrows :] for p in first], "fsdp", 0)
    normed = [normed_own] + [swap(normed_own, "context", k) for k in range(1, ctxs)]
    def whole_tokens(parts):
        out = jnp.zeros((seqs, length, parts[0].shape[-1]), parts[0].dtype)
        for k, part in enumerate(parts):
            part = part.reshape(seqs, piece, part.shape[-1])
            out = lax.dynamic_update_slice_in_dim(out, part, (ctx ^ k) * piece, 1)
        return out.reshape(rows, -1)

    def token_parts(array):
        array = array.reshape(seqs, length, array.shape[-1])
        parts = [piece_of(array, "context", 1, ctx ^ k) for k in range(ctxs)]
        return [part.reshape(seqs * piece, -1) for part in parts]

    def over_tokens(left, right):
        return total([dot(l, r, 0, 0) for l, r in zip(left, right)])

    taps_w, bias, dt_b = mine(conv_weight, 1), mine(conv_bias, 0), mine(dt_bias, 0)
    rates = -jnp.exp(mine(a_log, 1))
    skip = mine(d_skip, 0)

    conv_input = whole_tokens([dot(part, w_conv).astype(BF16) for part in normed])
    padded_ids = jnp.concatenate([jnp.full((seqs, tail), -1, jnp.int32), doc_ids], axis=1)
    same = [
        (padded_ids[:, tail - k : tail - k + length] == doc_ids).astype(F32)[..., None]
        for k in range(taps)
    ]
    padded = jnp.pad(conv_input.reshape(seqs, length, inner), ((0, 0), (tail, 0), (0, 0))).astype(F32)
    shifted = [padded[:, tail - k : tail - k + length] for k in range(taps)]
    conv_output = bias
    for k in range(taps):
        conv_output = conv_output + taps_w[k] * shifted[k] * same[k]
    conv_flat = conv_output.reshape(rows, inner)
    activated = jax.nn.silu(conv_flat).astype(BF16)
    def all_sum(part, *beside):
        halved = scatter_sum(part, "context", 1, F32)
        halved = after(halved, *beside)
        summed = scatter_sum(halved, "tensor", 1, BF16).astype(BF16)
        return gather(gather(summed, "tensor", 1), "context", 1), halved, summed

    keep = jnp.broadcast_to(same[1].reshape(rows, 1), (rows, LANES))
    projections, _, summed = all_sum(dot(w_x, activated, 1, 1), keep)
    w_gate = after(
        lax.all_gather(after(in_half[1], first), "fsdp", axis=0, tiled=True), summed
    )
    w_out = lax.all_gather(after(mine(out_proj, 0).T, conv_input), "fsdp", axis=0, tiled=True)
    own_cotangent = grad_output.reshape(seqs * piece, width)
    cotangent = [own_cotangent] + [
        swap(after(own_cotangent, conv_input), "context", k) for k in range(1, ctxs)
    ]
    dt_input = projections[:rank]
    gate = whole_tokens([dot(part, w_gate) for part in normed])
    gated, sloped, steps, slope, history, last = scan(
        projections, activated, gate, keep, rates * LOG2E, w_dt, dt_b[None], skip[None]
    )
    w_out = after(w_out, gated)

    def my_tokens(parts):
        return [parts[0]] + [swap(parts[k], "context", k) for k in range(1, ctxs)]

    def all_halves(weight):
        return [weight] + [swap(weight, "context", k) for k in range(1, ctxs)]

    zplace = lax.axis_index("tensor")
    x_flat = block_input.reshape(seqs * piece, width)
    gated_parts = token_parts(gated)
    branch = dot(
        jnp.concatenate(my_tokens(gated_parts), axis=1),
        jnp.concatenate(all_halves(w_out), axis=1),
        1,
        1,
    ).astype(BF16)
    later = [after(part, branch) for part in cotangent[1:]]
    d_gated = whole_tokens([dot(part, w_out) for part in cotangent[:1] + later])
    d_mixed = d_gated * jax.nn.silu(gate)
    d_gate = (d_gated * sloped).astype(BF16)
    branch = lax.psum_scatter(branch, "tensor", scatter_dimension=0, tiled=True).astype(F32)

    d_logits, d_act, d_part, d_rates, d_bias, d_skips = adjoint(
        projections, activated, steps, slope, d_mixed, keep, rates * LOG2E, w_dt, skip[None],
        history, last,
    )
    gate_halves, conv_halves = all_halves(w_gate), all_halves(w_conv)
    d_part, branch, gate_halves, conv_halves = after((d_part, branch, gate_halves, conv_halves))
    x_rows = piece_of(x_flat, "tensor", 0, zplace).astype(F32)
    output_rows = (x_rows + branch).astype(BF16)
    d_projections, halved, summed = all_sum(d_part, output_rows)
    block_output = lax.all_gather(output_rows[None], "tensor", axis=1, tiled=True)
    gate_parts = token_parts(d_gate)
    late_gate = after(gate_parts, halved)
    grad_gate_part = over_tokens(normed, late_gate)
    grad_dt_part = dot(dt_input, d_logits)
    d_act = d_act + dot(d_projections, w_x, 0, 0)
    grad_x_part = dot(d_projections, activated)
    d_conv = (d_act * silu_slope(conv_flat)).reshape(seqs, length, inner)
    d_conv_input = jnp.zeros((seqs, length, inner), F32)
    tap_grads = []
    for k in range(taps):
        masked = d_conv * same[k]
        late = jnp.pad(masked, ((0, 0), (0, tail), (0, 0)))[:, k : k + length]
        d_conv_input = d_conv_input + taps_w[k] * late
        tap_grads.append(jnp.sum(masked * shifted[k], axis=(0, 1)))
    d_conv_input = d_conv_input.reshape(rows, inner).astype(BF16)
    conv_parts = token_parts(d_conv_input)
    left = jnp.concatenate(my_tokens(gate_parts) + my_tokens(conv_parts), axis=1)
    right = jnp.concatenate(gate_halves + conv_halves, axis=1)
    partial = dot(left, right, 1, 1).astype(BF16)
    row_parts = [
        piece_of(partial, "tensor", 0, zplace ^ k) for k in range(lax.axis_size("tensor"))
    ]
    row_parts, block_output = after((row_parts, block_output))
    came = [swap(part, "tensor", 1) for part in row_parts[1::2]]
    row_parts = [own.astype(F32) + part.astype(F32) for own, part in zip(row_parts[::2], came)]
    d_normed = halving_sum(row_parts, "tensor", 2)
    grad_out_part = over_tokens(cotangent, after(gated_parts, came[1]))
    grad_conv_part = over_tokens(normed, conv_parts)
    d_rows = piece_of(own_cotangent, "tensor", 0, zplace).astype(F32)
    inv = inverse_rms(x_rows)
    scaled = d_normed * norm_gain
    inner_sum = jnp.sum(scaled * x_rows, axis=-1, keepdims=True)
    grad_rows = d_rows + inv * scaled - x_rows * (inv * inv * inv) * inner_sum / width
    grad_rows = after(grad_rows.astype(BF16))
    row_pieces = doubling_pieces(grad_rows, "tensor")
    gain = jnp.sum(d_normed * x_rows * inv, axis=0)
    devices = lax.axis_size("fsdp")

    def owned(parts, hold=()):
        pieces = [part.reshape(devices, -1, inner).astype(BF16) for part in parts]
        fill = -sum(piece.shape[1] for piece in pieces) % LANES
        pieces.append(jnp.zeros((devices, fill, inner), BF16))
        pieces = row_major(jnp.concatenate(pieces, axis=1).reshape(-1, inner))
        return lax.psum_scatter(after(pieces, hold), "fsdp", scatter_dimension=0, tiled=True)

    sums = jnp.concatenate(
        [
            owned((grad_conv_part, grad_out_part, grad_x_part, grad_dt_part), d_normed),
            owned((grad_gate_part,)),
        ]
    )
    thin = jnp.concatenate(
        [
            d_rates * rates,
            jnp.stack(tap_grads),
            jnp.sum(d_conv, axis=(0, 1))[None],
            d_bias,
            d_skips,
            gain.reshape(-1, inner),
        ],
        axis=0,
    )
    channels = states + taps + 3
    thin = doubling_sum(after(thin, row_pieces[1]), ("fsdp",))
    others = [thin] + [swap(thin, "context", k) for k in range(1, ctxs)]
    def side_by_side(parts, dim):
        size = parts[0].shape[dim]
        shape = parts[0].shape[:dim] + (size * ctxs,) + parts[0].shape[dim + 1 :]
        out = jnp.zeros(shape, parts[0].dtype)
        for k, part in enumerate(parts):
            out = lax.dynamic_update_slice_in_dim(out, part, (ctx ^ k) * size, dim)
        return out

    thin = side_by_side([part[:channels] for part in others], 1)
    sums = [sums] + [swap(sums, "context", k) for k in range(1, ctxs)]
    grad_in = side_by_side(
        [jnp.stack([part[:share], part[-share:]]).astype(F32) for part in sums], 2
    )
    grad_out = side_by_side([part[share : 2 * share].T.astype(F32) for part in sums], 0)
    thin_at = 2 * share + xcols
    grad_x = side_by_side([part[2 * share : thin_at].T.astype(F32) for part in sums], 0)
    grad_dt = side_by_side([part[thin_at : thin_at + dtrows].astype(F32) for part in sums], 1)
    gain = total([part[channels:] for part in others]).reshape(1, width)
    grad_gain = doubling_sum(gain, ("tensor",))[0]
    count = grad_rows.shape[0]
    grad_input = jnp.zeros((count * lax.axis_size("tensor"), width), BF16)
    row_pieces[-1] = after(row_pieces[-1], grad_in, grad_out, grad_x, grad_dt)
    for k, part in enumerate(row_pieces):
        grad_input = lax.dynamic_update_slice_in_dim(grad_input, part, (zplace ^ k) * count, 0)
    grad_input = grad_input.reshape(block_input.shape)

    return (
        block_output.reshape(block_input.shape),
        grad_input,
        grad_gain,
        grad_in,
        thin[states : states + taps],
        thin[states + taps],
        grad_x,
        grad_dt,
        thin[states + taps + 1],
        thin[:states],
        thin[states + taps + 2],
        grad_out,
    )


def solution(mesh):
    placed = (
        P("fsdp", "context", None),
        P("fsdp", None),
        P(),
        P(None, "fsdp", "tensor"),
        P(None, "tensor"),
        P("tensor"),
        P("tensor", "fsdp"),
        P("fsdp", "tensor"),
        P("tensor"),
        P(None, "tensor"),
        P("tensor"),
        P("tensor", "fsdp"),
        P("fsdp", "context", None),
    )
    return jax.shard_map(
        shards,
        mesh=mesh,
        in_specs=placed,
        out_specs=(
            P("fsdp", "context", None),
            P("fsdp", "context", None),
            P(),
            P(None, "fsdp", "tensor"),
            P(None, "tensor"),
            P("tensor"),
            P("tensor", "fsdp"),
            P("fsdp", "tensor"),
            P("tensor"),
            P(None, "tensor"),
            P("tensor"),
            P("tensor", "fsdp"),
        ),
        check_vma=False,
    )
```
